32 devices in a mesh: gx: 8 (over z, y), gy: 2 (over x), gz: 2 (over core).
Axes of the slice: x: 2, y: 2, z: 4, core: 2. Of those that a mesh axis runs over, the one named last changes fastest.
Arguments:
- populations: float32 [19, 64, 32, 256], P(None, 'gx', 'gy', 'gz'), as said below
- coarse_pops: float32 [19, 32, 16, 128], P(None, 'gx', 'gy', 'gz'), as said below
- fine_mask: int32 [64, 32, 256], P('gx', 'gy', 'gz'), may hold values 0 or 1
- coarse_mask: int32 [32, 16, 128], P('gx', 'gy', 'gz'), may hold values 0 or 1
- bead_data: float32 [8, 2, 2, 6, 512], P('gx', 'gy', 'gz'), as said below
- bead_bins: int32 [8, 2, 2, 1, 512], P('gx', 'gy', 'gz'), may hold values from -1 to 127, as said below
Outputs:
- fine_out: float32 [19, 64, 32, 256], P(None, 'gx', 'gy', 'gz')
- coarse_out: float32 [19, 32, 16, 128], P(None, 'gx', 'gy', 'gz')
The draws below stay inside these ranges and needn't reach their ends.
Inputs may be any that keep to these rules, and one draw needn't show every extreme that they name: `populations`: populations are positive; rest population near 1/3, axis ones near 1/18, edge ones near 1/36, density within 0.5 to 1.7. `coarse_pops`: same law as populations on the coarse grid. `bead_bins`: in each source's block of 32 slots for one owner, the live slots come first; one owner receives 32 live slots from every source in every draw. `bead_data`: row 0 and 1 lie in -0.5 to 1.5, row 2 in -0.5 to 32 - 0.5; values in empty slots are arbitrary.
All inputs are finite; a program needn't handle non-finite values. No bound on the sum of `fine_mask` or of `coarse_mask` on one device may be relied on, other than what follows from the above.
Results may differ from the reference program's by a relative error of at most 0.0003.
Values sent between devices are 32-bit elements; how exact they have to be, the bound alone decides.
A program may use at most 128 MiB of HBM per device.

```python
import jax
import jax.numpy as jnp
import numpy as np
from jax import lax

Q = 19
BIN_Z = 32
SLOT = 32
NX = 64
NY = 32
NZ = 256
N_GX = 8
N_GY = 2
N_GZ = 2


LATTICE_WEIGHTS = np.array([1.0 / 3.0] + [1.0 / 18.0] * 6 + [1.0 / 36.0] * 12)


def lattice_field(key, shape):
    first, second = jax.random.split(key)
    grid = shape[1:]
    density = 1.0 + 0.15 * jax.random.uniform(first, grid, jnp.float32, -1.0, 1.0)
    noise = 0.4 * jax.random.uniform(second, shape, jnp.float32, -1.0, 1.0)
    weights = jnp.asarray(LATTICE_WEIGHTS, jnp.float32).reshape((19, 1, 1, 1))
    return weights * density[None] * (1.0 + noise)


def draw_populations(key, part):
    return lattice_field(jax.random.fold_in(key, 11), (Q, NX, NY, NZ))


def draw_coarse_pops(key, part):
    return lattice_field(jax.random.fold_in(key, 12), (Q, NX // 2, NY // 2, NZ // 2))


def draw_bead_data(key, part):
    owners = N_GX * N_GY
    shape = (N_GX, N_GY, N_GZ, 1, owners * SLOT)
    keys = jax.random.split(jax.random.fold_in(key, 13), 5)
    first = jax.random.uniform(keys[0], shape, jnp.float32, -0.5, 1.5)
    second = jax.random.uniform(keys[1], shape, jnp.float32, -0.5, 1.5)
    third = jax.random.uniform(keys[2], shape, jnp.float32, -0.5, BIN_Z - 0.5)
    forces = 0.02 * jnp.clip(jax.random.normal(keys[3], (N_GX, N_GY, N_GZ, 3, owners * SLOT), jnp.float32), -4.0, 4.0)
    return jnp.concatenate([first, second, third, forces], axis=3)


def draw_bead_bins(key, part):
    owners = N_GX * N_GY
    bins_count = NX // N_GX // 2 * (NY // N_GY // 2) * (NZ // N_GZ // BIN_Z)
    keys = jax.random.split(jax.random.fold_in(key, 14), 5)
    load = jax.random.randint(keys[0], (owners,), 1, 5)
    counts = jax.random.randint(keys[1], (N_GX, N_GY, N_GZ, owners), 0, SLOT + 1)
    counts = jnp.minimum(SLOT, counts * load // 2)
    full_owner = jax.random.randint(keys[2], (), 0, owners)
    counts = jnp.where(jnp.arange(owners) == full_owner, SLOT, counts)
    first = jax.random.randint(keys[3], (N_GX, N_GY, N_GZ, owners, SLOT), 0, bins_count)
    second = jax.random.randint(keys[4], (N_GX, N_GY, N_GZ, owners, SLOT), 0, bins_count)
    chosen = jnp.minimum(first, second)
    live = jnp.arange(SLOT)[None, None, None, None, :] < counts[..., None]
    result = jnp.where(live, chosen, -1).astype(jnp.int32)
    return result.reshape(N_GX, N_GY, N_GZ, 1, owners * SLOT)


def place_ends(values, key, least, high):
    longest = values.shape.index(max(values.shape))
    spots = []
    for shift in (0, 1):
        where = [jax.random.randint(jax.random.fold_in(key, axis), (), 0, length) for axis, length in enumerate(values.shape)]
        where[longest] = (where[longest] + shift) % values.shape[longest]
        spots.append(tuple(where))
    return values.at[spots[0]].set(least).at[spots[1]].set(high)


def setup_inputs(seed: int = 0) -> dict:
    splits = jax.random.split(jax.random.key(seed), 7)
    populations = draw_populations(jax.random.fold_in(splits[6], 71), 0)
    coarse_pops = draw_coarse_pops(jax.random.fold_in(splits[6], 71), 0)
    fine_mask = place_ends((jax.random.randint(splits[2], (NX, NY, NZ), 0, 4) < 3).astype(jnp.int32), jax.random.fold_in(splits[2], 1), 0, 1)
    coarse_mask = place_ends((jax.random.randint(splits[3], (NX // 2, NY // 2, NZ // 2), 0, 2) < 1).astype(jnp.int32), jax.random.fold_in(splits[3], 1), 0, 1)
    bead_data = draw_bead_data(jax.random.fold_in(splits[6], 71), 0)
    bead_bins = draw_bead_bins(jax.random.fold_in(splits[6], 71), 0)
    return {"populations": populations, "coarse_pops": coarse_pops, "fine_mask": fine_mask, "coarse_mask": coarse_mask, "bead_data": bead_data, "bead_bins": bead_bins}


VELOCITIES = np.array([[0, 0, 0], [1, 0, 0], [-1, 0, 0], [0, 1, 0], [0, -1, 0], [0, 0, 1], [0, 0, -1], [1, 1, 0], [-1, -1, 0], [1, -1, 0], [-1, 1, 0], [1, 0, 1], [-1, 0, -1], [1, 0, -1], [-1, 0, 1], [0, 1, 1], [0, -1, -1], [0, 1, -1], [0, -1, 1]])
LATTICE_WEIGHTS = np.array([1.0 / 3.0] + [1.0 / 18.0] * 6 + [1.0 / 36.0] * 12)
TAU_FINE = 1.2
TAU_COARSE = 0.85
TO_COARSE = 2.0 * TAU_COARSE / TAU_FINE
TO_FINE = TAU_FINE / (2.0 * TAU_COARSE)


def weights_like(field):
    return jnp.asarray(LATTICE_WEIGHTS, field.dtype).reshape((19,) + (1,) * (field.ndim - 1))


def moments(pops):
    table = jnp.asarray(VELOCITIES, pops.dtype)
    density = jnp.sum(pops, axis=0)
    momentum = jnp.tensordot(table.T, pops, axes=1, precision=lax.Precision.HIGHEST)
    return density, momentum


def equilibrium(density, velocity, like):
    table = jnp.asarray(VELOCITIES, like.dtype)
    along = jnp.tensordot(table, velocity, axes=1, precision=lax.Precision.HIGHEST)
    speed = jnp.sum(velocity * velocity, axis=0)
    return weights_like(like) * density * (1.0 + 3.0 * along + 4.5 * along * along - 1.5 * speed)


def rescale(pops, factor):
    density, momentum = moments(pops)
    balance = equilibrium(density, momentum / density, pops)
    return balance + factor * (pops - balance)


def collide(pops, force, tau):
    density, momentum = moments(pops)
    if force is None:
        velocity = momentum / density
        return pops - (pops - equilibrium(density, velocity, pops)) / tau
    table = jnp.asarray(VELOCITIES, pops.dtype)
    velocity = (momentum + 0.5 * force) / density
    balance = equilibrium(density, velocity, pops)
    along = jnp.tensordot(table, velocity, axes=1, precision=lax.Precision.HIGHEST)
    pushed = jnp.tensordot(table, force, axes=1, precision=lax.Precision.HIGHEST)
    work = jnp.sum(velocity * force, axis=0)
    source = (1.0 - 0.5 / tau) * weights_like(pops) * (3.0 * (pushed - work) + 9.0 * along * pushed)
    return pops - (pops - balance) / tau + source


def kernel_window(start, position, cells, span, live, dtype):
    index = jnp.arange(cells).astype(jnp.int32)[None, :]
    offset = index - start[:, None]
    inside = (offset >= 0) & (offset < span) & live[:, None]
    distance = offset.astype(dtype) - position[:, None]
    return jnp.where(inside, jnp.exp(-0.5 * distance * distance), jnp.zeros_like(distance))


def spread_beads(data, bins, cells_x, cells_y, cells_z):
    nby, nbz = cells_y // 2, cells_z // BIN_Z
    count = data.shape[1]
    live = bins >= 0
    safe = jnp.maximum(bins, 0).astype(jnp.int32)
    block_x = safe // (nby * nbz)
    block_y = (safe // nbz) % nby
    block_z = safe % nbz
    kernel_x = kernel_window(2 * block_x, data[0], cells_x, 2, live, data.dtype)
    kernel_y = kernel_window(2 * block_y, data[1], cells_y, 2, live, data.dtype)
    kernel_z = kernel_window(BIN_Z * block_z, data[2], cells_z, BIN_Z, live, data.dtype)
    plane = (kernel_x[:, :, None] * kernel_y[:, None, :]).reshape(count, cells_x * cells_y)
    loaded = (data[3:6].T[:, :, None] * plane[:, None, :]).reshape(count, 3 * cells_x * cells_y)
    summed = lax.dot_general(loaded, kernel_z, (((0,), (0,)), ((), ())), precision=lax.Precision.HIGHEST)
    return summed.reshape(3, cells_x, cells_y, cells_z)


def expand_parent(parent):
    q, a, b, c = parent.shape
    grown = jnp.broadcast_to(parent[:, :, None, :, None, :, None], (q, a, 2, b, 2, c, 2))
    return grown.reshape(q, 2 * a, 2 * b, 2 * c)


def stream_periodic(post):
    moved = [jnp.roll(post[i], tuple(int(v) for v in VELOCITIES[i]), axis=(0, 1, 2)) for i in range(19)]
    return jnp.stack(moved)


def reference(populations, coarse_pops, fine_mask, coarse_mask, bead_data, bead_bins):
    owners = N_GX * N_GY
    cells_x, cells_y, cells_z = NX // N_GX, NY // N_GY, NZ // N_GZ
    data = bead_data.reshape(owners, N_GZ, 6, owners, SLOT).transpose(3, 1, 2, 0, 4).reshape(owners * N_GZ, 6, owners * SLOT)
    bins = bead_bins.reshape(owners, N_GZ, owners, SLOT).transpose(2, 1, 0, 3).reshape(owners * N_GZ, owners * SLOT)
    pieces = lax.map(lambda item: spread_beads(item[0], item[1], cells_x, cells_y, cells_z), (data, bins))
    pieces = pieces.reshape(N_GX, N_GY, N_GZ, 3, cells_x, cells_y, cells_z).transpose(3, 0, 4, 1, 5, 2, 6)
    force = pieces.reshape(3, NX, NY, NZ)
    restricted = populations.reshape(19, NX // 2, 2, NY // 2, 2, NZ // 2, 2).mean(axis=(2, 4, 6))
    coarse_pre = jnp.where(coarse_mask[None] == 1, rescale(restricted, TO_COARSE), coarse_pops)
    parent = expand_parent(rescale(coarse_pre, TO_FINE))
    fine_pre = jnp.where(fine_mask[None] == 1, populations, parent)
    fine_post = collide(fine_pre, force, TAU_FINE)
    fine_out = stream_periodic(fine_post)
    coarse_post = collide(coarse_pre, None, TAU_COARSE)
    coarse_out = stream_periodic(coarse_post)
    return fine_out, coarse_out
```

```python
import functools

import jax
import jax.numpy as jnp
from jax import lax
from jax.experimental import pallas as pl
from jax.experimental.pallas import tpu as pltpu
from jax.sharding import PartitionSpec as P

BIN_Z = 32
VELOCITIES = [
    (0, 0, 0), (1, 0, 0), (-1, 0, 0), (0, 1, 0), (0, -1, 0), (0, 0, 1), (0, 0, -1),
    (1, 1, 0), (-1, -1, 0), (1, -1, 0), (-1, 1, 0), (1, 0, 1), (-1, 0, -1), (1, 0, -1),
    (-1, 0, 1), (0, 1, 1), (0, -1, -1), (0, 1, -1), (0, -1, 1),
]
WEIGHTS = [1.0 / 3.0] + [1.0 / 18.0] * 6 + [1.0 / 36.0] * 12
TAU_FINE = 1.2
TAU_COARSE = 0.85
TO_COARSE = 2.0 * TAU_COARSE / TAU_FINE
TO_FINE = TAU_FINE / (2.0 * TAU_COARSE)
LANES = 128
FIELDS = 8
LIMIT = 24 * 2**20
MESH = pl.DeviceIdType.MESH
SIGNS = (1, -1)
FACE = {(a, s): [i for i in range(19) if VELOCITIES[i][a] == s] for a in range(3) for s in SIGNS}
EDGES = [i for i in range(7, 19)]
EDGES_YZ = [i for i in EDGES if not VELOCITIES[i][0]]


def along(vector, c):
    total = None
    for part, sign in zip(vector, c):
        if sign:
            total = part if total is None else (total + part if sign > 0 else total - part)
    return total


def moments(p):
    rho = p[0]
    sums = [None] * 19
    m = [None] * 3
    for i in range(1, 19, 2):
        rho = rho + (p[i] + p[i + 1])
        sums[i] = p[i] - p[i + 1]
        for axis, sign in enumerate(VELOCITIES[i]):
            if sign:
                if m[axis] is None:
                    m[axis] = sums[i]
                else:
                    m[axis] = m[axis] + sums[i] if sign > 0 else m[axis] - sums[i]
    return rho, m


def relax(p, rho, u, a, b, force=None, k=0.0):
    scaled = b * rho
    base = scaled * (1.0 - 1.5 * (u[0] * u[0] + u[1] * u[1] + u[2] * u[2]))
    lin = [3.0 * scaled * v for v in u]
    quad = [4.5 * scaled * v for v in u]
    if force is not None:
        base = base - (3.0 * k) * (u[0] * force[0] + u[1] * force[1] + u[2] * force[2])
        lin = [v + (3.0 * k) * f for v, f in zip(lin, force)]
        quad = [v + (9.0 * k) * f for v, f in zip(quad, force)]
    out = [None] * 19
    if p[0] is not None:
        out[0] = a * p[0] + WEIGHTS[0] * base
    for i in range(1, 19, 2):
        if p[i] is None and p[i + 1] is None:
            continue
        c, w = VELOCITIES[i], WEIGHTS[i]
        even = w * (base + along(u, c) * along(quad, c))
        odd = w * along(lin, c)
        if p[i] is not None:
            out[i] = a * p[i] + (even + odd)
        if p[i + 1] is not None:
            out[i + 1] = a * p[i + 1] + (even - odd)
    return out


def parts(x):
    high = x.astype(jnp.bfloat16)
    return high, (x - high.astype(jnp.float32)).astype(jnp.bfloat16)


def times_exact(x, table):
    high, low = parts(x)
    dot = functools.partial(jnp.dot, preferred_element_type=jnp.float32)
    return dot(high, table) + dot(low, table)


def moved(plane, c):
    rows, lanes = plane.shape
    if c[1]:
        plane = pltpu.roll(plane, 1 if c[1] > 0 else rows - 1, 0)
    if c[2]:
        plane = pltpu.roll(plane, 1 if c[2] > 0 else lanes - 1, 1)
    return plane


def side(sign, length):
    return 0 if sign > 0 else length - 1


def slot_of(sign):
    return 0 if sign > 0 else 1


def pack_x(target, xs, es):
    _, fx, fy, fz = target.shape
    row = lax.broadcasted_iota(jnp.int32, (fy, LANES), 0)
    diagonal = row == lax.broadcasted_iota(jnp.int32, (fy, LANES), 1)
    for s in SIGNS:
        for j, i in enumerate(FACE[0, s]):
            plane = target[i, side(s, fx)]
            xs[slot_of(s), j] = plane
            c = VELOCITIES[i]
            if c[1]:
                y = side(c[1], fy)
                es[EDGES.index(i), :, 0:fz] = plane[y : y + 1]
            elif c[2]:
                z = side(c[2], fz)
                turned = jnp.where(diagonal, plane[:, z : z + 1], 0.0)
                es[EDGES.index(i)] = jnp.sum(turned, axis=0, keepdims=True)


def pack_yz(target, ys, zs, es):
    _, fx, fy, fz = target.shape
    lane = lax.broadcasted_iota(jnp.int32, (fy, LANES), 1)
    for s in SIGNS:
        y, z = side(s, fy), side(s, fz)
        for j, i in enumerate(FACE[1, s]):
            for x in range(fx):
                ys[slot_of(s), j * fx + x] = target[i, x, y : y + 1, :]
        packed = jnp.zeros((fy, LANES), jnp.float32)
        for j, i in enumerate(FACE[2, s]):
            for x in range(fx):
                packed = jnp.where(lane == j * fx + x, target[i, x, :, z : z + 1], packed)
        zs[slot_of(s)] = packed
        for i in FACE[2, s]:
            c = VELOCITIES[i]
            if c[1]:
                y = side(c[1], fy)
                es[EDGES.index(i)] = packed[y : y + 1]


def finish(*refs):
    levels = ((refs[0], None, *refs[1:4], EDGES_YZ), (*refs[4:9], EDGES))
    outs, targets, store_sem = refs[9:11], refs[11:13], refs[13]
    stores = []
    for n in (0, 1):
        target = targets[n]
        source, xr, yr, zr, er, edges = levels[n]
        _, fx, fy, fz = target.shape
        lane = lax.broadcasted_iota(jnp.int32, (fy, LANES), 1)
        row = lax.broadcasted_iota(jnp.int32, (fy, LANES), 0)
        last = lax.broadcasted_iota(jnp.int32, (fy, fz), 1)
        columns = []
        for s in SIGNS:
            column = zr[slot_of(s)]
            for j, i in enumerate(FACE[2, s]):
                c = VELOCITIES[i]
                if c[0] and xr is not None:
                    value = jnp.sum(
                        jnp.where(row == lane, er[edges.index(i)], 0.0), axis=1, keepdims=True
                    )
                    column = jnp.where(lane == j * fx + side(c[0], fx), value, column)
                elif c[1]:
                    spot = (lane >= j * fx) & (lane < (j + 1) * fx) & (row == side(c[1], fy))
                    column = jnp.where(spot, er[edges.index(i)], column)
            columns.append(column)
        for i in range(19):
            c = VELOCITIES[i]
            target[i] = source[i]
            if c[0] and xr is not None:
                target[i, side(c[0], fx)] = xr[slot_of(c[0]), FACE[0, c[0]].index(i)]
            if c[1]:
                y, j = side(c[1], fy), FACE[1, c[1]].index(i)
                for x in range(fx):
                    if c[0] and xr is not None and x == side(c[0], fx):
                        piece = er[edges.index(i), :, 0:fz]
                    else:
                        piece = yr[slot_of(c[1]), j * fx + x]
                    target[i, x, y : y + 1, :] = piece
            if c[2]:
                j, column = FACE[2, c[2]].index(i), columns[slot_of(c[2])]
                for x in range(fx):
                    k = j * fx + x
                    target[i, x] = jnp.where(
                        last == side(c[2], fz), column[:, k : k + 1], target[i, x]
                    )
            store = pltpu.make_async_copy(target.at[i], outs[n].at[i], store_sem.at[n, i])
            store.start()
            stores.append(store)
    for store in stores:
        store.wait()


def repeat(count, act, most=8):
    if count > most:
        pl.loop(0, count)(act)
    else:
        for n in range(count):
            act(n)


def kernel(
    sizes, slots, pop_in, cpop_in, fmask_in, cmask_in, bead_in, bins_in,
    stream, fyr, fzr, fer, cstream, cxr, cyr, czr, cer,
    pops, cpops, fmask, cmask, bead_ref, bins_ref, summed, restricted, parent, wide, tall,
    force, halo_force, totals, halo_send, halo_recv,
    bead_rows, bead_send, bead_recv, fys, fzs, fes, cxs, cys, czs, ces,
    in_sem, bead_sem, send_sem, recv_sem,
):
    ngx, ngy, ngz = sizes
    gx, gy, gz = lax.axis_index("gx"), lax.axis_index("gy"), lax.axis_index("gz")
    owners = ngx * ngy
    me = gx * ngy + gy
    _, nx, ny, nz = pops.shape
    _, hx, hy, hz = cpops.shape
    chunks = bins_ref.shape[0]
    per = LANES // slots
    f32 = jnp.float32

    ends = [(0, 2), (nx - 2, 2)]
    middle = [(2, nx - 4)]
    loads = [
        pltpu.make_async_copy(src, dst, in_sem.at[n])
        for n, (src, dst) in enumerate(
            [(bead_in, bead_ref), (bins_in, bins_ref)]
            + [(pop_in.at[:, pl.ds(x, w)], pops.at[:, pl.ds(x, w)]) for x, w in ends]
            + [(cmask_in, cmask), (fmask_in, fmask), (cpop_in, cpops)]
            + [(pop_in.at[:, pl.ds(x, w)], pops.at[:, pl.ds(x, w)]) for x, w in middle]
        )
    ]
    for load in loads:
        load.start()

    def device(offset):
        return (
            lax.rem(gx + (offset[0] + ngx), ngx),
            lax.rem(gy + (offset[1] + ngy), ngy),
            lax.rem(gz + (offset[2] + ngz), ngz),
        )

    def owner(step):
        other = lax.rem(me + step, owners)
        return other, (other // ngy, lax.rem(other, ngy), gz)

    def each_peer(act):
        if owners > 32:
            pl.loop(1, owners)(act)
        else:
            for step in sorted(range(1, owners), key=lambda n: -min(n, owners - n)):
                act(step)

    barrier = pltpu.get_barrier_semaphore()
    cross = [(0, 0, 1), (0, 0, -1)] + [VELOCITIES[i] for i in EDGES if VELOCITIES[i][2]]

    with jax.named_scope("p_signals"):
        @each_peer
        def _(step):
            pl.semaphore_signal(barrier, inc=1, device_id=owner(step)[1], device_id_type=MESH)

        for offset in cross:
            pl.semaphore_signal(barrier, inc=1, device_id=device(offset), device_id_type=MESH)

    lane = lax.broadcasted_iota(jnp.int32, (FIELDS, LANES), 1)
    sub = lax.broadcasted_iota(jnp.int32, (FIELDS, LANES), 0)
    diagonal = (lax.div(lane, slots) + (FIELDS - sub)) & (per - 1)
    turn = sub & (per - 1)

    def put_block(o, block):
        a, b = o // ngy, lax.rem(o, ngy)
        bead_send[b, a + 1] = block

    def pack_chunk(chunk):
        bead_rows[0:6, :] = bead_ref[pl.ds(chunk, 6, stride=chunks), :]
        bead_rows[6:7, :] = bins_ref[pl.ds(chunk, 1), :].astype(f32)
        rows = bead_rows[...]
        turned = rows
        for m in range(1, per):
            turned = jnp.where(turn == m, pltpu.roll(rows, slots * m, 1), turned)
        for k in range(per):
            kept = jnp.where(diagonal == k, turned, 0.0)
            shift = 1
            while shift < per:
                kept = kept + pltpu.roll(kept, FIELDS - shift, 0)
                shift *= 2
            block = [kept[n : n + 1] for n in range(0, FIELDS, per)]
            o = chunk * per + k
            a, b = (o // ngy, o % ngy) if isinstance(o, int) else (lax.div(o, ngy), lax.rem(o, ngy))
            for n, part in enumerate(block):
                bead_send[b, a + 1, pl.ds(n, 1), :] = part

    with jax.named_scope("p_pack"):
        for load in loads[:2]:
            load.wait()
        bead_rows[7:8, :] = jnp.zeros((1, LANES), f32)
        repeat(chunks, pack_chunk)
        for b in range(ngy):
            bead_send[b, 0] = bead_send[b, ngx]
            bead_send[b, ngx + 1] = bead_send[b, 1]
        bead_recv[me] = bead_send[gy, pl.ds(gx, 3)]

    def send_beads():
        pl.semaphore_wait(barrier, len(cross) + owners - 1)

        @each_peer
        def _(step):
            _, where = owner(step)
            pltpu.make_async_remote_copy(
                src_ref=bead_send.at[where[1], pl.ds(where[0], 3)],
                dst_ref=bead_recv.at[me],
                send_sem=bead_sem.at[0],
                recv_sem=bead_sem.at[1],
                device_id=where,
                device_id_type=MESH,
            ).start()

    early = gx * 3 < ngx

    with jax.named_scope("p_barrier"):
        @pl.when(jnp.logical_not(early))
        def _():
            send_beads()

    fold = lax.broadcasted_iota(jnp.int32, (nz, hz), 0) - 2 * lax.broadcasted_iota(
        jnp.int32, (nz, hz), 1
    )
    fold = jnp.where((fold == 0) | (fold == 1), 0.125, 0.0).astype(jnp.bfloat16)
    spread = lax.broadcasted_iota(jnp.int32, (hz, nz), 1) - 2 * lax.broadcasted_iota(
        jnp.int32, (hz, nz), 0
    )
    spread = jnp.where((spread == 0) | (spread == 1), 1.0, 0.0).astype(jnp.bfloat16)

    def prepare(start, count, step):
        @pl.loop(0, 19)
        def _(q):
            for n in range(count):
                total = None
                for i in range(2):
                    for j in range(2):
                        piece = pops[q, 2 * (start + n * step) + i, pl.ds(j, hy, stride=2), :]
                        total = piece if total is None else total + piece
                summed[n, q] = total

        rows = count * 19 * hy
        restricted[0:count] = times_exact(summed[0:count].reshape(rows, nz), fold).reshape(
            count, 19, hy, hz
        )

        @pl.loop(0, count)
        def _(n):
            x = start + n * step
            p = [restricted[n, i] for i in range(19)]
            rho, m = moments(p)
            inv = 1.0 / rho
            pre = relax(p, rho, [v * inv for v in m], TO_COARSE, 1.0 - TO_COARSE)
            live = cmask[x] == 1
            pre = [jnp.where(live, pre[i], cpops[i, x]) for i in range(19)]
            rho, m = moments(pre)
            inv = 1.0 / rho
            u = [v * inv for v in m]
            down = relax(pre, rho, u, TO_FINE, 1.0 - TO_FINE)
            post = relax(pre, rho, u, 1.0 - 1.0 / TAU_COARSE, 1.0 / TAU_COARSE)
            for i in range(19):
                c = VELOCITIES[i]
                parent[n, i] = down[i]
                cstream[i, lax.rem(x + (c[0] + hx), hx)] = moved(post[i], c)

        wide[0:count] = times_exact(parent[0:count].reshape(rows, hz), spread).reshape(
            count, 19, hy, nz
        )

        @pl.loop(0, 19)
        def _(q):
            for n in range(count):
                value = wide[n, q]
                tall[n, pl.ds(0, hy, stride=2), :] = value
                tall[n, pl.ds(1, hy, stride=2), :] = value
            for n in range(count):
                for i in range(2):
                    x = 2 * (start + n * step) + i
                    pops[q, x] = jnp.where(fmask[x] == 1, pops[q, x], tall[n])

    with jax.named_scope("p_ends"):
        for load in loads[2:7]:
            load.wait()
        prepare(0, 2, hx - 1)
        for s in SIGNS:
            x = nx - 1 if s > 0 else 0
            p = [pops[i, x] for i in range(19)]
            rho, m = moments(p)
            for n, value in enumerate([rho, *m, *[p[i] for i in FACE[0, s]]]):
                halo_send[slot_of(s), n] = value

    with jax.named_scope("p_barrier2"):
        @pl.when(early)
        def _():
            send_beads()

    copies = []

    def send(src, dst, offset):
        n = len(copies)
        copy = pltpu.make_async_remote_copy(
            src_ref=src, dst_ref=dst, send_sem=send_sem.at[n], recv_sem=recv_sem.at[n],
            device_id=device(offset), device_id_type=MESH,
        )
        copy.start()
        copies.append(copy)

    for s in SIGNS:
        send(halo_send.at[slot_of(s)], halo_recv.at[slot_of(s)], (s, 0, 0))

    with jax.named_scope("p_middle"):
        for load in loads[7:]:
            load.wait()
        prepare(1, hx - 2, 1)

    with jax.named_scope("p_csend"):
        pack_x(cstream, cxs, ces)
        for s in SIGNS:
            send(cxs.at[slot_of(s)], cxr.at[slot_of(s)], (s, 0, 0))
        pack_yz(cstream, cys, czs, ces)
        for s in SIGNS:
            send(cys.at[slot_of(s)], cyr.at[slot_of(s)], (0, s, 0))
            send(czs.at[slot_of(s)], czr.at[slot_of(s)], (0, 0, s))
        for n, i in enumerate(EDGES):
            send(ces.at[n], cer.at[n], VELOCITIES[i])
        for n in range(2):
            fzs[n] = jnp.zeros((ny, LANES), f32)

    with jax.named_scope("p_beadwait"):
        arrived = bead_recv.at[pl.ds(0, owners - 1)]
        pltpu.make_async_copy(arrived, arrived, bead_sem.at[1]).wait()

    bins_y, bins_z = ny // 2, nz // BIN_Z
    bins_xy = (nx // 2) * bins_y
    near = jnp.where(sub < per, 0, 1)

    def gathered(t, side_of, mine):
        source = [
            [
                jnp.broadcast_to(bead_recv[t * per + j, side_of, pl.ds(n, 1), :], (FIELDS, LANES))
                for n in range(FIELDS // per)
            ]
            for j in range(per)
        ]
        both = []
        for rows in source:
            value = rows[0]
            for n in range(1, FIELDS // per):
                value = jnp.where(sub >= n * per, rows[n], value)
            both.append(value)
        where = (diagonal + (per - mine)) & (per - 1)
        tile = None
        for m in range(per):
            mixed = both[m % per]
            for f in range(1, per):
                mixed = jnp.where(turn == f, both[(f + m) % per], mixed)
            if m:
                mixed = pltpu.roll(mixed, slots * m, 1)
            tile = mixed if tile is None else jnp.where(where == m, mixed, tile)
        return tile

    row_i = lax.div(sub, 2).astype(f32)
    row_j = (sub & 1).astype(f32)
    depth = lax.broadcasted_iota(jnp.int32, (BIN_Z, LANES), 0).astype(f32)
    own_rows = lax.broadcasted_iota(jnp.int32, (bins_xy, LANES), 0).astype(f32)
    side_rows = lax.broadcasted_iota(jnp.int32, (bins_y, LANES), 0).astype(f32)
    bf16 = jnp.bfloat16

    def operands(t, side_of, mine):
        tile = gathered(t, side_of, mine)
        number = tile[6:7]
        column = jnp.floor((number + 0.5) * (1.0 / bins_z))
        layer = number - column * bins_z
        dx, dy = row_i - tile[0:1], row_j - tile[1:2]
        weight = jnp.exp(-0.5 * (dx * dx + dy * dy))
        if side_of == 1:
            mask, picks = own_rows == column, range(4)
        elif side_of == 0:
            mask, picks = side_rows + float(bins_xy - bins_y) == column, (2, 3)
        else:
            mask, picks = side_rows == column, (0, 1)
        highs, lows = [], []
        for d in range(3):
            pushed = weight * tile[3 + d : 4 + d]
            high = pushed.astype(bf16).astype(f32)
            low = pushed - high
            for n in picks:
                highs.append(jnp.where(mask, high[n : n + 1], 0.0))
                lows.append(jnp.where(mask, low[n : n + 1], 0.0))
        lh = jnp.concatenate(highs, axis=0).astype(bf16)
        ll = jnp.concatenate(lows, axis=0).astype(bf16)
        dz = depth - tile[2:3]
        fall = jnp.exp(-0.5 * (dz * dz))
        fh = fall.astype(bf16).astype(f32)
        fl = fall - fh
        rh = jnp.concatenate([jnp.where(layer == n, fh, 0.0) for n in range(bins_z)], axis=0)
        rl = jnp.concatenate([jnp.where(layer == n, fl, 0.0) for n in range(bins_z)], axis=0)
        rh, rl = rh.astype(bf16), rl.astype(bf16)
        return [lh, lh, ll], [rh, rl, rh]

    tiles = owners // per
    group = next(n for n in (4, 2, 1) if tiles % n == 0)

    def product(g, side_of):
        mine = lax.rem(lax.rem(gx + (side_of - 1 + ngx), ngx) * ngy + gy, per)
        left, right = [], []
        for n in range(group):
            more = operands(g * group + n, side_of, mine)
            left += more[0]
            right += more[1]
        return lax.dot_general(
            jnp.concatenate(left, axis=1),
            jnp.concatenate(right, axis=1),
            (((1,), (1,)), ((), ())),
            preferred_element_type=f32,
        )

    def whole(side_of):
        if tiles == group:
            return product(0, side_of)
        rows = 12 * bins_xy if side_of == 1 else 6 * bins_y
        totals[0:rows] = jnp.zeros((rows, nz), f32)

        @pl.loop(0, tiles // group)
        def _(g):
            totals[0:rows] += product(g, side_of)

        return totals[0:rows]

    with jax.named_scope("p_force"):
        value = whole(1)
        for d in range(3):
            for i in range(2):
                for j in range(2):
                    for b in range(nx // 2):
                        start = ((d * 2 + i) * 2 + j) * bins_xy + b * bins_y
                        force[d, 2 * b + i, pl.ds(j, bins_y, stride=2), :] = value[
                            start : start + bins_y
                        ]

    with jax.named_scope("p_hforce"):
        for n, side_of in enumerate((0, 2)):
            value = whole(side_of)
            for d in range(3):
                for j in range(2):
                    start = (d * 2 + j) * bins_y
                    halo_force[n, d, pl.ds(j, bins_y, stride=2), :] = value[start : start + bins_y]

    wide_lane = lax.broadcasted_iota(jnp.int32, (ny, LANES), 1)

    def collide(p, rho, m, f, x):
        inv = 1.0 / rho
        u = [(v + 0.5 * w) * inv for v, w in zip(m, f)]
        post = relax(
            p, rho, u, 1.0 - 1.0 / TAU_FINE, 1.0 / TAU_FINE, f, 1.0 - 0.5 / TAU_FINE
        )
        columns = [fzs[n] for n in range(2)]
        for i in range(19):
            c = VELOCITIES[i]
            if post[i] is None:
                continue
            at = x + c[0]
            if isinstance(at, int) and not 0 <= at < nx:
                continue
            plane = moved(post[i], c)
            stream[i, at] = plane
            if c[1]:
                y = side(c[1], ny)
                fys[slot_of(c[1]), FACE[1, c[1]].index(i) * nx + at] = plane[y : y + 1]
            if c[2]:
                n, z = slot_of(c[2]), side(c[2], nz)
                k = FACE[2, c[2]].index(i) * nx + at
                columns[n] = jnp.where(wide_lane == k, plane[:, z : z + 1], columns[n])
        for n in range(2):
            fzs[n] = columns[n]

    def collide_own(x):
        p = [pops[i, x] for i in range(19)]
        rho, m = moments(p)
        collide(p, rho, m, [force[d, x] for d in range(3)], x)

    with jax.named_scope("p_collide"):
        collide_own(0)
        pl.loop(1, nx - 1)(collide_own)
        collide_own(nx - 1)

    with jax.named_scope("p_hwait"):
        for copy in copies[:2]:
            copy.wait_recv()

    with jax.named_scope("p_hcollide"):
        for s in SIGNS:
            n = slot_of(s)
            p = [None] * 19
            for j, i in enumerate(FACE[0, s]):
                p[i] = halo_recv[n, 4 + j]
            collide(
                p, halo_recv[n, 0], [halo_recv[n, 1 + d] for d in range(3)],
                [halo_force[n, d] for d in range(3)], -1 if s > 0 else nx,
            )

    with jax.named_scope("p_sendyz"):
        for s in SIGNS:
            send(fys.at[slot_of(s)], fyr.at[slot_of(s)], (0, s, 0))
        for n, i in enumerate(EDGES_YZ):
            y = side(VELOCITIES[i][1], ny)
            fes[n] = fzs[slot_of(VELOCITIES[i][2]), y : y + 1, :]
            send(fes.at[n], fer.at[n], VELOCITIES[i])
        for s in SIGNS:
            send(fzs.at[slot_of(s)], fzr.at[slot_of(s)], (0, 0, s))

    with jax.named_scope("p_final"):
        pltpu.make_async_copy(arrived, arrived, bead_sem.at[0]).wait()
        for copy in copies[:2]:
            copy.wait_send()
        for copy in copies[2:]:
            copy.wait()


def local(populations, coarse_pops, fine_mask, coarse_mask, bead_data, bead_bins):
    _, nx, ny, nz = populations.shape
    _, hx, hy, hz = coarse_pops.shape
    sizes = tuple(lax.axis_size(axis) for axis in ("gx", "gy", "gz"))
    owners = sizes[0] * sizes[1]
    total = bead_data.shape[4]
    chunks = total // LANES
    slots = total // owners
    per = LANES // slots
    rows = FIELDS // per
    beads = bead_data.reshape(6 * chunks, LANES)
    bins = bead_bins.reshape(chunks, LANES)
    f32, i32 = jnp.float32, jnp.int32
    any_spec = pl.BlockSpec(memory_space=pl.ANY)
    hbm_spec = pl.BlockSpec(memory_space=pltpu.HBM)
    vmem_spec = pl.BlockSpec(memory_space=pltpu.VMEM)
    dma = pltpu.SemaphoreType.DMA

    fine_rim = [(2, 5 * nx, 1, nz), (2, ny, LANES), (len(EDGES_YZ), 1, LANES)]
    coarse_rim = [(2, 5, hy, hz), (2, 5 * hx, 1, hz), (2, hy, LANES), (12, 1, LANES)]
    shapes = [populations.shape, *fine_rim, coarse_pops.shape, *coarse_rim]
    count = max(2, hx - 2)
    pieces = pl.pallas_call(
        functools.partial(kernel, sizes, slots),
        out_shape=[jax.ShapeDtypeStruct(shape, f32) for shape in shapes],
        in_specs=[hbm_spec] * 6,
        out_specs=[vmem_spec] + [any_spec] * 3 + [vmem_spec] + [any_spec] * 4,
        scratch_shapes=[
            pltpu.VMEM((19, nx, ny, nz), f32),
            pltpu.VMEM((19, hx, hy, hz), f32),
            pltpu.VMEM((nx, ny, nz), i32),
            pltpu.VMEM((hx, hy, hz), i32),
            pltpu.VMEM((6 * chunks, LANES), f32),
            pltpu.VMEM((chunks, LANES), i32),
            pltpu.VMEM((count, 19, hy, nz), f32),
            pltpu.VMEM((count, 19, hy, hz), f32),
            pltpu.VMEM((count, 19, hy, hz), f32),
            pltpu.VMEM((count, 19, hy, nz), f32),
            pltpu.VMEM((count, ny, nz), f32),
            pltpu.VMEM((3, nx, ny, nz), f32),
            pltpu.VMEM((2, 3, ny, nz), f32),
            pltpu.VMEM((12 * (nx // 2) * (ny // 2), nz), f32),
            pltpu.VMEM((2, 9, ny, nz), f32),
            pltpu.VMEM((2, 9, ny, nz), f32),
            pltpu.VMEM((FIELDS, LANES), f32),
            pltpu.VMEM((sizes[1], sizes[0] + 2, rows, LANES), f32),
            pltpu.VMEM((owners, 3, rows, LANES), f32),
            *[pltpu.VMEM(shape, f32) for shape in fine_rim + coarse_rim],
            dma((8,)),
            dma((2,)),
            dma((28,)),
            dma((28,)),
        ],
        compiler_params=pltpu.CompilerParams(
            collective_id=0, has_side_effects=True, vmem_limit_bytes=LIMIT
        ),
    )(*[pltpu.with_memory_space_constraint(v, pltpu.HBM) for v in (populations, coarse_pops, fine_mask, coarse_mask, beads, bins)])
    return tuple(
        pl.pallas_call(
            finish,
            out_shape=[
                jax.ShapeDtypeStruct(populations.shape, f32),
                jax.ShapeDtypeStruct(coarse_pops.shape, f32),
            ],
            in_specs=[vmem_spec] * len(shapes),
            out_specs=[any_spec] * 2,
            scratch_shapes=[
                pltpu.VMEM(populations.shape, f32),
                pltpu.VMEM(coarse_pops.shape, f32),
                dma((2, 19)),
            ],
            compiler_params=pltpu.CompilerParams(vmem_limit_bytes=LIMIT),
        )(*pieces)
    )


def solution(mesh):
    in_specs = (
        P(None, "gx", "gy", "gz"),
        P(None, "gx", "gy", "gz"),
        P("gx", "gy", "gz"),
        P("gx", "gy", "gz"),
        P("gx", "gy", "gz", None, None),
        P("gx", "gy", "gz", None, None),
    )
    out_specs = (P(None, "gx", "gy", "gz"), P(None, "gx", "gy", "gz"))
    return jax.shard_map(local, mesh=mesh, in_specs=in_specs, out_specs=out_specs, check_vma=False)
```

```python
import functools

import jax
import jax.numpy as jnp
from jax import lax
from jax.experimental import pallas as pl
from jax.experimental.pallas import tpu as pltpu
from jax.sharding import PartitionSpec as P

BIN_Z = 32
VELOCITIES = [
    (0, 0, 0), (1, 0, 0), (-1, 0, 0), (0, 1, 0), (0, -1, 0), (0, 0, 1), (0, 0, -1),
    (1, 1, 0), (-1, -1, 0), (1, -1, 0), (-1, 1, 0), (1, 0, 1), (-1, 0, -1), (1, 0, -1),
    (-1, 0, 1), (0, 1, 1), (0, -1, -1), (0, 1, -1), (0, -1, 1),
]
WEIGHTS = [1.0 / 3.0] + [1.0 / 18.0] * 6 + [1.0 / 36.0] * 12
TAU_FINE = 1.2
TAU_COARSE = 0.85
TO_COARSE = 2.0 * TAU_COARSE / TAU_FINE
TO_FINE = TAU_FINE / (2.0 * TAU_COARSE)
LANES = 128
FIELDS = 8
LIMIT = 24 * 2**20
MESH = pl.DeviceIdType.MESH
SIGNS = (1, -1)
FACE = {(a, s): [i for i in range(19) if VELOCITIES[i][a] == s] for a in range(3) for s in SIGNS}
EDGES = [i for i in range(7, 19)]
EDGES_YZ = [i for i in EDGES if not VELOCITIES[i][0]]


def along(vector, c):
    total = None
    for part, sign in zip(vector, c):
        if sign:
            total = part if total is None else (total + part if sign > 0 else total - part)
    return total


def moments(p):
    rho = p[0]
    sums = [None] * 19
    m = [None] * 3
    for i in range(1, 19, 2):
        rho = rho + (p[i] + p[i + 1])
        sums[i] = p[i] - p[i + 1]
        for axis, sign in enumerate(VELOCITIES[i]):
            if sign:
                if m[axis] is None:
                    m[axis] = sums[i]
                else:
                    m[axis] = m[axis] + sums[i] if sign > 0 else m[axis] - sums[i]
    return rho, m


def setup(rho, u, b, force=None, k=0.0):
    scaled = b * rho
    base = scaled * (1.0 - 1.5 * (u[0] * u[0] + u[1] * u[1] + u[2] * u[2]))
    lin = [3.0 * scaled * v for v in u]
    quad = [4.5 * scaled * v for v in u]
    if force is not None:
        base = base - (3.0 * k) * (u[0] * force[0] + u[1] * force[1] + u[2] * force[2])
        lin = [v + (3.0 * k) * f for v, f in zip(lin, force)]
        quad = [v + (9.0 * k) * f for v, f in zip(quad, force)]
    return u, base, lin, quad


def halves(i, made):
    u, base, lin, quad = made
    first = i if i % 2 else i - 1
    c, w = VELOCITIES[first], WEIGHTS[first]
    odd = w * along(lin, c)
    return w * (base + along(u, c) * along(quad, c)), odd if i % 2 else -odd


def relax(p, rho, u, a, b, force=None, k=0.0):
    made = setup(rho, u, b, force, k)
    out = [None] * 19
    if p[0] is not None:
        out[0] = a * p[0] + WEIGHTS[0] * made[1]
    for i in range(1, 19, 2):
        if p[i] is None and p[i + 1] is None:
            continue
        even, odd = halves(i, made)
        if p[i] is not None:
            out[i] = a * p[i] + (even + odd)
        if p[i + 1] is not None:
            out[i + 1] = a * p[i + 1] + (even - odd)
    return out


def parts(x):
    high = x.astype(jnp.bfloat16)
    return high, (x - high.astype(jnp.float32)).astype(jnp.bfloat16)


def times_exact(x, table):
    high, low = parts(x)
    dot = functools.partial(jnp.dot, preferred_element_type=jnp.float32)
    return dot(high, table) + dot(low, table)


def moved(plane, c):
    rows, lanes = plane.shape
    if c[1]:
        plane = pltpu.roll(plane, 1 if c[1] > 0 else rows - 1, 0)
    if c[2]:
        plane = pltpu.roll(plane, 1 if c[2] > 0 else lanes - 1, 1)
    return plane


def side(sign, length):
    return 0 if sign > 0 else length - 1


def slot_of(sign):
    return 0 if sign > 0 else 1


def pack_x(target, xs, es):
    _, fx, fy, fz = target.shape
    row = lax.broadcasted_iota(jnp.int32, (fy, LANES), 0)
    diagonal = row == lax.broadcasted_iota(jnp.int32, (fy, LANES), 1)
    for s in SIGNS:
        for j, i in enumerate(FACE[0, s]):
            plane = target[i, side(s, fx)]
            xs[slot_of(s), j] = plane
            c = VELOCITIES[i]
            if c[1]:
                y = side(c[1], fy)
                es[EDGES.index(i), :, 0:fz] = plane[y : y + 1]
            elif c[2]:
                z = side(c[2], fz)
                turned = jnp.where(diagonal, plane[:, z : z + 1], 0.0)
                es[EDGES.index(i)] = jnp.sum(turned, axis=0, keepdims=True)


def pack_yz(target, ys, zs, es):
    _, fx, fy, fz = target.shape
    lane = lax.broadcasted_iota(jnp.int32, (fy, LANES), 1)
    for s in SIGNS:
        y, z = side(s, fy), side(s, fz)
        for j, i in enumerate(FACE[1, s]):
            for x in range(fx):
                ys[slot_of(s), j * fx + x] = target[i, x, y : y + 1, :]
        packed = jnp.zeros((fy, LANES), jnp.float32)
        for j, i in enumerate(FACE[2, s]):
            for x in range(fx):
                packed = jnp.where(lane == j * fx + x, target[i, x, :, z : z + 1], packed)
        zs[slot_of(s)] = packed
        for i in FACE[2, s]:
            c = VELOCITIES[i]
            if c[1]:
                y = side(c[1], fy)
                es[EDGES.index(i)] = packed[y : y + 1]


def fill_coarse(target, xr, yr, zr, er):
    _, fx, fy, fz = target.shape
    lane = lax.broadcasted_iota(jnp.int32, (fy, LANES), 1)
    row = lax.broadcasted_iota(jnp.int32, (fy, LANES), 0)
    last = lax.broadcasted_iota(jnp.int32, (fy, fz), 1)
    columns = []
    for s in SIGNS:
        column = zr[slot_of(s)]
        for j, i in enumerate(FACE[2, s]):
            c = VELOCITIES[i]
            if c[0]:
                value = jnp.sum(
                    jnp.where(row == lane, er[EDGES.index(i)], 0.0), axis=1, keepdims=True
                )
                column = jnp.where(lane == j * fx + side(c[0], fx), value, column)
            elif c[1]:
                spot = (lane >= j * fx) & (lane < (j + 1) * fx) & (row == side(c[1], fy))
                column = jnp.where(spot, er[EDGES.index(i)], column)
        columns.append(column)
    for i in range(1, 19):
        c = VELOCITIES[i]
        if c[0]:
            target[i, side(c[0], fx)] = xr[slot_of(c[0]), FACE[0, c[0]].index(i)]
        if c[1]:
            y, j = side(c[1], fy), FACE[1, c[1]].index(i)
            for x in range(fx):
                if c[0] and x == side(c[0], fx):
                    piece = er[EDGES.index(i), :, 0:fz]
                else:
                    piece = yr[slot_of(c[1]), j * fx + x]
                target[i, x, y : y + 1, :] = piece
        if c[2]:
            j, column = FACE[2, c[2]].index(i), columns[slot_of(c[2])]
            for x in range(fx):
                k = j * fx + x
                target[i, x] = jnp.where(
                    last == side(c[2], fz), column[:, k : k + 1], target[i, x]
                )


def finish(nx, fine, columns, coarse, fine_out, coarse_out, target, store_sem):
    _, height, nz = fine.shape
    ny = height // nx
    order = [i for i in range(19) if not VELOCITIES[i][2]]
    turned = [i for i in range(19) if VELOCITIES[i][2]]
    stores = [pltpu.make_async_copy(coarse, coarse_out, store_sem.at[19])]
    for i in order + turned:
        source = target.at[turned.index(i)] if i in turned else fine.at[i]
        stores.append(pltpu.make_async_copy(source, fine_out.at[i], store_sem.at[i]))
    for store in stores[: 1 + len(order)]:
        store.start()
    last = lax.broadcasted_iota(jnp.int32, (ny, nz), 1)
    row = lax.broadcasted_iota(jnp.int32, (ny, nz), 0)
    for n, i in enumerate(turned):
        c = VELOCITIES[i]
        column = columns[slot_of(c[2])]
        spot = last == side(c[2], nz)
        if c[1]:
            spot = spot & (row != side(c[1], ny))
        for x in range(nx):
            k = FACE[2, c[2]].index(i) * nx + x
            target[n, x * ny : (x + 1) * ny, :] = jnp.where(
                spot, column[:, k : k + 1], fine[i, x * ny : (x + 1) * ny, :]
            )
        stores[1 + len(order) + n].start()
    for store in stores:
        store.wait()


def repeat(count, act, most=8):
    if count > most:
        pl.loop(0, count)(act)
    else:
        for n in range(count):
            act(n)


def kernel(
    sizes, slots, pop_in, cpop_in, fmask_in, cmask_in, bead_in, bins_in,
    stream, fzr, cstream,
    pops, cpops, fmask, cmask, bead_ref, bins_ref, tall,
    force, halo_force, halo_send, halo_recv, brim_send, brim_recv,
    bead_rows, bead_send, bead_recv, fys, fzs, cxs, cys, czs, ces,
    fyr, fer, cxr, cyr, czr, cer,
    in_sem, bead_sem, tile_sem, ready_sem, cross_sem, send_sem, recv_sem,
):
    ngx, ngy, ngz = sizes
    gx, gy, gz = lax.axis_index("gx"), lax.axis_index("gy"), lax.axis_index("gz")
    owners = ngx * ngy
    me = gx * ngy + gy
    nx, ny, nz = fmask.shape
    _, hx, hy, hz = cpops.shape
    chunks = bins_ref.shape[0]
    per = LANES // slots
    tiles = owners // per
    f32 = jnp.float32

    ends = [(0, 2), (nx - 2, 2)]
    middle = [(2, nx - 4)]
    loads = [
        pltpu.make_async_copy(src, dst, in_sem.at[n])
        for n, (src, dst) in enumerate(
            [(bead_in, bead_ref), (bins_in, bins_ref)]
            + [(pop_in.at[:, pl.ds(x * ny, w * ny)], pops.at[:, pl.ds(x * ny, w * ny)]) for x, w in ends]
            + [(cmask_in, cmask), (fmask_in, fmask), (cpop_in, cpops)]
            + [(pop_in.at[:, pl.ds(x * ny, w * ny)], pops.at[:, pl.ds(x * ny, w * ny)]) for x, w in middle]
        )
    ]
    for load in loads:
        load.start()

    def plane_at(x):
        return pl.ds(x * ny, ny)

    def rows_at(y):
        return pl.ds(y, nx, stride=ny)

    def device(offset):
        return (
            lax.rem(gx + (offset[0] + ngx), ngx),
            lax.rem(gy + (offset[1] + ngy), ngy),
            lax.rem(gz + (offset[2] + ngz), ngz),
        )

    def place(o):
        return lax.div(o, ngy), lax.rem(o, ngy), gz

    def number(where):
        return (where[0] * ngy + where[1]) * ngz + where[2]

    def cross_peers(act, later):
        mine = number((gx, gy, gz))
        for offset in cross:
            where = device(offset)
            other = number(where)

            @pl.when(other > mine if later else other < mine)
            def _():
                act(where)

    def loop(start, stop, act):
        lax.fori_loop(start, stop, lambda n, carry: (act(n), carry)[1], 0)

    barrier = pltpu.get_barrier_semaphore()
    cross = [(0, 0, 1), (0, 0, -1)] + [VELOCITIES[i] for i in EDGES if VELOCITIES[i][2]]
    lower = jnp.int32(0)
    for offset in cross:
        lower = lower + (number(device(offset)) < number((gx, gy, gz))).astype(jnp.int32)

    with jax.named_scope("p_signals"):
        loop(
            0, owners - 1 - me,
            lambda n: pl.semaphore_signal(
                barrier, inc=1, device_id=place(owners - 1 - n), device_id_type=MESH
            ),
        )

        @pl.when(me > 0)
        def _():
            pl.semaphore_signal(barrier, inc=1, device_id=place(0), device_id_type=MESH)

        cross_peers(
            lambda where: pl.semaphore_signal(
                barrier, inc=1, device_id=where, device_id_type=MESH
            ),
            later=True,
        )

    lane = lax.broadcasted_iota(jnp.int32, (FIELDS, LANES), 1)
    sub = lax.broadcasted_iota(jnp.int32, (FIELDS, LANES), 0)
    diagonal = (lax.div(lane, slots) + (FIELDS - sub)) & (per - 1)
    turn = sub & (per - 1)

    def put_block(o, block):
        a, b = o // ngy, lax.rem(o, ngy)
        bead_send[b, a + 1] = block

    def pack_chunk(chunk):
        bead_rows[0:6, :] = bead_ref[pl.ds(chunk, 6, stride=chunks), :]
        bead_rows[6:7, :] = bins_ref[pl.ds(chunk, 1), :].astype(f32)
        rows = bead_rows[...]
        turned = rows
        for m in range(1, per):
            turned = jnp.where(turn == m, pltpu.roll(rows, slots * m, 1), turned)
        for k in range(per):
            kept = jnp.where(diagonal == k, turned, 0.0)
            shift = 1
            while shift < per:
                kept = kept + pltpu.roll(kept, FIELDS - shift, 0)
                shift *= 2
            block = [kept[n : n + 1] for n in range(0, FIELDS, per)]
            o = chunk * per + k
            a, b = (o // ngy, o % ngy) if isinstance(o, int) else (lax.div(o, ngy), lax.rem(o, ngy))
            for n, part in enumerate(block):
                bead_send[b, a + 1, pl.ds(n, 1), :] = part

    with jax.named_scope("p_barrier"):
        @pl.when(me > 0)
        def _():
            pl.semaphore_wait(barrier, me + lower)
            loop(
                1, me,
                lambda o: pl.semaphore_signal(
                    ready_sem.at[me // per], inc=1, device_id=place(o), device_id_type=MESH
                ),
            )

    with jax.named_scope("p_pack"):
        for load in loads[:2]:
            load.wait()
        bead_rows[7:8, :] = jnp.zeros((1, LANES), f32)
        repeat(chunks, pack_chunk)
        for b in range(ngy):
            bead_send[b, 0] = bead_send[b, ngx]
            bead_send[b, ngx + 1] = bead_send[b, 1]
        own_beads = pltpu.make_async_copy(
            bead_send.at[gy, pl.ds(gx, 3)], bead_recv.at[me], tile_sem.at[me // per]
        )
        own_beads.start()

    def send_beads(o):
        where = place(o)
        pltpu.make_async_remote_copy(
            src_ref=bead_send.at[where[1], pl.ds(where[0], 3)],
            dst_ref=bead_recv.at[me],
            send_sem=bead_sem,
            recv_sem=tile_sem.at[me // per],
            device_id=where,
            device_id_type=MESH,
        ).start()

    def reply_cross():
        cross_peers(
            lambda where: pl.semaphore_signal(
                cross_sem, inc=1, device_id=where, device_id_type=MESH
            ),
            later=False,
        )

    with jax.named_scope("p_answer"):
        @pl.when(me > 0)
        def _():
            loop(0, me, send_beads)
            reply_cross()

    fold = lax.broadcasted_iota(jnp.int32, (nz, hz), 0) - 2 * lax.broadcasted_iota(
        jnp.int32, (nz, hz), 1
    )
    fold = jnp.where((fold == 0) | (fold == 1), 0.125, 0.0).astype(jnp.bfloat16)
    spread = lax.broadcasted_iota(jnp.int32, (hz, nz), 1) - 2 * lax.broadcasted_iota(
        jnp.int32, (hz, nz), 0
    )
    spread = jnp.where((spread == 0) | (spread == 1), 1.0, 0.0).astype(jnp.bfloat16)

    def prepare(x):
        sums = []
        for q in range(19):
            total = None
            for i in range(2):
                for j in range(2):
                    piece = pops[q, pl.ds((2 * x + i) * ny + j, hy, stride=2), :]
                    total = piece if total is None else total + piece
            sums.append(total)
        restricted = times_exact(jnp.concatenate(sums, axis=0), fold)
        p = [restricted[i * hy : (i + 1) * hy] for i in range(19)]
        rho, m = moments(p)
        inv = 1.0 / rho
        pre = relax(p, rho, [v * inv for v in m], TO_COARSE, 1.0 - TO_COARSE)
        live = cmask[x] == 1
        pre = [jnp.where(live, pre[i], cpops[i, x]) for i in range(19)]
        rho, m = moments(pre)
        inv = 1.0 / rho
        u = [v * inv for v in m]
        down = relax(pre, rho, u, TO_FINE, 1.0 - TO_FINE)
        post = relax(pre, rho, u, 1.0 - 1.0 / TAU_COARSE, 1.0 / TAU_COARSE)
        for i in range(19):
            c = VELOCITIES[i]
            cstream[i, lax.rem(x + (c[0] + hx), hx)] = moved(post[i], c)
        wide = times_exact(jnp.concatenate(down, axis=0), spread)
        for q in range(19):
            value = wide[q * hy : (q + 1) * hy]
            tall[q, pl.ds(0, hy, stride=2), :] = value
            tall[q, pl.ds(1, hy, stride=2), :] = value
        for i in range(2):
            kept = fmask[2 * x + i] == 1
            at = plane_at(2 * x + i)
            for q in range(19):
                pops[q, at] = jnp.where(kept, pops[q, at], tall[q])

    with jax.named_scope("p_ends"):
        for load in loads[2:7]:
            load.wait()
        pl.loop(0, 2)(lambda n: prepare(n * (hx - 1)))
        for s in SIGNS:
            x = nx - 1 if s > 0 else 0
            p = [pops[i, plane_at(x)] for i in range(19)]
            rho, m = moments(p)
            for n, value in enumerate([rho, *m, *[p[i] for i in FACE[0, s]]]):
                halo_send[slot_of(s), n] = value
            for t in SIGNS:
                y = ny - 1 if t > 0 else 0
                for n, value in enumerate([rho, *m, p[VELOCITIES.index((s, t, 0))]]):
                    brim_send[slot_of(s), slot_of(t), n : n + 1, :] = value[y : y + 1]

    copies = []

    def plan(src, dst, offset):
        n = len(copies)
        copy = pltpu.make_async_remote_copy(
            src_ref=src, dst_ref=dst, send_sem=send_sem.at[n], recv_sem=recv_sem.at[n],
            device_id=device(offset), device_id_type=MESH,
        )
        copies.append(copy)
        return copy

    def send(src, dst, offset):
        plan(src, dst, offset).start()

    planned = [
        [plan(src.at[slot_of(s)], dst.at[slot_of(s)], (s, 0, 0)) for s in SIGNS]
        for src, dst in ((brim_send, brim_recv), (halo_send, halo_recv))
    ]

    def send_ends(pair, later):
        for n, s in enumerate(SIGNS):
            other = number(device((s, 0, 0)))
            mine = number((gx, gy, gz))

            @pl.when(other > mine if later else other < mine)
            def _():
                pair[n].start()

    for pair in planned:
        send_ends(pair, later=False)

    with jax.named_scope("p_middle"):
        for load in loads[7:]:
            load.wait()
        pl.loop(1, hx - 1)(prepare)

    def send_group(g):
        pl.semaphore_wait(ready_sem.at[g], jnp.minimum(per, (g + 1) * per - 1 - me))
        loop(jnp.maximum(me + 1, g * per), (g + 1) * per, send_beads)

    with jax.named_scope("p_barrier2"):
        @pl.when(me == 0)
        def _():
            pl.semaphore_wait(barrier, owners - 1 + lower)
            loop(0, owners - 1, lambda n: send_beads(owners - 1 - n))
            reply_cross()

        @pl.when(me > 0)
        def _():
            loop(lax.div(me + 1, per), tiles, send_group)

        send_ends(planned[0], later=True)

        @pl.when(lower < len(cross))
        def _():
            pl.semaphore_wait(cross_sem, len(cross) - lower)

    with jax.named_scope("p_csend"):
        pack_x(cstream, cxs, ces)
        for s in SIGNS:
            send(cxs.at[slot_of(s)], cxr.at[slot_of(s)], (s, 0, 0))
        pack_yz(cstream, cys, czs, ces)
        for s in SIGNS:
            send(cys.at[slot_of(s)], cyr.at[slot_of(s)], (0, s, 0))
            send(czs.at[slot_of(s)], czr.at[slot_of(s)], (0, 0, s))
        for n, i in enumerate(EDGES):
            send(ces.at[n], cer.at[n], VELOCITIES[i])
        for n in range(2):
            fzs[n] = jnp.zeros((ny, LANES), f32)
        send_ends(planned[1], later=True)
        force[...] = jnp.zeros_like(force)
        halo_force[...] = jnp.zeros_like(halo_force)

    bins_y, bins_z = ny // 2, nz // BIN_Z
    bins_xy = (nx // 2) * bins_y
    near = jnp.where(sub < per, 0, 1)

    def gathered(t, side_of, mine):
        source = [
            [
                jnp.broadcast_to(bead_recv[t * per + j, side_of, pl.ds(n, 1), :], (FIELDS, LANES))
                for n in range(FIELDS // per)
            ]
            for j in range(per)
        ]
        both = []
        for rows in source:
            value = rows[0]
            for n in range(1, FIELDS // per):
                value = jnp.where(sub >= n * per, rows[n], value)
            both.append(value)
        where = (diagonal + (per - mine)) & (per - 1)
        tile = None
        for m in range(per):
            mixed = both[m % per]
            for f in range(1, per):
                mixed = jnp.where(turn == f, both[(f + m) % per], mixed)
            if m:
                mixed = pltpu.roll(mixed, slots * m, 1)
            tile = mixed if tile is None else jnp.where(where == m, mixed, tile)
        return tile

    row_i = lax.div(sub, 2).astype(f32)
    row_j = (sub & 1).astype(f32)
    depth = lax.broadcasted_iota(jnp.int32, (BIN_Z, LANES), 0).astype(f32)
    own_rows = lax.broadcasted_iota(jnp.int32, (bins_xy, LANES), 0).astype(f32)
    side_rows = lax.broadcasted_iota(jnp.int32, (bins_y, LANES), 0).astype(f32)
    bf16 = jnp.bfloat16

    def product(t, side_of, first, spots, offset, count):
        mine = lax.rem(lax.rem(gx + (side_of + (ngx - 1)), ngx) * ngy + gy, per)
        tile = gathered(t, side_of, mine)
        number = tile[6:7]
        column = jnp.floor((number + 0.5) * (1.0 / bins_z))
        layer = number - column * bins_z
        dx, dy = first - tile[0:1], row_j - tile[1:2]
        weight = jnp.exp(-0.5 * (dx * dx + dy * dy))
        mask = spots + offset == column
        highs, lows = [], []
        for d in range(3):
            pushed = weight * tile[3 + d : 4 + d]
            high = pushed.astype(bf16).astype(f32)
            low = pushed - high
            for n in range(count):
                highs.append(jnp.where(mask, high[n : n + 1], 0.0))
                lows.append(jnp.where(mask, low[n : n + 1], 0.0))
        lh = jnp.concatenate(highs, axis=0).astype(bf16)
        ll = jnp.concatenate(lows, axis=0).astype(bf16)
        dz = depth - tile[2:3]
        fall = jnp.exp(-0.5 * (dz * dz))
        fh = fall.astype(bf16).astype(f32)
        fl = fall - fh
        rh = jnp.concatenate([jnp.where(layer == n, fh, 0.0) for n in range(bins_z)], axis=0)
        rl = jnp.concatenate([jnp.where(layer == n, fl, 0.0) for n in range(bins_z)], axis=0)
        rh, rl = rh.astype(bf16), rl.astype(bf16)
        return lax.dot_general(
            jnp.concatenate([lh, lh, ll], axis=1),
            jnp.concatenate([rh, rl, rh], axis=1),
            (((1,), (1,)), ((), ())),
            preferred_element_type=f32,
        )

    far = lax.div(2 * gx, ngx)

    with jax.named_scope("p_force"):
        @pl.loop(0, tiles)
        def _(n):
            near = lax.rem(n + jnp.minimum(me, 1), tiles)
            t = near + far * (tiles - 1 - n - near)
            arrived = bead_recv.at[pl.ds(t * per, per)]
            pltpu.make_async_copy(arrived, arrived, tile_sem.at[t]).wait()

            value = product(t, 1, row_i, own_rows, 0.0, 4)
            for d in range(3):
                for i in range(2):
                    for j in range(2):
                        for b in range(nx // 2):
                            start = ((d * 2 + i) * 2 + j) * bins_xy + b * bins_y
                            at = pl.ds((2 * b + i) * ny + j, bins_y, stride=2)
                            force[d, at, :] += value[start : start + bins_y]

            for h in range(2):
                first = float(1 - h)
                value = product(t, 2 * h, first, side_rows, first * (bins_xy - bins_y), 2)
                for d in range(3):
                    for j in range(2):
                        start = (d * 2 + j) * bins_y
                        at = pl.ds(j, bins_y, stride=2)
                        halo_force[h, d, at, :] += value[start : start + bins_y]

    wide_lane = lax.broadcasted_iota(jnp.int32, (ny, LANES), 1)

    def collided(p, rho, m, f):
        inv = 1.0 / rho
        u = [(v + 0.5 * w) * inv for v, w in zip(m, f)]
        return relax(
            p, rho, u, 1.0 - 1.0 / TAU_FINE, 1.0 / TAU_FINE, f, 1.0 - 0.5 / TAU_FINE
        )

    with jax.named_scope("p_hwait"):
        for copy in copies[:2]:
            copy.wait_recv()

    def made_of(rho, m, f):
        inv = 1.0 / rho
        u = [(v + 0.5 * w) * inv for v, w in zip(m, f)]
        return setup(rho, u, 1.0 / TAU_FINE, f, 1.0 - 0.5 / TAU_FINE)

    keep = 1.0 - 1.0 / TAU_FINE
    row_x = lax.broadcasted_iota(jnp.int32, (nx, nz), 0)

    def rows(n):
        sign = (1 - 2 * n).astype(f32)
        y = (ny - 1) * (1 - n)
        p = [pops[i, rows_at(y), :] for i in range(19)]
        made = made_of(*moments(p), [force[d, rows_at(y), :] for d in range(3)])
        ends = []
        for h in range(2):
            ends.append(
                made_of(
                    brim_recv[h, n, 0:1, :],
                    [brim_recv[h, n, 1 + d : 2 + d, :] for d in range(3)],
                    [halo_force[h, d, pl.ds(y, 1), :] for d in range(3)],
                )
            )
        for j, i in enumerate(FACE[1, 1]):
            c = VELOCITIES[i]
            other = FACE[1, -1][j]
            even, odd = halves(i, made)
            block = keep * jnp.where(n == 0, p[i], p[other]) + (even + sign * odd)
            if c[2]:
                block = pltpu.roll(block, (1 if c[2] > 0 else nz - 1) + n * (c[2] * (nz - 2)), 1)
            if c[0]:
                block = pltpu.roll(block, (1 if c[0] > 0 else nx - 1) + n * (c[0] * (nx - 2)), 0)
                for h in range(2):
                    even, odd = halves(i, ends[h])
                    end = keep * brim_recv[h, n, 4:5, :] + (even + sign * odd)
                    row = (nx - 1) * h
                    enters = n == (h if c[0] > 0 else 1 - h)
                    block = jnp.where((row_x == row) & enters, end, block)
            fys[n, j] = block

    with jax.named_scope("p_rows"):
        pl.loop(0, 2)(rows)
        for s in SIGNS:
            send(fys.at[slot_of(s)], fyr.at[slot_of(s)], (0, s, 0))
        for n, i in enumerate(EDGES_YZ):
            s = VELOCITIES[i][1]
            send(fys.at[slot_of(s), FACE[1, s].index(i)], fer.at[n], VELOCITIES[i])

    def collide(p, rho, m, f, x):
        post = collided(p, rho, m, f)
        columns = [fzs[n] for n in range(2)]
        for i in range(19):
            c = VELOCITIES[i]
            if post[i] is None:
                continue
            at = x + c[0] if isinstance(x, int) else lax.rem(x + (c[0] + nx), nx)
            plane = moved(post[i], (0, c[1], 0))
            stream[i, plane_at(at)] = moved(plane, (0, 0, c[2]))
            if c[2]:
                n = slot_of(c[2])
                k = FACE[2, c[2]].index(i) * nx + at
                turned = pltpu.roll(plane, lax.rem(k + (1 - n), LANES), 1)
                columns[n] = jnp.where(wide_lane == k, turned, columns[n])
        for n in range(2):
            fzs[n] = columns[n]

    def collide_own(x):
        p = [pops[i, plane_at(x)] for i in range(19)]
        rho, m = moments(p)
        collide(p, rho, m, [force[d, plane_at(x)] for d in range(3)], x)

    with jax.named_scope("p_collide"):
        pl.loop(0, nx)(collide_own)

    with jax.named_scope("p_hwait2"):
        for copy in copies[2:4]:
            copy.wait_recv()

    with jax.named_scope("p_hcollide"):
        for s in SIGNS:
            n = slot_of(s)
            p = [None] * 19
            for j, i in enumerate(FACE[0, s]):
                p[i] = halo_recv[n, 4 + j]
            collide(
                p, halo_recv[n, 0], [halo_recv[n, 1 + d] for d in range(3)],
                [halo_force[n, d] for d in range(3)], -1 if s > 0 else nx,
            )

    with jax.named_scope("p_sendz"):
        for s in SIGNS:
            send(fzs.at[slot_of(s)], fzr.at[slot_of(s)], (0, 0, s))

    with jax.named_scope("p_coarse"):
        for copy in copies[4:22]:
            copy.wait()
        fill_coarse(cstream, cxr, cyr, czr, cer)

    with jax.named_scope("p_ywait"):
        for copy in copies[22:28]:
            copy.wait()

    with jax.named_scope("p_yfill"):
        corner = lax.broadcasted_iota(jnp.int32, (nx, nz), 1)
        for s in SIGNS:
            for j, i in enumerate(FACE[1, s]):
                c = VELOCITIES[i]
                block = fyr[slot_of(s), j]
                if c[2]:
                    block = jnp.where(corner == side(c[2], nz), fer[EDGES_YZ.index(i)], block)
                stream[i, rows_at(side(s, ny)), :] = block

    with jax.named_scope("p_zwait"):
        for copy in copies[28:30]:
            copy.wait()

    with jax.named_scope("p_final"):
        sent = bead_recv.at[pl.ds(0, owners - 1)]
        pltpu.make_async_copy(sent, sent, bead_sem).wait()
        for copy in copies[:4]:
            copy.wait_send()


def local(populations, coarse_pops, fine_mask, coarse_mask, bead_data, bead_bins):
    _, nx, ny, nz = populations.shape
    _, hx, hy, hz = coarse_pops.shape
    sizes = tuple(lax.axis_size(axis) for axis in ("gx", "gy", "gz"))
    owners = sizes[0] * sizes[1]
    total = bead_data.shape[4]
    chunks = total // LANES
    slots = total // owners
    per = LANES // slots
    rows = FIELDS // per
    beads = bead_data.reshape(6 * chunks, LANES)
    bins = bead_bins.reshape(chunks, LANES)
    f32, i32 = jnp.float32, jnp.int32
    any_spec = pl.BlockSpec(memory_space=pl.ANY)
    hbm_spec = pl.BlockSpec(memory_space=pltpu.HBM)
    vmem_spec = pl.BlockSpec(memory_space=pltpu.VMEM)
    dma = pltpu.SemaphoreType.DMA

    fine_rim = [(2, 5, nx, nz), (2, ny, LANES), (len(EDGES_YZ), nx, nz)]
    coarse_rim = [(2, 5, hy, hz), (2, 5 * hx, 1, hz), (2, hy, LANES), (12, 1, LANES)]
    shapes = [(19, nx * ny, nz), (2, ny, LANES), coarse_pops.shape]
    vmem = [
        (3, nx * ny, nz), (2, 3, ny, nz),
        (2, 9, ny, nz), (2, 9, ny, nz), (2, 2, 8, nz), (2, 2, 8, nz),
        (FIELDS, LANES), (sizes[1], sizes[0] + 2, rows, LANES), (owners, 3, rows, LANES),
        *fine_rim[:2], *coarse_rim, fine_rim[0], fine_rim[2], *coarse_rim,
    ]
    operands = (
        populations.reshape(19, nx * ny, nz), coarse_pops, fine_mask, coarse_mask, beads, bins
    )
    fine, columns, coarse = pl.pallas_call(
        functools.partial(kernel, sizes, slots),
        out_shape=[jax.ShapeDtypeStruct(shape, f32) for shape in shapes],
        in_specs=[hbm_spec] * 6,
        out_specs=[vmem_spec, any_spec, vmem_spec],
        scratch_shapes=[
            pltpu.VMEM((19, nx * ny, nz), f32),
            pltpu.VMEM((19, hx, hy, hz), f32),
            pltpu.VMEM((nx, ny, nz), i32),
            pltpu.VMEM((hx, hy, hz), i32),
            pltpu.VMEM((6 * chunks, LANES), f32),
            pltpu.VMEM((chunks, LANES), i32),
            pltpu.VMEM((19, ny, nz), f32),
            *[pltpu.VMEM(shape, f32) for shape in vmem],
            dma((8,)),
            dma,
            dma((owners // per,)),
            pltpu.SemaphoreType.REGULAR((owners // per,)),
            pltpu.SemaphoreType.REGULAR,
            dma((30,)),
            dma((30,)),
        ],
        compiler_params=pltpu.CompilerParams(
            collective_id=0, has_side_effects=True, vmem_limit_bytes=LIMIT
        ),
    )(*[pltpu.with_memory_space_constraint(v, pltpu.HBM) for v in operands])
    fine, coarse = pl.pallas_call(
        functools.partial(finish, nx),
        out_shape=[jax.ShapeDtypeStruct(shape, f32) for shape in (shapes[0], shapes[2])],
        in_specs=[vmem_spec] * 3,
        out_specs=[any_spec] * 2,
        scratch_shapes=[pltpu.VMEM((10, nx * ny, nz), f32), dma((20,))],
        compiler_params=pltpu.CompilerParams(vmem_limit_bytes=LIMIT),
    )(fine, columns, coarse)
    return fine.reshape(populations.shape), coarse


def solution(mesh):
    in_specs = (
        P(None, "gx", "gy", "gz"),
        P(None, "gx", "gy", "gz"),
        P("gx", "gy", "gz"),
        P("gx", "gy", "gz"),
        P("gx", "gy", "gz", None, None),
        P("gx", "gy", "gz", None, None),
    )
    out_specs = (P(None, "gx", "gy", "gz"), P(None, "gx", "gy", "gz"))
    return jax.shard_map(local, mesh=mesh, in_specs=in_specs, out_specs=out_specs, check_vma=False)
```

```python
import functools

import jax
import jax.numpy as jnp
from jax import lax
from jax.experimental import pallas as pl
from jax.experimental.pallas import tpu as pltpu
from jax.sharding import PartitionSpec as P

BIN_Z = 32
VELOCITIES = [
    (0, 0, 0), (1, 0, 0), (-1, 0, 0), (0, 1, 0), (0, -1, 0), (0, 0, 1), (0, 0, -1),
    (1, 1, 0), (-1, -1, 0), (1, -1, 0), (-1, 1, 0), (1, 0, 1), (-1, 0, -1), (1, 0, -1),
    (-1, 0, 1), (0, 1, 1), (0, -1, -1), (0, 1, -1), (0, -1, 1),
]
WEIGHTS = [1.0 / 3.0] + [1.0 / 18.0] * 6 + [1.0 / 36.0] * 12
TAU_FINE = 1.2
TAU_COARSE = 0.85
TO_COARSE = 2.0 * TAU_COARSE / TAU_FINE
TO_FINE = TAU_FINE / (2.0 * TAU_COARSE)
LANES = 128
FIELDS = 8
LIMIT = 24 * 2**20
MESH = pl.DeviceIdType.MESH
SIGNS = (1, -1)
FACE = {(a, s): [i for i in range(19) if VELOCITIES[i][a] == s] for a in range(3) for s in SIGNS}
EDGES = [i for i in range(7, 19)]
EDGES_YZ = [i for i in EDGES if not VELOCITIES[i][0]]


def along(vector, c):
    total = None
    for part, sign in zip(vector, c):
        if sign:
            total = part if total is None else (total + part if sign > 0 else total - part)
    return total


def moments(p):
    rho = p[0]
    sums = [None] * 19
    m = [None] * 3
    for i in range(1, 19, 2):
        rho = rho + (p[i] + p[i + 1])
        sums[i] = p[i] - p[i + 1]
        for axis, sign in enumerate(VELOCITIES[i]):
            if sign:
                if m[axis] is None:
                    m[axis] = sums[i]
                else:
                    m[axis] = m[axis] + sums[i] if sign > 0 else m[axis] - sums[i]
    return rho, m


def setup(rho, u, b, force=None, k=0.0):
    scaled = b * rho
    base = scaled * (1.0 - 1.5 * (u[0] * u[0] + u[1] * u[1] + u[2] * u[2]))
    lin = [3.0 * scaled * v for v in u]
    quad = [4.5 * scaled * v for v in u]
    if force is not None:
        base = base - (3.0 * k) * (u[0] * force[0] + u[1] * force[1] + u[2] * force[2])
        lin = [v + (3.0 * k) * f for v, f in zip(lin, force)]
        quad = [v + (9.0 * k) * f for v, f in zip(quad, force)]
    return u, base, lin, quad


def halves(i, made):
    u, base, lin, quad = made
    first = i if i % 2 else i - 1
    c, w = VELOCITIES[first], WEIGHTS[first]
    odd = w * along(lin, c)
    return w * (base + along(u, c) * along(quad, c)), odd if i % 2 else -odd


def relax(p, rho, u, a, b, force=None, k=0.0):
    made = setup(rho, u, b, force, k)
    out = [None] * 19
    if p[0] is not None:
        out[0] = a * p[0] + WEIGHTS[0] * made[1]
    for i in range(1, 19, 2):
        if p[i] is None and p[i + 1] is None:
            continue
        even, odd = halves(i, made)
        if p[i] is not None:
            out[i] = a * p[i] + (even + odd)
        if p[i + 1] is not None:
            out[i + 1] = a * p[i + 1] + (even - odd)
    return out


def parts(x):
    high = x.astype(jnp.bfloat16)
    return high, (x - high.astype(jnp.float32)).astype(jnp.bfloat16)


def times_exact(x, table):
    high, low = parts(x)
    dot = functools.partial(jnp.dot, preferred_element_type=jnp.float32)
    return dot(high, table) + dot(low, table)


def moved(plane, c):
    rows, lanes = plane.shape
    if c[1]:
        plane = pltpu.roll(plane, 1 if c[1] > 0 else rows - 1, 0)
    if c[2]:
        plane = pltpu.roll(plane, 1 if c[2] > 0 else lanes - 1, 1)
    return plane


def side(sign, length):
    return 0 if sign > 0 else length - 1


def slot_of(sign):
    return 0 if sign > 0 else 1


def pack_x(target, xs, es):
    _, fx, fy, fz = target.shape
    row = lax.broadcasted_iota(jnp.int32, (fy, LANES), 0)
    diagonal = row == lax.broadcasted_iota(jnp.int32, (fy, LANES), 1)
    for s in SIGNS:
        for j, i in enumerate(FACE[0, s]):
            plane = target[i, side(s, fx)]
            xs[slot_of(s), j] = plane
            c = VELOCITIES[i]
            if c[1]:
                y = side(c[1], fy)
                es[EDGES.index(i), :, 0:fz] = plane[y : y + 1]
            elif c[2]:
                z = side(c[2], fz)
                turned = jnp.where(diagonal, plane[:, z : z + 1], 0.0)
                es[EDGES.index(i)] = jnp.sum(turned, axis=0, keepdims=True)


def pack_yz(target, ys, zs, es):
    _, fx, fy, fz = target.shape
    lane = lax.broadcasted_iota(jnp.int32, (fy, LANES), 1)
    for s in SIGNS:
        y, z = side(s, fy), side(s, fz)
        for j, i in enumerate(FACE[1, s]):
            for x in range(fx):
                ys[slot_of(s), j * fx + x] = target[i, x, y : y + 1, :]
        packed = jnp.zeros((fy, LANES), jnp.float32)
        for j, i in enumerate(FACE[2, s]):
            for x in range(fx):
                packed = jnp.where(lane == j * fx + x, target[i, x, :, z : z + 1], packed)
        zs[slot_of(s)] = packed
        for i in FACE[2, s]:
            c = VELOCITIES[i]
            if c[1]:
                y = side(c[1], fy)
                es[EDGES.index(i)] = packed[y : y + 1]


def fill_coarse(target, xr, yr, zr, er):
    _, fx, fy, fz = target.shape
    lane = lax.broadcasted_iota(jnp.int32, (fy, LANES), 1)
    row = lax.broadcasted_iota(jnp.int32, (fy, LANES), 0)
    last = lax.broadcasted_iota(jnp.int32, (fy, fz), 1)
    columns = []
    for s in SIGNS:
        column = zr[slot_of(s)]
        for j, i in enumerate(FACE[2, s]):
            c = VELOCITIES[i]
            if c[0]:
                value = jnp.sum(
                    jnp.where(row == lane, er[EDGES.index(i)], 0.0), axis=1, keepdims=True
                )
                column = jnp.where(lane == j * fx + side(c[0], fx), value, column)
            elif c[1]:
                spot = (lane >= j * fx) & (lane < (j + 1) * fx) & (row == side(c[1], fy))
                column = jnp.where(spot, er[EDGES.index(i)], column)
        columns.append(column)
    for i in range(1, 19):
        c = VELOCITIES[i]
        if c[0]:
            target[i, side(c[0], fx)] = xr[slot_of(c[0]), FACE[0, c[0]].index(i)]
        if c[1]:
            y, j = side(c[1], fy), FACE[1, c[1]].index(i)
            for x in range(fx):
                if c[0] and x == side(c[0], fx):
                    piece = er[EDGES.index(i), :, 0:fz]
                else:
                    piece = yr[slot_of(c[1]), j * fx + x]
                target[i, x, y : y + 1, :] = piece
        if c[2]:
            j, column = FACE[2, c[2]].index(i), columns[slot_of(c[2])]
            for x in range(fx):
                k = j * fx + x
                target[i, x] = jnp.where(
                    last == side(c[2], fz), column[:, k : k + 1], target[i, x]
                )


def finish(nx, fine, columns, coarse, fine_out, coarse_out, target, store_sem):
    _, height, nz = fine.shape
    ny = height // nx
    turned = [5, 6, *range(11, 19)]
    parts = [(coarse, coarse_out), (fine.at[0:5], fine_out.at[0:5]), (fine.at[7:11], fine_out.at[7:11])]
    for n in range(0, 10, 2):
        parts.append((target.at[n : n + 2], fine_out.at[turned[n] : turned[n] + 2]))
    stores = [pltpu.make_async_copy(src, dst, store_sem.at[n]) for n, (src, dst) in enumerate(parts)]
    for store in stores[:3]:
        store.start()
    last = lax.broadcasted_iota(jnp.int32, (ny, nz), 1)
    row = lax.broadcasted_iota(jnp.int32, (ny, nz), 0)
    for n, i in enumerate(turned):
        c = VELOCITIES[i]
        column = columns[slot_of(c[2])]
        spot = last == side(c[2], nz)
        if c[1]:
            spot = spot & (row != side(c[1], ny))
        for x in range(nx):
            k = FACE[2, c[2]].index(i) * nx + x
            target[n, x * ny : (x + 1) * ny, :] = jnp.where(
                spot, column[:, k : k + 1], fine[i, x * ny : (x + 1) * ny, :]
            )
        if n % 2:
            stores[3 + n // 2].start()
    for store in stores:
        store.wait()


def repeat(count, act, most=8):
    if count > most:
        pl.loop(0, count)(act)
    else:
        for n in range(count):
            act(n)


def kernel(
    sizes, slots, pop_in, cpop_in, fmask_in, cmask_in, bead_in, bins_in,
    stream, fzr, cstream,
    pops, cpops, fmask, cmask, bead_ref, bins_ref, tall,
    force, halo_force, halo_send, halo_recv, brim_send, brim_recv,
    bead_rows, bead_send, bead_recv, fys, fzs, fxs, fxr, cxs, cys, czs, ces,
    fyr, fer, cxr, cyr, czr, cer,
    in_sem, bead_sem, tile_sem, ready_sem, cross_sem, send_sem, recv_sem,
):
    ngx, ngy, ngz = sizes
    gx, gy, gz = lax.axis_index("gx"), lax.axis_index("gy"), lax.axis_index("gz")
    owners = ngx * ngy
    me = gx * ngy + gy
    nx, ny, nz = fmask.shape
    _, hx, hy, hz = cpops.shape
    chunks = bins_ref.shape[0]
    per = LANES // slots
    tiles = owners // per
    f32 = jnp.float32

    barrier = pltpu.get_barrier_semaphore()
    half = tiles // 2
    late = me >= half * per

    @pl.when(late & (me > 0))
    def _():
        pl.semaphore_signal(barrier, inc=1, device_id=(0, 0, gz), device_id_type=MESH)

    def part(x, w):
        return pop_in.at[:, pl.ds(x * ny, w * ny)], pops.at[:, pl.ds(x * ny, w * ny)]

    loads = [
        pltpu.make_async_copy(src, dst, in_sem.at[n])
        for n, src, dst in (
            (0, bead_in, bead_ref), (1, bins_in, bins_ref), (2, *part(0, 2)), (2, *part(nx - 2, 2)),
            (3, cmask_in, cmask), (4, fmask_in, fmask), (5, cpop_in, cpops),
            (6, *part(2, nx - 4)),
        )
    ]
    for load in loads:
        load.start()

    def plane_at(x):
        return pl.ds(x * ny, ny)

    def rows_at(y):
        return pl.ds(y, nx, stride=ny)

    def device(offset):
        return (
            lax.rem(gx + (offset[0] + ngx), ngx),
            lax.rem(gy + (offset[1] + ngy), ngy),
            lax.rem(gz + (offset[2] + ngz), ngz),
        )

    def place(o):
        return lax.div(o, ngy), lax.rem(o, ngy), gz

    def number(where):
        return (where[0] * ngy + where[1]) * ngz + where[2]

    def cross_peers(act, later):
        mine = number((gx, gy, gz))
        for offset in cross:
            where = device(offset)
            other = number(where)

            @pl.when(other > mine if later else other < mine)
            def _():
                act(where)

    def loop(start, stop, act):
        lax.fori_loop(start, stop, lambda n, carry: (act(n), carry)[1], 0)

    cross = [(0, 0, 1), (0, 0, -1)] + [VELOCITIES[i] for i in EDGES if VELOCITIES[i][2]]
    lower = jnp.int32(0)
    for offset in cross:
        lower = lower + (number(device(offset)) < number((gx, gy, gz))).astype(jnp.int32)

    with jax.named_scope("p_signals"):
        loop(
            0, owners - 1 - me,
            lambda n: pl.semaphore_signal(
                barrier, inc=1, device_id=place(owners - 1 - n), device_id_type=MESH
            ),
        )
        cross_peers(
            lambda where: pl.semaphore_signal(
                barrier, inc=1, device_id=where, device_id_type=MESH
            ),
            later=True,
        )

    lane = lax.broadcasted_iota(jnp.int32, (FIELDS, LANES), 1)
    sub = lax.broadcasted_iota(jnp.int32, (FIELDS, LANES), 0)
    diagonal = (lax.div(lane, slots) + (FIELDS - sub)) & (per - 1)
    turn = sub & (per - 1)

    def put_block(o, block):
        a, b = o // ngy, lax.rem(o, ngy)
        bead_send[b, a + 1] = block

    def pack_chunk(chunk):
        bead_rows[0:6, :] = bead_ref[pl.ds(chunk, 6, stride=chunks), :]
        bead_rows[6:7, :] = bins_ref[pl.ds(chunk, 1), :].astype(f32)
        rows = bead_rows[...]
        turned = rows
        for m in range(1, per):
            turned = jnp.where(turn == m, pltpu.roll(rows, slots * m, 1), turned)
        for k in range(per):
            kept = jnp.where(diagonal == k, turned, 0.0)
            shift = 1
            while shift < per:
                kept = kept + pltpu.roll(kept, FIELDS - shift, 0)
                shift *= 2
            block = [kept[n : n + 1] for n in range(0, FIELDS, per)]
            o = chunk * per + k
            a, b = (o // ngy, o % ngy) if isinstance(o, int) else (lax.div(o, ngy), lax.rem(o, ngy))
            for n, part in enumerate(block):
                bead_send[b, a + 1, pl.ds(n, 1), :] = part

    with jax.named_scope("p_barrier"):
        @pl.when(me > 0)
        def _():
            pl.semaphore_wait(barrier, me + lower)
            loop(
                late.astype(jnp.int32), me,
                lambda o: pl.semaphore_signal(
                    ready_sem.at[me // per], inc=1, device_id=place(o), device_id_type=MESH
                ),
            )

    with jax.named_scope("p_pack"):
        for load in loads[:2]:
            load.wait()
        bead_rows[7:8, :] = jnp.zeros((1, LANES), f32)
        repeat(chunks, pack_chunk)
        for b in range(ngy):
            bead_send[b, 0] = bead_send[b, ngx]
            bead_send[b, ngx + 1] = bead_send[b, 1]
        own_beads = pltpu.make_async_copy(
            bead_send.at[gy, pl.ds(gx, 3)], bead_recv.at[me], tile_sem.at[me // per]
        )
        own_beads.start()

    def send_beads(o):
        where = place(o)
        pltpu.make_async_remote_copy(
            src_ref=bead_send.at[where[1], pl.ds(where[0], 3)],
            dst_ref=bead_recv.at[me],
            send_sem=bead_sem,
            recv_sem=tile_sem.at[me // per],
            device_id=where,
            device_id_type=MESH,
        ).start()

    def reply_cross():
        cross_peers(
            lambda where: pl.semaphore_signal(
                cross_sem, inc=1, device_id=where, device_id_type=MESH
            ),
            later=False,
        )

    with jax.named_scope("p_answer"):
        @pl.when(me > 0)
        def _():
            loop(0, me, send_beads)
            reply_cross()

    fold = lax.broadcasted_iota(jnp.int32, (nz, hz), 0) - 2 * lax.broadcasted_iota(
        jnp.int32, (nz, hz), 1
    )
    fold = jnp.where((fold == 0) | (fold == 1), 0.125, 0.0).astype(jnp.bfloat16)
    spread = lax.broadcasted_iota(jnp.int32, (hz, nz), 1) - 2 * lax.broadcasted_iota(
        jnp.int32, (hz, nz), 0
    )
    spread = jnp.where((spread == 0) | (spread == 1), 1.0, 0.0).astype(jnp.bfloat16)

    def prepare(x):
        sums = []
        for q in range(19):
            total = None
            for i in range(2):
                for j in range(2):
                    piece = pops[q, pl.ds((2 * x + i) * ny + j, hy, stride=2), :]
                    total = piece if total is None else total + piece
            sums.append(total)
        restricted = times_exact(jnp.concatenate(sums, axis=0), fold)
        p = [restricted[i * hy : (i + 1) * hy] for i in range(19)]
        rho, m = moments(p)
        inv = 1.0 / rho
        pre = relax(p, rho, [v * inv for v in m], TO_COARSE, 1.0 - TO_COARSE)
        live = cmask[x] == 1
        pre = [jnp.where(live, pre[i], cpops[i, x]) for i in range(19)]
        rho, m = moments(pre)
        inv = 1.0 / rho
        u = [v * inv for v in m]
        down = relax(pre, rho, u, TO_FINE, 1.0 - TO_FINE)
        post = relax(pre, rho, u, 1.0 - 1.0 / TAU_COARSE, 1.0 / TAU_COARSE)
        for i in range(19):
            c = VELOCITIES[i]
            cstream[i, lax.rem(x + (c[0] + hx), hx)] = moved(post[i], c)
        wide = times_exact(jnp.concatenate(down, axis=0), spread)
        for q in range(19):
            value = wide[q * hy : (q + 1) * hy]
            tall[q, pl.ds(0, hy, stride=2), :] = value
            tall[q, pl.ds(1, hy, stride=2), :] = value
        for i in range(2):
            kept = fmask[2 * x + i] == 1
            at = plane_at(2 * x + i)
            for q in range(19):
                pops[q, at] = jnp.where(kept, pops[q, at], tall[q])

    with jax.named_scope("p_ends"):
        pltpu.make_async_copy(*part(0, 4), in_sem.at[2]).wait()
        for load in loads[4:7]:
            load.wait()
        pl.loop(0, 2)(lambda n: prepare(n * (hx - 1)))
        for s in SIGNS:
            x = nx - 1 if s > 0 else 0
            p = [pops[i, plane_at(x)] for i in range(19)]
            rho, m = moments(p)
            for n, value in enumerate([rho, *m, *[p[i] for i in FACE[0, s]]]):
                halo_send[slot_of(s), n] = value
            for t in SIGNS:
                y = ny - 1 if t > 0 else 0
                for n, value in enumerate([rho, *m, p[VELOCITIES.index((s, t, 0))]]):
                    brim_send[slot_of(s), slot_of(t), n : n + 1, :] = value[y : y + 1]

    BRIM, HALO, COARSE_X, COARSE_Y, COARSE_Z, COARSE_EDGE, ROWS, CORNERS, ENDS, COLUMNS = range(10)
    buffers = [
        (brim_send, brim_recv), (halo_send, halo_recv),
        (cxs, cxr), (cys, cyr), (czs, czr), (ces, cer),
        (fys, fyr), (fer, fer), (fxs, fxr), (fzs, fzr),
    ]

    def plan(kind, src, dst, offset):
        return pltpu.make_async_remote_copy(
            src_ref=src, dst_ref=dst, send_sem=send_sem.at[kind], recv_sem=recv_sem.at[kind],
            device_id=device(offset), device_id_type=MESH,
        )

    def send(kind, part, offset):
        src, dst = buffers[kind]
        plan(kind, src.at[part], dst.at[part], offset).start()

    def arrive(*kinds):
        for kind in kinds:
            dst = buffers[kind][1]
            pltpu.make_async_copy(dst, dst, recv_sem.at[kind]).wait()

    def leave(*kinds):
        for kind in kinds:
            src = buffers[kind][0]
            pltpu.make_async_copy(src, src, send_sem.at[kind]).wait()

    def send_ends(kind, later):
        for s in SIGNS:
            other = number(device((s, 0, 0)))
            mine = number((gx, gy, gz))

            @pl.when(other > mine if later else other < mine)
            def _():
                send(kind, slot_of(s), (s, 0, 0))

    send_ends(BRIM, later=False)
    send_ends(HALO, later=False)

    with jax.named_scope("p_middle"):
        for load in loads[7:]:
            load.wait()
        pl.loop(1, hx - 1)(prepare)

    def send_group(g):
        pl.semaphore_wait(ready_sem.at[g], jnp.minimum(per, (g + 1) * per - 1 - me))
        loop(jnp.maximum(me + 1, g * per), (g + 1) * per, send_beads)

    with jax.named_scope("p_barrier2"):
        @pl.when(me == 0)
        def _():
            loop(0, half, send_group)
            pl.semaphore_wait(barrier, owners - max(1, half * per) + lower)
            first = max(1, half * per)
            loop(0, owners - first, lambda n: send_beads(owners - 1 - n))
            reply_cross()

        @pl.when(me > 0)
        def _():
            loop(lax.div(me + 1, per), tiles, send_group)

        send_ends(BRIM, later=True)

        @pl.when(lower < len(cross))
        def _():
            pl.semaphore_wait(cross_sem, len(cross) - lower)

    with jax.named_scope("p_csend"):
        pack_x(cstream, cxs, ces)
        for s in SIGNS:
            send(COARSE_X, slot_of(s), (s, 0, 0))
        pack_yz(cstream, cys, czs, ces)
        for s in SIGNS:
            send(COARSE_Y, slot_of(s), (0, s, 0))
            send(COARSE_Z, slot_of(s), (0, 0, s))
        for n, i in enumerate(EDGES):
            send(COARSE_EDGE, n, VELOCITIES[i])
        for n in range(2):
            fzs[n] = jnp.zeros((ny, LANES), f32)
        send_ends(HALO, later=True)
        force[...] = jnp.zeros_like(force)
        halo_force[...] = jnp.zeros_like(halo_force)

    bins_y, bins_z = ny // 2, nz // BIN_Z
    bins_xy = (nx // 2) * bins_y
    near = jnp.where(sub < per, 0, 1)

    def gathered(t, side_of, mine):
        source = [
            [
                jnp.broadcast_to(bead_recv[t * per + j, side_of, pl.ds(n, 1), :], (FIELDS, LANES))
                for n in range(FIELDS // per)
            ]
            for j in range(per)
        ]
        both = []
        for rows in source:
            value = rows[0]
            for n in range(1, FIELDS // per):
                value = jnp.where(sub >= n * per, rows[n], value)
            both.append(value)
        where = (diagonal + (per - mine)) & (per - 1)
        tile = None
        for m in range(per):
            mixed = both[m % per]
            for f in range(1, per):
                mixed = jnp.where(turn == f, both[(f + m) % per], mixed)
            if m:
                mixed = pltpu.roll(mixed, slots * m, 1)
            tile = mixed if tile is None else jnp.where(where == m, mixed, tile)
        return tile

    row_i = lax.div(sub, 2).astype(f32)
    row_j = (sub & 1).astype(f32)
    depth = lax.broadcasted_iota(jnp.int32, (BIN_Z, LANES), 0).astype(f32)
    own_rows = lax.broadcasted_iota(jnp.int32, (bins_xy, LANES), 0).astype(f32)
    side_rows = lax.broadcasted_iota(jnp.int32, (bins_y, LANES), 0).astype(f32)
    bf16 = jnp.bfloat16

    def product(t, side_of, first, spots, offset, count):
        mine = lax.rem(lax.rem(gx + (side_of + (ngx - 1)), ngx) * ngy + gy, per)
        tile = gathered(t, side_of, mine)
        number = tile[6:7]
        column = jnp.floor((number + 0.5) * (1.0 / bins_z))
        layer = number - column * bins_z
        dx, dy = first - tile[0:1], row_j - tile[1:2]
        weight = jnp.exp(-0.5 * (dx * dx + dy * dy))
        mask = spots + offset == column
        highs, lows = [], []
        for d in range(3):
            pushed = weight * tile[3 + d : 4 + d]
            high = pushed.astype(bf16).astype(f32)
            low = pushed - high
            for n in range(count):
                highs.append(jnp.where(mask, high[n : n + 1], 0.0))
                lows.append(jnp.where(mask, low[n : n + 1], 0.0))
        lh = jnp.concatenate(highs, axis=0).astype(bf16)
        ll = jnp.concatenate(lows, axis=0).astype(bf16)
        dz = depth - tile[2:3]
        fall = jnp.exp(-0.5 * (dz * dz))
        fh = fall.astype(bf16).astype(f32)
        fl = fall - fh
        rh = jnp.concatenate([jnp.where(layer == n, fh, 0.0) for n in range(bins_z)], axis=0)
        rl = jnp.concatenate([jnp.where(layer == n, fl, 0.0) for n in range(bins_z)], axis=0)
        rh, rl = rh.astype(bf16), rl.astype(bf16)
        return lax.dot_general(
            jnp.concatenate([lh, lh, ll], axis=1),
            jnp.concatenate([rh, rl, rh], axis=1),
            (((1,), (1,)), ((), ())),
            preferred_element_type=f32,
        )

    far = lax.div(2 * gx, ngx)

    with jax.named_scope("p_force"):
        @pl.loop(0, tiles)
        def _(n):
            near = lax.rem(n + jnp.minimum(me, 1), tiles)
            t = near + far * (tiles - 1 - n - near)
            arrived = bead_recv.at[pl.ds(t * per, per)]
            pltpu.make_async_copy(arrived, arrived, tile_sem.at[t]).wait()

            value = product(t, 1, row_i, own_rows, 0.0, 4)
            for d in range(3):
                for i in range(2):
                    for j in range(2):
                        for b in range(nx // 2):
                            start = ((d * 2 + i) * 2 + j) * bins_xy + b * bins_y
                            at = pl.ds((2 * b + i) * ny + j, bins_y, stride=2)
                            force[d, at, :] += value[start : start + bins_y]

            for h in range(2):
                first = float(1 - h)
                value = product(t, 2 * h, first, side_rows, first * (bins_xy - bins_y), 2)
                for d in range(3):
                    for j in range(2):
                        start = (d * 2 + j) * bins_y
                        at = pl.ds(j, bins_y, stride=2)
                        halo_force[h, d, at, :] += value[start : start + bins_y]

    wide_lane = lax.broadcasted_iota(jnp.int32, (ny, LANES), 1)

    def collided(p, rho, m, f):
        inv = 1.0 / rho
        u = [(v + 0.5 * w) * inv for v, w in zip(m, f)]
        return relax(
            p, rho, u, 1.0 - 1.0 / TAU_FINE, 1.0 / TAU_FINE, f, 1.0 - 0.5 / TAU_FINE
        )

    def made_of(rho, m, f):
        inv = 1.0 / rho
        u = [(v + 0.5 * w) * inv for v, w in zip(m, f)]
        return setup(rho, u, 1.0 / TAU_FINE, f, 1.0 - 0.5 / TAU_FINE)

    keep = 1.0 - 1.0 / TAU_FINE

    def rows(n):
        sign = (1 - 2 * n).astype(f32)
        y = (ny - 1) * (1 - n)
        p = [pops[i, rows_at(y), :] for i in range(19)]
        made = made_of(*moments(p), [force[d, rows_at(y), :] for d in range(3)])
        for j, i in enumerate(FACE[1, 1]):
            c = VELOCITIES[i]
            other = FACE[1, -1][j]
            even, odd = halves(i, made)
            block = keep * jnp.where(n == 0, p[i], p[other]) + (even + sign * odd)
            if c[2]:
                block = pltpu.roll(block, (1 if c[2] > 0 else nz - 1) + n * (c[2] * (nz - 2)), 1)
            if c[0]:
                block = pltpu.roll(block, (1 if c[0] > 0 else nx - 1) + n * (c[0] * (nx - 2)), 0)
            fys[n, j] = block

    with jax.named_scope("p_rows"):
        pl.loop(0, 2)(rows)
        for s in SIGNS:
            send(ROWS, slot_of(s), (0, s, 0))
        for n, i in enumerate(EDGES_YZ):
            s = VELOCITIES[i][1]
            block = fys.at[slot_of(s), FACE[1, s].index(i)]
            plan(CORNERS, block, fer.at[n], VELOCITIES[i]).start()

    def end_rows(n):
        sign = (1 - 2 * n).astype(f32)
        y = (ny - 1) * (1 - n)
        for h in range(2):
            made = made_of(
                brim_recv[h, n, 0:1, :],
                [brim_recv[h, n, 1 + d : 2 + d, :] for d in range(3)],
                [halo_force[h, d, pl.ds(y, 1), :] for d in range(3)],
            )
            both = [halves(VELOCITIES.index((s, 1, 0)), made) for s in SIGNS]
            straight = n == h
            even = jnp.where(straight, both[0][0], both[1][0])
            odd = jnp.where(straight, both[0][1], both[1][1])
            fxs[n, h : h + 1, :] = keep * brim_recv[h, n, 4:5, :] + (even + sign * odd)

    with jax.named_scope("p_hwait"):
        arrive(BRIM)

    with jax.named_scope("p_endrows"):
        pl.loop(0, 2)(end_rows)
        for s in SIGNS:
            send(ENDS, slot_of(s), (0, s, 0))

    def collide(p, rho, m, f, x):
        post = collided(p, rho, m, f)
        columns = [fzs[n] for n in range(2)]
        for i in range(19):
            c = VELOCITIES[i]
            if post[i] is None:
                continue
            at = x + c[0] if isinstance(x, int) else lax.rem(x + (c[0] + nx), nx)
            plane = moved(post[i], (0, c[1], 0))
            stream[i, plane_at(at)] = moved(plane, (0, 0, c[2]))
            if c[2]:
                n = slot_of(c[2])
                k = FACE[2, c[2]].index(i) * nx + at
                turned = pltpu.roll(plane, lax.rem(k + (1 - n), LANES), 1)
                columns[n] = jnp.where(wide_lane == k, turned, columns[n])
        for n in range(2):
            fzs[n] = columns[n]

    def collide_own(x):
        p = [pops[i, plane_at(x)] for i in range(19)]
        rho, m = moments(p)
        collide(p, rho, m, [force[d, plane_at(x)] for d in range(3)], x)

    with jax.named_scope("p_collide"):
        pl.loop(0, nx)(collide_own)

    with jax.named_scope("p_hwait2"):
        arrive(HALO)

    with jax.named_scope("p_hcollide"):
        for s in SIGNS:
            n = slot_of(s)
            p = [None] * 19
            for j, i in enumerate(FACE[0, s]):
                p[i] = halo_recv[n, 4 + j]
            collide(
                p, halo_recv[n, 0], [halo_recv[n, 1 + d] for d in range(3)],
                [halo_force[n, d] for d in range(3)], -1 if s > 0 else nx,
            )

    with jax.named_scope("p_sendz"):
        for s in SIGNS:
            send(COLUMNS, slot_of(s), (0, 0, s))

    with jax.named_scope("p_coarse"):
        arrive(COARSE_X, COARSE_Y, COARSE_Z, COARSE_EDGE)
        fill_coarse(cstream, cxr, cyr, czr, cer)

    with jax.named_scope("p_ywait"):
        arrive(ROWS, CORNERS, ENDS)

    with jax.named_scope("p_yfill"):
        corner = lax.broadcasted_iota(jnp.int32, (nx, nz), 1)
        row_x = lax.broadcasted_iota(jnp.int32, (nx, nz), 0)
        for s in SIGNS:
            for j, i in enumerate(FACE[1, s]):
                c = VELOCITIES[i]
                block = fyr[slot_of(s), j]
                if c[2]:
                    block = jnp.where(corner == side(c[2], nz), fer[EDGES_YZ.index(i)], block)
                if c[0]:
                    h = slot_of(c[0])
                    end = fxr[slot_of(s), h : h + 1, :]
                    block = jnp.where(row_x == side(c[0], nx), end, block)
                stream[i, rows_at(side(s, ny)), :] = block

    with jax.named_scope("p_zwait"):
        arrive(COLUMNS)

    with jax.named_scope("p_final"):
        sent = bead_recv.at[pl.ds(0, owners - 1)]
        pltpu.make_async_copy(sent, sent, bead_sem).wait()
        leave(*range(10))


def local(populations, coarse_pops, fine_mask, coarse_mask, bead_data, bead_bins):
    _, nx, ny, nz = populations.shape
    _, hx, hy, hz = coarse_pops.shape
    sizes = tuple(lax.axis_size(axis) for axis in ("gx", "gy", "gz"))
    owners = sizes[0] * sizes[1]
    total = bead_data.shape[4]
    chunks = total // LANES
    slots = total // owners
    per = LANES // slots
    rows = FIELDS // per
    beads = bead_data.reshape(6 * chunks, LANES)
    bins = bead_bins.reshape(chunks, LANES)
    f32, i32 = jnp.float32, jnp.int32
    any_spec = pl.BlockSpec(memory_space=pl.ANY)
    hbm_spec = pl.BlockSpec(memory_space=pltpu.HBM)
    vmem_spec = pl.BlockSpec(memory_space=pltpu.VMEM)
    dma = pltpu.SemaphoreType.DMA

    fine_rim = [(2, 5, nx, nz), (2, ny, LANES), (len(EDGES_YZ), nx, nz)]
    coarse_rim = [(2, 5, hy, hz), (2, 5 * hx, 1, hz), (2, hy, LANES), (12, 1, LANES)]
    shapes = [(19, nx * ny, nz), (2, ny, LANES), coarse_pops.shape]
    vmem = [
        (3, nx * ny, nz), (2, 3, ny, nz),
        (2, 9, ny, nz), (2, 9, ny, nz), (2, 2, 8, nz), (2, 2, 8, nz),
        (FIELDS, LANES), (sizes[1], sizes[0] + 2, rows, LANES), (owners, 3, rows, LANES),
        *fine_rim[:2], (2, 2, nz), (2, 2, nz), *coarse_rim, fine_rim[0], fine_rim[2], *coarse_rim,
    ]
    operands = (
        populations.reshape(19, nx * ny, nz), coarse_pops, fine_mask, coarse_mask, beads, bins
    )
    fine, columns, coarse = pl.pallas_call(
        functools.partial(kernel, sizes, slots),
        out_shape=[jax.ShapeDtypeStruct(shape, f32) for shape in shapes],
        in_specs=[hbm_spec] * 6,
        out_specs=[vmem_spec, any_spec, vmem_spec],
        scratch_shapes=[
            pltpu.VMEM((19, nx * ny, nz), f32),
            pltpu.VMEM((19, hx, hy, hz), f32),
            pltpu.VMEM((nx, ny, nz), i32),
            pltpu.VMEM((hx, hy, hz), i32),
            pltpu.VMEM((6 * chunks, LANES), f32),
            pltpu.VMEM((chunks, LANES), i32),
            pltpu.VMEM((19, ny, nz), f32),
            *[pltpu.VMEM(shape, f32) for shape in vmem],
            dma((7,)),
            dma,
            dma((owners // per,)),
            pltpu.SemaphoreType.REGULAR((owners // per,)),
            pltpu.SemaphoreType.REGULAR,
            dma((10,)),
            dma((10,)),
        ],
        compiler_params=pltpu.CompilerParams(
            collective_id=0, has_side_effects=True, vmem_limit_bytes=LIMIT
        ),
    )(*[pltpu.with_memory_space_constraint(v, pltpu.HBM) for v in operands])
    fine, coarse = pl.pallas_call(
        functools.partial(finish, nx),
        out_shape=[jax.ShapeDtypeStruct(shape, f32) for shape in (shapes[0], shapes[2])],
        in_specs=[vmem_spec] * 3,
        out_specs=[any_spec] * 2,
        scratch_shapes=[pltpu.VMEM((10, nx * ny, nz), f32), dma((8,))],
        compiler_params=pltpu.CompilerParams(vmem_limit_bytes=LIMIT),
    )(fine, columns, coarse)
    return fine.reshape(populations.shape), coarse


def solution(mesh):
    in_specs = (
        P(None, "gx", "gy", "gz"),
        P(None, "gx", "gy", "gz"),
        P("gx", "gy", "gz"),
        P("gx", "gy", "gz"),
        P("gx", "gy", "gz", None, None),
        P("gx", "gy", "gz", None, None),
    )
    out_specs = (P(None, "gx", "gy", "gz"), P(None, "gx", "gy", "gz"))
    return jax.shard_map(local, mesh=mesh, in_specs=in_specs, out_specs=out_specs, check_vma=False)
```

```python
import functools

import jax
import jax.numpy as jnp
from jax import lax
from jax.experimental import pallas as pl
from jax.experimental.pallas import tpu as pltpu
from jax.sharding import PartitionSpec as P

BIN_Z = 32
VELOCITIES = [
    (0, 0, 0), (1, 0, 0), (-1, 0, 0), (0, 1, 0), (0, -1, 0), (0, 0, 1), (0, 0, -1),
    (1, 1, 0), (-1, -1, 0), (1, -1, 0), (-1, 1, 0), (1, 0, 1), (-1, 0, -1), (1, 0, -1),
    (-1, 0, 1), (0, 1, 1), (0, -1, -1), (0, 1, -1), (0, -1, 1),
]
WEIGHTS = [1.0 / 3.0] + [1.0 / 18.0] * 6 + [1.0 / 36.0] * 12
TAU_FINE = 1.2
TAU_COARSE = 0.85
TO_COARSE = 2.0 * TAU_COARSE / TAU_FINE
TO_FINE = TAU_FINE / (2.0 * TAU_COARSE)
LANES = 128
FIELDS = 8
LIMIT = 24 * 2**20
MESH = pl.DeviceIdType.MESH
SIGNS = (1, -1)
FACE = {(a, s): [i for i in range(19) if VELOCITIES[i][a] == s] for a in range(3) for s in SIGNS}
EDGES = [i for i in range(7, 19)]
EDGES_YZ = [i for i in EDGES if not VELOCITIES[i][0]]


def along(vector, c):
    total = None
    for part, sign in zip(vector, c):
        if sign:
            total = part if total is None else (total + part if sign > 0 else total - part)
    return total


def moments(p):
    rho = p[0]
    sums = [None] * 19
    m = [None] * 3
    for i in range(1, 19, 2):
        rho = rho + (p[i] + p[i + 1])
        sums[i] = p[i] - p[i + 1]
        for axis, sign in enumerate(VELOCITIES[i]):
            if sign:
                if m[axis] is None:
                    m[axis] = sums[i]
                else:
                    m[axis] = m[axis] + sums[i] if sign > 0 else m[axis] - sums[i]
    return rho, m


def setup(rho, u, b, force=None, k=0.0):
    scaled = b * rho
    base = scaled * (1.0 - 1.5 * (u[0] * u[0] + u[1] * u[1] + u[2] * u[2]))
    lin = [3.0 * scaled * v for v in u]
    quad = [4.5 * scaled * v for v in u]
    if force is not None:
        base = base - (3.0 * k) * (u[0] * force[0] + u[1] * force[1] + u[2] * force[2])
        lin = [v + (3.0 * k) * f for v, f in zip(lin, force)]
        quad = [v + (9.0 * k) * f for v, f in zip(quad, force)]
    return u, base, lin, quad


def halves(i, made):
    u, base, lin, quad = made
    first = i if i % 2 else i - 1
    c, w = VELOCITIES[first], WEIGHTS[first]
    odd = w * along(lin, c)
    return w * (base + along(u, c) * along(quad, c)), odd if i % 2 else -odd


def relax(p, rho, u, a, b, force=None, k=0.0):
    made = setup(rho, u, b, force, k)
    out = [None] * 19
    if p[0] is not None:
        out[0] = a * p[0] + WEIGHTS[0] * made[1]
    for i in range(1, 19, 2):
        if p[i] is None and p[i + 1] is None:
            continue
        even, odd = halves(i, made)
        if p[i] is not None:
            out[i] = a * p[i] + (even + odd)
        if p[i + 1] is not None:
            out[i + 1] = a * p[i + 1] + (even - odd)
    return out


def parts(x):
    high = x.astype(jnp.bfloat16)
    return high, (x - high.astype(jnp.float32)).astype(jnp.bfloat16)


def times_exact(x, table):
    high, low = parts(x)
    dot = functools.partial(jnp.dot, preferred_element_type=jnp.float32)
    return dot(high, table) + dot(low, table)


def moved(plane, c):
    rows, lanes = plane.shape
    if c[1]:
        plane = pltpu.roll(plane, 1 if c[1] > 0 else rows - 1, 0)
    if c[2]:
        plane = pltpu.roll(plane, 1 if c[2] > 0 else lanes - 1, 1)
    return plane


def side(sign, length):
    return 0 if sign > 0 else length - 1


def slot_of(sign):
    return 0 if sign > 0 else 1


def pack_x(target, xs, es):
    _, fx, fy, fz = target.shape
    row = lax.broadcasted_iota(jnp.int32, (fy, LANES), 0)
    diagonal = row == lax.broadcasted_iota(jnp.int32, (fy, LANES), 1)
    for s in SIGNS:
        for j, i in enumerate(FACE[0, s]):
            plane = target[i, side(s, fx)]
            xs[slot_of(s), j] = plane
            c = VELOCITIES[i]
            if c[1]:
                y = side(c[1], fy)
                es[EDGES.index(i), :, 0:fz] = plane[y : y + 1]
            elif c[2]:
                z = side(c[2], fz)
                turned = jnp.where(diagonal, plane[:, z : z + 1], 0.0)
                es[EDGES.index(i)] = jnp.sum(turned, axis=0, keepdims=True)


def pack_yz(target, ys, zs, es):
    _, fx, fy, fz = target.shape
    lane = lax.broadcasted_iota(jnp.int32, (fy, LANES), 1)
    for s in SIGNS:
        y, z = side(s, fy), side(s, fz)
        for j, i in enumerate(FACE[1, s]):
            for x in range(fx):
                ys[slot_of(s), j * fx + x] = target[i, x, y : y + 1, :]
        packed = jnp.zeros((fy, LANES), jnp.float32)
        for j, i in enumerate(FACE[2, s]):
            for x in range(fx):
                packed = jnp.where(lane == j * fx + x, target[i, x, :, z : z + 1], packed)
        zs[slot_of(s)] = packed
        for i in FACE[2, s]:
            c = VELOCITIES[i]
            if c[1]:
                y = side(c[1], fy)
                es[EDGES.index(i)] = packed[y : y + 1]


def fill_coarse(target, xr, yr, zr, er):
    _, fx, fy, fz = target.shape
    lane = lax.broadcasted_iota(jnp.int32, (fy, LANES), 1)
    row = lax.broadcasted_iota(jnp.int32, (fy, LANES), 0)
    last = lax.broadcasted_iota(jnp.int32, (fy, fz), 1)
    columns = []
    for s in SIGNS:
        column = zr[slot_of(s)]
        for j, i in enumerate(FACE[2, s]):
            c = VELOCITIES[i]
            if c[0]:
                value = jnp.sum(
                    jnp.where(row == lane, er[EDGES.index(i)], 0.0), axis=1, keepdims=True
                )
                column = jnp.where(lane == j * fx + side(c[0], fx), value, column)
            elif c[1]:
                spot = (lane >= j * fx) & (lane < (j + 1) * fx) & (row == side(c[1], fy))
                column = jnp.where(spot, er[EDGES.index(i)], column)
        columns.append(column)
    for i in range(1, 19):
        c = VELOCITIES[i]
        if c[0]:
            target[i, side(c[0], fx)] = xr[slot_of(c[0]), FACE[0, c[0]].index(i)]
        if c[1]:
            y, j = side(c[1], fy), FACE[1, c[1]].index(i)
            for x in range(fx):
                if c[0] and x == side(c[0], fx):
                    piece = er[EDGES.index(i), :, 0:fz]
                else:
                    piece = yr[slot_of(c[1]), j * fx + x]
                target[i, x, y : y + 1, :] = piece
        if c[2]:
            j, column = FACE[2, c[2]].index(i), columns[slot_of(c[2])]
            for x in range(fx):
                k = j * fx + x
                target[i, x] = jnp.where(
                    last == side(c[2], fz), column[:, k : k + 1], target[i, x]
                )


def finish(nx, fine, columns, coarse, fine_out, coarse_out, target, store_sem):
    _, height, nz = fine.shape
    ny = height // nx
    turned = [5, 6, *range(11, 19)]
    parts = [(coarse, coarse_out), (fine.at[0:5], fine_out.at[0:5]), (fine.at[7:11], fine_out.at[7:11])]
    for n in range(0, 10, 2):
        parts.append((target.at[n : n + 2], fine_out.at[turned[n] : turned[n] + 2]))
    stores = [pltpu.make_async_copy(src, dst, store_sem.at[n]) for n, (src, dst) in enumerate(parts)]
    for store in stores[:3]:
        store.start()
    last = lax.broadcasted_iota(jnp.int32, (ny, nz), 1)
    row = lax.broadcasted_iota(jnp.int32, (ny, nz), 0)
    for n, i in enumerate(turned):
        c = VELOCITIES[i]
        column = columns[slot_of(c[2])]
        spot = last == side(c[2], nz)
        if c[1]:
            spot = spot & (row != side(c[1], ny))
        for x in range(nx):
            k = FACE[2, c[2]].index(i) * nx + x
            target[n, x * ny : (x + 1) * ny, :] = jnp.where(
                spot, column[:, k : k + 1], fine[i, x * ny : (x + 1) * ny, :]
            )
        if n % 2:
            stores[3 + n // 2].start()
    for store in stores:
        store.wait()


def repeat(count, act, most=8):
    if count > most:
        pl.loop(0, count)(act)
    else:
        for n in range(count):
            act(n)


def kernel(
    sizes, slots, pop_in, cpop_in, fmask_in, cmask_in, bead_in, bins_in,
    stream, fzr, cstream,
    pops, cpops, fmask, cmask, bead_ref, bins_ref, tall,
    force, halo_force, halo_send, halo_recv, brim_send, brim_recv,
    bead_rows, bead_send, bead_recv, fys, fzs, fxs, fxr, cxs, cys, czs, ces,
    fyr, fer, cxr, cyr, czr, cer,
    in_sem, bead_sem, tile_sem, ready_sem, cross_sem, send_sem, recv_sem,
):
    ngx, ngy, ngz = sizes
    gx, gy, gz = lax.axis_index("gx"), lax.axis_index("gy"), lax.axis_index("gz")
    owners = ngx * ngy
    me = gx * ngy + gy
    nx, ny, nz = fmask.shape
    _, hx, hy, hz = cpops.shape
    chunks = bins_ref.shape[0]
    per = LANES // slots
    tiles = owners // per
    f32 = jnp.float32

    barrier = pltpu.get_barrier_semaphore()
    first = me < per

    def loop(start, stop, act):
        lax.fori_loop(start, stop, lambda n, carry: (act(n), carry)[1], 0)

    def place(o):
        return lax.div(o, ngy), lax.rem(o, ngy), gz

    def greet(o):
        pl.semaphore_signal(barrier, inc=1, device_id=place(o), device_id_type=MESH)

    loop(0, jnp.minimum(me, per), greet)

    def part(x, w):
        return pop_in.at[:, pl.ds(x * ny, w * ny)], pops.at[:, pl.ds(x * ny, w * ny)]

    loads = [
        pltpu.make_async_copy(src, dst, in_sem.at[n])
        for n, src, dst in (
            (0, bead_in, bead_ref), (1, bins_in, bins_ref), (2, *part(0, 2)), (2, *part(nx - 2, 2)),
            (3, cmask_in, cmask), (4, fmask_in, fmask), (5, cpop_in, cpops),
            (6, *part(2, nx - 4)),
        )
    ]
    for load in loads:
        load.start()

    def plane_at(x):
        return pl.ds(x * ny, ny)

    def rows_at(y):
        return pl.ds(y, nx, stride=ny)

    def device(offset):
        return (
            lax.rem(gx + (offset[0] + ngx), ngx),
            lax.rem(gy + (offset[1] + ngy), ngy),
            lax.rem(gz + (offset[2] + ngz), ngz),
        )

    def number(where):
        return (where[0] * ngy + where[1]) * ngz + where[2]

    def cross_peers(act, later):
        mine = number((gx, gy, gz))
        for offset in cross:
            where = device(offset)
            other = number(where)

            @pl.when(other > mine if later else other < mine)
            def _():
                act(where)

    cross = [(0, 0, 1), (0, 0, -1)] + [VELOCITIES[i] for i in EDGES if VELOCITIES[i][2]]
    lower = jnp.int32(0)
    for offset in cross:
        lower = lower + (number(device(offset)) < number((gx, gy, gz))).astype(jnp.int32)

    with jax.named_scope("p_signals"):
        loop(0, owners - jnp.maximum(per, me + 1), lambda n: greet(owners - 1 - n))

        @pl.when(first)
        def _():
            loop(me + 1, per, greet)

        cross_peers(
            lambda where: pl.semaphore_signal(
                barrier, inc=1, device_id=where, device_id_type=MESH
            ),
            later=True,
        )

    lane = lax.broadcasted_iota(jnp.int32, (FIELDS, LANES), 1)
    sub = lax.broadcasted_iota(jnp.int32, (FIELDS, LANES), 0)
    diagonal = (lax.div(lane, slots) + (FIELDS - sub)) & (per - 1)
    turn = sub & (per - 1)

    def put_block(o, block):
        a, b = o // ngy, lax.rem(o, ngy)
        bead_send[b, a + 1] = block

    def pack_chunk(chunk):
        bead_rows[0:6, :] = bead_ref[pl.ds(chunk, 6, stride=chunks), :]
        bead_rows[6:7, :] = bins_ref[pl.ds(chunk, 1), :].astype(f32)
        rows = bead_rows[...]
        turned = rows
        for m in range(1, per):
            turned = jnp.where(turn == m, pltpu.roll(rows, slots * m, 1), turned)
        for k in range(per):
            kept = jnp.where(diagonal == k, turned, 0.0)
            shift = 1
            while shift < per:
                kept = kept + pltpu.roll(kept, FIELDS - shift, 0)
                shift *= 2
            block = [kept[n : n + 1] for n in range(0, FIELDS, per)]
            o = chunk * per + k
            a, b = (o // ngy, o % ngy) if isinstance(o, int) else (lax.div(o, ngy), lax.rem(o, ngy))
            for n, part in enumerate(block):
                bead_send[b, a + 1, pl.ds(n, 1), :] = part

    with jax.named_scope("p_pack"):
        for load in loads[:2]:
            load.wait()
        bead_rows[7:8, :] = jnp.zeros((1, LANES), f32)
        repeat(chunks, pack_chunk)
        for b in range(ngy):
            bead_send[b, 0] = bead_send[b, ngx]
            bead_send[b, ngx + 1] = bead_send[b, 1]
        own_beads = pltpu.make_async_copy(
            bead_send.at[gy, pl.ds(gx, 3)], bead_recv.at[me], tile_sem.at[me // per]
        )
        own_beads.start()

    with jax.named_scope("p_barrier"):
        @pl.when(jnp.logical_not(first))
        def _():
            pl.semaphore_wait(barrier, me + lower)
            loop(
                per, me,
                lambda o: pl.semaphore_signal(
                    ready_sem.at[me // per], inc=1, device_id=place(o), device_id_type=MESH
                ),
            )

    def send_beads(o):
        where = place(o)
        pltpu.make_async_remote_copy(
            src_ref=bead_send.at[where[1], pl.ds(where[0], 3)],
            dst_ref=bead_recv.at[me],
            send_sem=bead_sem,
            recv_sem=tile_sem.at[me // per],
            device_id=where,
            device_id_type=MESH,
        ).start()

    def reply_cross():
        cross_peers(
            lambda where: pl.semaphore_signal(
                cross_sem, inc=1, device_id=where, device_id_type=MESH
            ),
            later=False,
        )

    with jax.named_scope("p_answer"):
        @pl.when(jnp.logical_not(first))
        def _():
            loop(0, me, send_beads)
            reply_cross()

    fold = lax.broadcasted_iota(jnp.int32, (nz, hz), 0) - 2 * lax.broadcasted_iota(
        jnp.int32, (nz, hz), 1
    )
    fold = jnp.where((fold == 0) | (fold == 1), 0.125, 0.0).astype(jnp.bfloat16)
    spread = lax.broadcasted_iota(jnp.int32, (hz, nz), 1) - 2 * lax.broadcasted_iota(
        jnp.int32, (hz, nz), 0
    )
    spread = jnp.where((spread == 0) | (spread == 1), 1.0, 0.0).astype(jnp.bfloat16)

    def prepare(x):
        sums = []
        for q in range(19):
            total = None
            for i in range(2):
                for j in range(2):
                    piece = pops[q, pl.ds((2 * x + i) * ny + j, hy, stride=2), :]
                    total = piece if total is None else total + piece
            sums.append(total)
        restricted = times_exact(jnp.concatenate(sums, axis=0), fold)
        p = [restricted[i * hy : (i + 1) * hy] for i in range(19)]
        rho, m = moments(p)
        inv = 1.0 / rho
        pre = relax(p, rho, [v * inv for v in m], TO_COARSE, 1.0 - TO_COARSE)
        live = cmask[x] == 1
        pre = [jnp.where(live, pre[i], cpops[i, x]) for i in range(19)]
        rho, m = moments(pre)
        inv = 1.0 / rho
        u = [v * inv for v in m]
        down = relax(pre, rho, u, TO_FINE, 1.0 - TO_FINE)
        post = relax(pre, rho, u, 1.0 - 1.0 / TAU_COARSE, 1.0 / TAU_COARSE)
        for i in range(19):
            c = VELOCITIES[i]
            cstream[i, lax.rem(x + (c[0] + hx), hx)] = moved(post[i], c)
        wide = times_exact(jnp.concatenate(down, axis=0), spread)
        for q in range(19):
            value = wide[q * hy : (q + 1) * hy]
            tall[q, pl.ds(0, hy, stride=2), :] = value
            tall[q, pl.ds(1, hy, stride=2), :] = value
        for i in range(2):
            kept = fmask[2 * x + i] == 1
            at = plane_at(2 * x + i)
            for q in range(19):
                pops[q, at] = jnp.where(kept, pops[q, at], tall[q])

    with jax.named_scope("p_ends"):
        pltpu.make_async_copy(*part(0, 4), in_sem.at[2]).wait()
        for load in loads[4:7]:
            load.wait()
        pl.loop(0, 2)(lambda n: prepare(n * (hx - 1)))
        for s in SIGNS:
            x = nx - 1 if s > 0 else 0
            p = [pops[i, plane_at(x)] for i in range(19)]
            rho, m = moments(p)
            for n, value in enumerate([rho, *m, *[p[i] for i in FACE[0, s]]]):
                halo_send[slot_of(s), n] = value
            for t in SIGNS:
                y = ny - 1 if t > 0 else 0
                for n, value in enumerate([rho, *m, p[VELOCITIES.index((s, t, 0))]]):
                    brim_send[slot_of(s), slot_of(t), n : n + 1, :] = value[y : y + 1]

    BRIM, HALO, COARSE_X, COARSE_Y, COARSE_Z, COARSE_EDGE, ROWS, CORNERS, ENDS, COLUMNS = range(10)
    buffers = [
        (brim_send, brim_recv), (halo_send, halo_recv),
        (cxs, cxr), (cys, cyr), (czs, czr), (ces, cer),
        (fys, fyr), (fer, fer), (fxs, fxr), (fzs, fzr),
    ]

    def move(kind, src, dst, where):
        return pltpu.make_async_remote_copy(
            src_ref=src, dst_ref=dst, send_sem=send_sem.at[kind], recv_sem=recv_sem.at[kind],
            device_id=where, device_id_type=MESH,
        )

    def plan(kind, src, dst, offset):
        return move(kind, src, dst, device(offset))

    def send(kind, part, offset):
        src, dst = buffers[kind]
        plan(kind, src.at[part], dst.at[part], offset).start()

    def arrive(*kinds):
        for kind in kinds:
            dst = buffers[kind][1]
            pltpu.make_async_copy(dst, dst, recv_sem.at[kind]).wait()

    def leave(*kinds):
        for kind in kinds:
            src = buffers[kind][0]
            pltpu.make_async_copy(src, src, send_sem.at[kind]).wait()

    def send_ends(kind, later, signs=SIGNS):
        for s in signs:
            other = number(device((s, 0, 0)))
            mine = number((gx, gy, gz))

            @pl.when(other > mine if later else other < mine)
            def _():
                send(kind, slot_of(s), (s, 0, 0))

    @pl.when(jnp.logical_not(first))
    def _():
        send_ends(BRIM, later=False)
        send_ends(HALO, later=False)

    with jax.named_scope("p_middle"):
        for load in loads[7:]:
            load.wait()
        pl.loop(1, hx - 1)(prepare)

    def send_group(g):
        pl.semaphore_wait(ready_sem.at[g], jnp.minimum(per, (g + 1) * per - 1 - me))
        loop(jnp.maximum(me + 1, g * per), (g + 1) * per, send_beads)

    with jax.named_scope("p_barrier2"):
        @pl.when(first)
        def _():
            pl.semaphore_wait(barrier, owners - 1 + lower)
            loop(0, me, send_beads)
            loop(me + 1, owners, send_beads)
            reply_cross()
            send_ends(BRIM, later=False)
            send_ends(HALO, later=False)

        @pl.when(jnp.logical_not(first))
        def _():
            loop(lax.div(me + 1, per), tiles, send_group)

        send_ends(BRIM, later=True)

        @pl.when(lower < len(cross))
        def _():
            pl.semaphore_wait(cross_sem, len(cross) - lower)

    with jax.named_scope("p_csend"):
        pack_x(cstream, cxs, ces)
        for s in SIGNS:
            send(COARSE_X, slot_of(s), (s, 0, 0))
        pack_yz(cstream, cys, czs, ces)
        for s in SIGNS:
            send(COARSE_Y, slot_of(s), (0, s, 0))
            send(COARSE_Z, slot_of(s), (0, 0, s))
        for n, i in enumerate(EDGES):
            send(COARSE_EDGE, n, VELOCITIES[i])
        for n in range(2):
            fzs[n] = jnp.zeros((ny, LANES), f32)
        send_ends(HALO, later=True, signs=(1,))
        force[...] = jnp.zeros_like(force)
        halo_force[...] = jnp.zeros_like(halo_force)

    bins_y, bins_z = ny // 2, nz // BIN_Z
    bins_xy = (nx // 2) * bins_y
    near = jnp.where(sub < per, 0, 1)

    def gathered(t, side_of, mine):
        source = [
            [
                jnp.broadcast_to(bead_recv[t * per + j, side_of, pl.ds(n, 1), :], (FIELDS, LANES))
                for n in range(FIELDS // per)
            ]
            for j in range(per)
        ]
        both = []
        for rows in source:
            value = rows[0]
            for n in range(1, FIELDS // per):
                value = jnp.where(sub >= n * per, rows[n], value)
            both.append(value)
        where = (diagonal + (per - mine)) & (per - 1)
        tile = None
        for m in range(per):
            mixed = both[m % per]
            for f in range(1, per):
                mixed = jnp.where(turn == f, both[(f + m) % per], mixed)
            if m:
                mixed = pltpu.roll(mixed, slots * m, 1)
            tile = mixed if tile is None else jnp.where(where == m, mixed, tile)
        return tile

    row_i = lax.div(sub, 2).astype(f32)
    row_j = (sub & 1).astype(f32)
    depth = lax.broadcasted_iota(jnp.int32, (BIN_Z, LANES), 0).astype(f32)
    own_rows = lax.broadcasted_iota(jnp.int32, (bins_xy, LANES), 0).astype(f32)
    side_rows = lax.broadcasted_iota(jnp.int32, (bins_y, LANES), 0).astype(f32)
    bf16 = jnp.bfloat16

    def product(t, side_of, first, spots, offset, count):
        mine = lax.rem(lax.rem(gx + (side_of + (ngx - 1)), ngx) * ngy + gy, per)
        tile = gathered(t, side_of, mine)
        number = tile[6:7]
        column = jnp.floor((number + 0.5) * (1.0 / bins_z))
        layer = number - column * bins_z
        dx, dy = first - tile[0:1], row_j - tile[1:2]
        weight = jnp.exp(-0.5 * (dx * dx + dy * dy))
        mask = spots + offset == column
        highs, lows = [], []
        for d in range(3):
            pushed = weight * tile[3 + d : 4 + d]
            high = pushed.astype(bf16).astype(f32)
            low = pushed - high
            for n in range(count):
                highs.append(jnp.where(mask, high[n : n + 1], 0.0))
                lows.append(jnp.where(mask, low[n : n + 1], 0.0))
        lh = jnp.concatenate(highs, axis=0).astype(bf16)
        ll = jnp.concatenate(lows, axis=0).astype(bf16)
        dz = depth - tile[2:3]
        fall = jnp.exp(-0.5 * (dz * dz))
        fh = fall.astype(bf16).astype(f32)
        fl = fall - fh
        rh = jnp.concatenate([jnp.where(layer == n, fh, 0.0) for n in range(bins_z)], axis=0)
        rl = jnp.concatenate([jnp.where(layer == n, fl, 0.0) for n in range(bins_z)], axis=0)
        rh, rl = rh.astype(bf16), rl.astype(bf16)
        return lax.dot_general(
            jnp.concatenate([lh, lh, ll], axis=1),
            jnp.concatenate([rh, rl, rh], axis=1),
            (((1,), (1,)), ((), ())),
            preferred_element_type=f32,
        )

    far = lax.div(2 * gx, ngx)

    with jax.named_scope("p_force"):
        @pl.loop(0, tiles)
        def _(n):
            near = (1 - lax.div(n + 2, tiles)) * (n + 1) + lax.div(n + 1, tiles) * (tiles - 1)
            t = near + far * (tiles - 1 - n - near)
            arrived = bead_recv.at[pl.ds(t * per, per)]
            pltpu.make_async_copy(arrived, arrived, tile_sem.at[t]).wait()

            value = product(t, 1, row_i, own_rows, 0.0, 4)
            for d in range(3):
                for i in range(2):
                    for j in range(2):
                        for b in range(nx // 2):
                            start = ((d * 2 + i) * 2 + j) * bins_xy + b * bins_y
                            at = pl.ds((2 * b + i) * ny + j, bins_y, stride=2)
                            force[d, at, :] += value[start : start + bins_y]

            for h in range(2):
                first = float(1 - h)
                value = product(t, 2 * h, first, side_rows, first * (bins_xy - bins_y), 2)
                for d in range(3):
                    for j in range(2):
                        start = (d * 2 + j) * bins_y
                        at = pl.ds(j, bins_y, stride=2)
                        halo_force[h, d, at, :] += value[start : start + bins_y]

    send_ends(HALO, later=True, signs=(-1,))

    wide_lane = lax.broadcasted_iota(jnp.int32, (ny, LANES), 1)

    def collided(p, rho, m, f):
        inv = 1.0 / rho
        u = [(v + 0.5 * w) * inv for v, w in zip(m, f)]
        return relax(
            p, rho, u, 1.0 - 1.0 / TAU_FINE, 1.0 / TAU_FINE, f, 1.0 - 0.5 / TAU_FINE
        )

    def made_of(rho, m, f):
        inv = 1.0 / rho
        u = [(v + 0.5 * w) * inv for v, w in zip(m, f)]
        return setup(rho, u, 1.0 / TAU_FINE, f, 1.0 - 0.5 / TAU_FINE)

    keep = 1.0 - 1.0 / TAU_FINE

    def rows(n):
        sign = (1 - 2 * n).astype(f32)
        y = (ny - 1) * (1 - n)
        p = [pops[i, rows_at(y), :] for i in range(19)]
        made = made_of(*moments(p), [force[d, rows_at(y), :] for d in range(3)])
        for j, i in enumerate(FACE[1, 1]):
            c = VELOCITIES[i]
            other = FACE[1, -1][j]
            even, odd = halves(i, made)
            block = keep * jnp.where(n == 0, p[i], p[other]) + (even + sign * odd)
            if c[2]:
                block = pltpu.roll(block, (1 if c[2] > 0 else nz - 1) + n * (c[2] * (nz - 2)), 1)
            if c[0]:
                block = pltpu.roll(block, (1 if c[0] > 0 else nx - 1) + n * (c[0] * (nx - 2)), 0)
            fys[n, j] = block
        where = (gx, lax.rem(gy + (1 - 2 * n) + ngy, ngy), gz)
        move(ROWS, fys.at[n], fyr.at[n], where).start()

    with jax.named_scope("p_rows"):
        pl.loop(0, 2)(rows)
        for n, i in enumerate(EDGES_YZ):
            s = VELOCITIES[i][1]
            block = fys.at[slot_of(s), FACE[1, s].index(i)]
            plan(CORNERS, block, fer.at[n], VELOCITIES[i]).start()

    def end_rows(n):
        sign = (1 - 2 * n).astype(f32)
        y = (ny - 1) * (1 - n)
        for h in range(2):
            made = made_of(
                brim_recv[h, n, 0:1, :],
                [brim_recv[h, n, 1 + d : 2 + d, :] for d in range(3)],
                [halo_force[h, d, pl.ds(y, 1), :] for d in range(3)],
            )
            both = [halves(VELOCITIES.index((s, 1, 0)), made) for s in SIGNS]
            straight = n == h
            even = jnp.where(straight, both[0][0], both[1][0])
            odd = jnp.where(straight, both[0][1], both[1][1])
            fxs[n, h : h + 1, :] = keep * brim_recv[h, n, 4:5, :] + (even + sign * odd)

    with jax.named_scope("p_hwait"):
        arrive(BRIM)

    with jax.named_scope("p_endrows"):
        pl.loop(0, 2)(end_rows)
        for s in SIGNS:
            send(ENDS, slot_of(s), (0, s, 0))

    def collide(p, rho, m, f, x):
        post = collided(p, rho, m, f)
        columns = [fzs[n] for n in range(2)]
        for i in range(19):
            c = VELOCITIES[i]
            if post[i] is None:
                continue
            at = x + c[0] if isinstance(x, int) else lax.rem(x + (c[0] + nx), nx)
            plane = moved(post[i], (0, c[1], 0))
            stream[i, plane_at(at)] = moved(plane, (0, 0, c[2]))
            if c[2]:
                n = slot_of(c[2])
                k = FACE[2, c[2]].index(i) * nx + at
                turned = pltpu.roll(plane, lax.rem(k + (1 - n), LANES), 1)
                columns[n] = jnp.where(wide_lane == k, turned, columns[n])
        for n in range(2):
            fzs[n] = columns[n]

    def collide_own(x):
        p = [pops[i, plane_at(x)] for i in range(19)]
        rho, m = moments(p)
        collide(p, rho, m, [force[d, plane_at(x)] for d in range(3)], x)

    with jax.named_scope("p_collide"):
        pl.loop(0, nx)(collide_own)

    with jax.named_scope("p_hwait2"):
        arrive(HALO)

    with jax.named_scope("p_hcollide"):
        for s in SIGNS:
            n = slot_of(s)
            p = [None] * 19
            for j, i in enumerate(FACE[0, s]):
                p[i] = halo_recv[n, 4 + j]
            collide(
                p, halo_recv[n, 0], [halo_recv[n, 1 + d] for d in range(3)],
                [halo_force[n, d] for d in range(3)], -1 if s > 0 else nx,
            )

    with jax.named_scope("p_sendz"):
        for s in SIGNS:
            send(COLUMNS, slot_of(s), (0, 0, s))

    with jax.named_scope("p_coarse"):
        arrive(COARSE_X, COARSE_Y, COARSE_Z, COARSE_EDGE)
        fill_coarse(cstream, cxr, cyr, czr, cer)

    with jax.named_scope("p_ywait"):
        arrive(ROWS, CORNERS, ENDS)

    with jax.named_scope("p_yfill"):
        corner = lax.broadcasted_iota(jnp.int32, (nx, nz), 1)
        row_x = lax.broadcasted_iota(jnp.int32, (nx, nz), 0)
        for s in SIGNS:
            for j, i in enumerate(FACE[1, s]):
                c = VELOCITIES[i]
                block = fyr[slot_of(s), j]
                if c[2]:
                    block = jnp.where(corner == side(c[2], nz), fer[EDGES_YZ.index(i)], block)
                if c[0]:
                    h = slot_of(c[0])
                    end = fxr[slot_of(s), h : h + 1, :]
                    block = jnp.where(row_x == side(c[0], nx), end, block)
                stream[i, rows_at(side(s, ny)), :] = block

    with jax.named_scope("p_zwait"):
        arrive(COLUMNS)

    with jax.named_scope("p_final"):
        sent = bead_recv.at[pl.ds(0, owners - 1)]
        pltpu.make_async_copy(sent, sent, bead_sem).wait()
        leave(*range(10))


def local(populations, coarse_pops, fine_mask, coarse_mask, bead_data, bead_bins):
    _, nx, ny, nz = populations.shape
    _, hx, hy, hz = coarse_pops.shape
    sizes = tuple(lax.axis_size(axis) for axis in ("gx", "gy", "gz"))
    owners = sizes[0] * sizes[1]
    total = bead_data.shape[4]
    chunks = total // LANES
    slots = total // owners
    per = LANES // slots
    rows = FIELDS // per
    beads = bead_data.reshape(6 * chunks, LANES)
    bins = bead_bins.reshape(chunks, LANES)
    f32, i32 = jnp.float32, jnp.int32
    any_spec = pl.BlockSpec(memory_space=pl.ANY)
    hbm_spec = pl.BlockSpec(memory_space=pltpu.HBM)
    vmem_spec = pl.BlockSpec(memory_space=pltpu.VMEM)
    dma = pltpu.SemaphoreType.DMA

    fine_rim = [(2, 5, nx, nz), (2, ny, LANES), (len(EDGES_YZ), nx, nz)]
    coarse_rim = [(2, 5, hy, hz), (2, 5 * hx, 1, hz), (2, hy, LANES), (12, 1, LANES)]
    shapes = [(19, nx * ny, nz), (2, ny, LANES), coarse_pops.shape]
    vmem = [
        (3, nx * ny, nz), (2, 3, ny, nz),
        (2, 9, ny, nz), (2, 9, ny, nz), (2, 2, 8, nz), (2, 2, 8, nz),
        (FIELDS, LANES), (sizes[1], sizes[0] + 2, rows, LANES), (owners, 3, rows, LANES),
        *fine_rim[:2], (2, 2, nz), (2, 2, nz), *coarse_rim, fine_rim[0], fine_rim[2], *coarse_rim,
    ]
    operands = (
        populations.reshape(19, nx * ny, nz), coarse_pops, fine_mask, coarse_mask, beads, bins
    )
    fine, columns, coarse = pl.pallas_call(
        functools.partial(kernel, sizes, slots),
        out_shape=[jax.ShapeDtypeStruct(shape, f32) for shape in shapes],
        in_specs=[hbm_spec] * 6,
        out_specs=[vmem_spec, any_spec, vmem_spec],
        scratch_shapes=[
            pltpu.VMEM((19, nx * ny, nz), f32),
            pltpu.VMEM((19, hx, hy, hz), f32),
            pltpu.VMEM((nx, ny, nz), i32),
            pltpu.VMEM((hx, hy, hz), i32),
            pltpu.VMEM((6 * chunks, LANES), f32),
            pltpu.VMEM((chunks, LANES), i32),
            pltpu.VMEM((19, ny, nz), f32),
            *[pltpu.VMEM(shape, f32) for shape in vmem],
            dma((7,)),
            dma,
            dma((owners // per,)),
            pltpu.SemaphoreType.REGULAR((owners // per,)),
            pltpu.SemaphoreType.REGULAR,
            dma((10,)),
            dma((10,)),
        ],
        compiler_params=pltpu.CompilerParams(
            collective_id=0, has_side_effects=True, vmem_limit_bytes=LIMIT
        ),
    )(*[pltpu.with_memory_space_constraint(v, pltpu.HBM) for v in operands])
    fine, coarse = pl.pallas_call(
        functools.partial(finish, nx),
        out_shape=[jax.ShapeDtypeStruct(shape, f32) for shape in (shapes[0], shapes[2])],
        in_specs=[vmem_spec] * 3,
        out_specs=[any_spec] * 2,
        scratch_shapes=[pltpu.VMEM((10, nx * ny, nz), f32), dma((8,))],
        compiler_params=pltpu.CompilerParams(vmem_limit_bytes=LIMIT),
    )(fine, columns, coarse)
    return fine.reshape(populations.shape), coarse


def solution(mesh):
    in_specs = (
        P(None, "gx", "gy", "gz"),
        P(None, "gx", "gy", "gz"),
        P("gx", "gy", "gz"),
        P("gx", "gy", "gz"),
        P("gx", "gy", "gz", None, None),
        P("gx", "gy", "gz", None, None),
    )
    out_specs = (P(None, "gx", "gy", "gz"), P(None, "gx", "gy", "gz"))
    return jax.shard_map(local, mesh=mesh, in_specs=in_specs, out_specs=out_specs, check_vma=False)
```

```python
import functools

import jax
import jax.numpy as jnp
from jax import lax
from jax.experimental import pallas as pl
from jax.experimental.pallas import tpu as pltpu
from jax.sharding import PartitionSpec as P

BIN_Z = 32
VELOCITIES = [
    (0, 0, 0), (1, 0, 0), (-1, 0, 0), (0, 1, 0), (0, -1, 0), (0, 0, 1), (0, 0, -1),
    (1, 1, 0), (-1, -1, 0), (1, -1, 0), (-1, 1, 0), (1, 0, 1), (-1, 0, -1), (1, 0, -1),
    (-1, 0, 1), (0, 1, 1), (0, -1, -1), (0, 1, -1), (0, -1, 1),
]
WEIGHTS = [1.0 / 3.0] + [1.0 / 18.0] * 6 + [1.0 / 36.0] * 12
TAU_FINE = 1.2
TAU_COARSE = 0.85
TO_COARSE = 2.0 * TAU_COARSE / TAU_FINE
TO_FINE = TAU_FINE / (2.0 * TAU_COARSE)
LANES = 128
FIELDS = 8
LIMIT = 24 * 2**20
MESH = pl.DeviceIdType.MESH
SIGNS = (1, -1)
FACE = {(a, s): [i for i in range(19) if VELOCITIES[i][a] == s] for a in range(3) for s in SIGNS}
EDGES = [i for i in range(7, 19)]
EDGES_YZ = [i for i in EDGES if not VELOCITIES[i][0]]


def along(vector, c):
    total = None
    for part, sign in zip(vector, c):
        if sign:
            total = part if total is None else (total + part if sign > 0 else total - part)
    return total


def moments(p):
    rho = p[0]
    sums = [None] * 19
    m = [None] * 3
    for i in range(1, 19, 2):
        rho = rho + (p[i] + p[i + 1])
        sums[i] = p[i] - p[i + 1]
        for axis, sign in enumerate(VELOCITIES[i]):
            if sign:
                if m[axis] is None:
                    m[axis] = sums[i]
                else:
                    m[axis] = m[axis] + sums[i] if sign > 0 else m[axis] - sums[i]
    return rho, m


def setup(rho, u, b, force=None, k=0.0):
    scaled = b * rho
    base = scaled * (1.0 - 1.5 * (u[0] * u[0] + u[1] * u[1] + u[2] * u[2]))
    lin = [3.0 * scaled * v for v in u]
    quad = [4.5 * scaled * v for v in u]
    if force is not None:
        base = base - (3.0 * k) * (u[0] * force[0] + u[1] * force[1] + u[2] * force[2])
        lin = [v + (3.0 * k) * f for v, f in zip(lin, force)]
        quad = [v + (9.0 * k) * f for v, f in zip(quad, force)]
    return u, base, lin, quad


def halves(i, made):
    u, base, lin, quad = made
    first = i if i % 2 else i - 1
    c, w = VELOCITIES[first], WEIGHTS[first]
    odd = w * along(lin, c)
    return w * (base + along(u, c) * along(quad, c)), odd if i % 2 else -odd


def relax(p, rho, u, a, b, force=None, k=0.0):
    made = setup(rho, u, b, force, k)
    out = [None] * 19
    if p[0] is not None:
        out[0] = a * p[0] + WEIGHTS[0] * made[1]
    for i in range(1, 19, 2):
        if p[i] is None and p[i + 1] is None:
            continue
        even, odd = halves(i, made)
        if p[i] is not None:
            out[i] = a * p[i] + (even + odd)
        if p[i + 1] is not None:
            out[i + 1] = a * p[i + 1] + (even - odd)
    return out


def parts(x):
    high = x.astype(jnp.bfloat16)
    return high, (x - high.astype(jnp.float32)).astype(jnp.bfloat16)


def times_exact(x, table):
    high, low = parts(x)
    dot = functools.partial(jnp.dot, preferred_element_type=jnp.float32)
    return dot(high, table) + dot(low, table)


def moved(plane, c):
    rows, lanes = plane.shape
    if c[1]:
        plane = pltpu.roll(plane, 1 if c[1] > 0 else rows - 1, 0)
    if c[2]:
        plane = pltpu.roll(plane, 1 if c[2] > 0 else lanes - 1, 1)
    return plane


def side(sign, length):
    return 0 if sign > 0 else length - 1


def slot_of(sign):
    return 0 if sign > 0 else 1


def pack_x(target, xs, es):
    _, fx, fy, fz = target.shape
    row = lax.broadcasted_iota(jnp.int32, (fy, LANES), 0)
    diagonal = row == lax.broadcasted_iota(jnp.int32, (fy, LANES), 1)
    for s in SIGNS:
        for j, i in enumerate(FACE[0, s]):
            plane = target[i, side(s, fx)]
            xs[slot_of(s), j] = plane
            c = VELOCITIES[i]
            if c[1]:
                y = side(c[1], fy)
                es[EDGES.index(i), :, 0:fz] = plane[y : y + 1]
            elif c[2]:
                z = side(c[2], fz)
                turned = jnp.where(diagonal, plane[:, z : z + 1], 0.0)
                es[EDGES.index(i)] = jnp.sum(turned, axis=0, keepdims=True)


def pack_yz(target, ys, zs, es):
    _, fx, fy, fz = target.shape
    lane = lax.broadcasted_iota(jnp.int32, (fy, LANES), 1)
    for s in SIGNS:
        y, z = side(s, fy), side(s, fz)
        for j, i in enumerate(FACE[1, s]):
            for x in range(fx):
                ys[slot_of(s), j * fx + x] = target[i, x, y : y + 1, :]
        packed = jnp.zeros((fy, LANES), jnp.float32)
        for j, i in enumerate(FACE[2, s]):
            for x in range(fx):
                packed = jnp.where(lane == j * fx + x, target[i, x, :, z : z + 1], packed)
        zs[slot_of(s)] = packed
        for i in FACE[2, s]:
            c = VELOCITIES[i]
            if c[1]:
                y = side(c[1], fy)
                es[EDGES.index(i)] = packed[y : y + 1]


def fill_coarse(target, xr, yr, zr, er):
    _, fx, fy, fz = target.shape
    lane = lax.broadcasted_iota(jnp.int32, (fy, LANES), 1)
    row = lax.broadcasted_iota(jnp.int32, (fy, LANES), 0)
    last = lax.broadcasted_iota(jnp.int32, (fy, fz), 1)
    columns = []
    for s in SIGNS:
        column = zr[slot_of(s)]
        for j, i in enumerate(FACE[2, s]):
            c = VELOCITIES[i]
            if c[0]:
                value = jnp.sum(
                    jnp.where(row == lane, er[EDGES.index(i)], 0.0), axis=1, keepdims=True
                )
                column = jnp.where(lane == j * fx + side(c[0], fx), value, column)
            elif c[1]:
                spot = (lane >= j * fx) & (lane < (j + 1) * fx) & (row == side(c[1], fy))
                column = jnp.where(spot, er[EDGES.index(i)], column)
        columns.append(column)
    for i in range(1, 19):
        c = VELOCITIES[i]
        if c[0]:
            target[i, side(c[0], fx)] = xr[slot_of(c[0]), FACE[0, c[0]].index(i)]
        if c[1]:
            y, j = side(c[1], fy), FACE[1, c[1]].index(i)
            for x in range(fx):
                if c[0] and x == side(c[0], fx):
                    piece = er[EDGES.index(i), :, 0:fz]
                else:
                    piece = yr[slot_of(c[1]), j * fx + x]
                target[i, x, y : y + 1, :] = piece
        if c[2]:
            j, column = FACE[2, c[2]].index(i), columns[slot_of(c[2])]
            for x in range(fx):
                k = j * fx + x
                target[i, x] = jnp.where(
                    last == side(c[2], fz), column[:, k : k + 1], target[i, x]
                )


def finish(nx, fine, columns, coarse, fine_out, coarse_out, target, store_sem):
    _, height, nz = fine.shape
    ny = height // nx
    turned = [5, 6, *range(11, 19)]
    parts = [(coarse, coarse_out), (fine.at[0:5], fine_out.at[0:5]), (fine.at[7:11], fine_out.at[7:11])]
    for n in range(0, 10, 2):
        parts.append((target.at[n : n + 2], fine_out.at[turned[n] : turned[n] + 2]))
    stores = [pltpu.make_async_copy(src, dst, store_sem.at[n]) for n, (src, dst) in enumerate(parts)]
    for store in stores[:3]:
        store.start()
    last = lax.broadcasted_iota(jnp.int32, (ny, nz), 1)
    row = lax.broadcasted_iota(jnp.int32, (ny, nz), 0)
    for n, i in enumerate(turned):
        c = VELOCITIES[i]
        column = columns[slot_of(c[2])]
        spot = last == side(c[2], nz)
        if c[1]:
            spot = spot & (row != side(c[1], ny))
        for x in range(nx):
            k = FACE[2, c[2]].index(i) * nx + x
            target[n, x * ny : (x + 1) * ny, :] = jnp.where(
                spot, column[:, k : k + 1], fine[i, x * ny : (x + 1) * ny, :]
            )
        if n % 2:
            stores[3 + n // 2].start()
    for store in stores:
        store.wait()


def repeat(count, act, most=8):
    if count > most:
        pl.loop(0, count)(act)
    else:
        for n in range(count):
            act(n)


def kernel(
    sizes, slots, pop_in, cpop_in, fmask_in, cmask_in, bead_in, bins_in,
    stream, fzr, cstream,
    pops, cpops, fmask, cmask, bead_ref, bins_ref, tall,
    force, halo_force, halo_send, halo_recv, brim_send, brim_recv,
    bead_rows, bead_send, bead_recv, fys, fzs, fxs, fxr, cxs, cys, czs, ces,
    fyr, fer, cxr, cyr, czr, cer,
    in_sem, bead_sem, tile_sem, ready_sem, cross_sem, send_sem, recv_sem,
):
    ngx, ngy, ngz = sizes
    gx, gy, gz = lax.axis_index("gx"), lax.axis_index("gy"), lax.axis_index("gz")
    owners = ngx * ngy
    me = gx * ngy + gy
    nx, ny, nz = fmask.shape
    _, hx, hy, hz = cpops.shape
    chunks = bins_ref.shape[0]
    per = LANES // slots
    tiles = owners // per
    f32 = jnp.float32

    barrier = pltpu.get_barrier_semaphore()
    heads = ngy
    first = me < heads

    def loop(start, stop, act):
        lax.fori_loop(start, stop, lambda n, carry: (act(n), carry)[1], 0)

    def place(o):
        return lax.div(o, ngy), lax.rem(o, ngy), gz

    def greet(o):
        pl.semaphore_signal(barrier, inc=1, device_id=place(o), device_id_type=MESH)

    loop(0, jnp.minimum(me, heads), greet)

    def part(x, w):
        return pop_in.at[:, pl.ds(x * ny, w * ny)], pops.at[:, pl.ds(x * ny, w * ny)]

    loads = [
        pltpu.make_async_copy(src, dst, in_sem.at[n])
        for n, src, dst in (
            (0, bead_in, bead_ref), (1, bins_in, bins_ref), (2, *part(0, 2)), (2, *part(nx - 2, 2)),
            (3, cmask_in, cmask), (4, fmask_in, fmask), (5, cpop_in, cpops),
            (6, *part(2, nx - 4)),
        )
    ]
    for load in loads:
        load.start()

    def plane_at(x):
        return pl.ds(x * ny, ny)

    def rows_at(y):
        return pl.ds(y, nx, stride=ny)

    def device(offset):
        return (
            lax.rem(gx + (offset[0] + ngx), ngx),
            lax.rem(gy + (offset[1] + ngy), ngy),
            lax.rem(gz + (offset[2] + ngz), ngz),
        )

    def number(where):
        return (where[0] * ngy + where[1]) * ngz + where[2]

    def cross_peers(act, later):
        mine = number((gx, gy, gz))
        for offset in cross:
            where = device(offset)
            other = number(where)

            @pl.when(other > mine if later else other < mine)
            def _():
                act(where)

    cross = [(0, 0, 1), (0, 0, -1)] + [VELOCITIES[i] for i in EDGES if VELOCITIES[i][2]]
    lower = jnp.int32(0)
    for offset in cross:
        lower = lower + (number(device(offset)) < number((gx, gy, gz))).astype(jnp.int32)

    with jax.named_scope("p_signals"):
        loop(0, owners - jnp.maximum(heads, me + 1), lambda n: greet(owners - 1 - n))

        @pl.when(first)
        def _():
            loop(me + 1, heads, greet)

        cross_peers(
            lambda where: pl.semaphore_signal(
                barrier, inc=1, device_id=where, device_id_type=MESH
            ),
            later=True,
        )

    lane = lax.broadcasted_iota(jnp.int32, (FIELDS, LANES), 1)
    sub = lax.broadcasted_iota(jnp.int32, (FIELDS, LANES), 0)
    diagonal = (lax.div(lane, slots) + (FIELDS - sub)) & (per - 1)
    turn = sub & (per - 1)

    def put_block(o, block):
        a, b = o // ngy, lax.rem(o, ngy)
        bead_send[b, a + 1] = block

    def pack_chunk(chunk):
        bead_rows[0:6, :] = bead_ref[pl.ds(chunk, 6, stride=chunks), :]
        bead_rows[6:7, :] = bins_ref[pl.ds(chunk, 1), :].astype(f32)
        rows = bead_rows[...]
        turned = rows
        for m in range(1, per):
            turned = jnp.where(turn == m, pltpu.roll(rows, slots * m, 1), turned)
        for k in range(per):
            kept = jnp.where(diagonal == k, turned, 0.0)
            shift = 1
            while shift < per:
                kept = kept + pltpu.roll(kept, FIELDS - shift, 0)
                shift *= 2
            block = [kept[n : n + 1] for n in range(0, FIELDS, per)]
            o = chunk * per + k
            a, b = (o // ngy, o % ngy) if isinstance(o, int) else (lax.div(o, ngy), lax.rem(o, ngy))
            for n, part in enumerate(block):
                bead_send[b, a + 1, pl.ds(n, 1), :] = part

    with jax.named_scope("p_pack"):
        for load in loads[:2]:
            load.wait()
        bead_rows[7:8, :] = jnp.zeros((1, LANES), f32)
        repeat(chunks, pack_chunk)
        for b in range(ngy):
            bead_send[b, 0] = bead_send[b, ngx]
            bead_send[b, ngx + 1] = bead_send[b, 1]
        own_beads = pltpu.make_async_copy(
            bead_send.at[gy, pl.ds(gx, 3)], bead_recv.at[me], tile_sem.at[me // per]
        )
        own_beads.start()

    def send_beads(o):
        where = place(o)
        pltpu.make_async_remote_copy(
            src_ref=bead_send.at[where[1], pl.ds(where[0], 3)],
            dst_ref=bead_recv.at[me],
            send_sem=bead_sem,
            recv_sem=tile_sem.at[me // per],
            device_id=where,
            device_id_type=MESH,
        ).start()

    def reply_cross():
        cross_peers(
            lambda where: pl.semaphore_signal(
                cross_sem, inc=1, device_id=where, device_id_type=MESH
            ),
            later=False,
        )

    with jax.named_scope("p_barrier"):
        @pl.when(jnp.logical_not(first))
        def _():
            pl.semaphore_wait(barrier, me + lower)
            loop(0, heads, send_beads)
            loop(
                heads, me,
                lambda o: pl.semaphore_signal(
                    ready_sem.at[me // per], inc=1, device_id=place(o), device_id_type=MESH
                ),
            )
            loop(heads, me, send_beads)
            reply_cross()

    fold = lax.broadcasted_iota(jnp.int32, (nz, hz), 0) - 2 * lax.broadcasted_iota(
        jnp.int32, (nz, hz), 1
    )
    fold = jnp.where((fold == 0) | (fold == 1), 0.125, 0.0).astype(jnp.bfloat16)
    spread = lax.broadcasted_iota(jnp.int32, (hz, nz), 1) - 2 * lax.broadcasted_iota(
        jnp.int32, (hz, nz), 0
    )
    spread = jnp.where((spread == 0) | (spread == 1), 1.0, 0.0).astype(jnp.bfloat16)

    def prepare(x):
        sums = []
        for q in range(19):
            total = None
            for i in range(2):
                for j in range(2):
                    piece = pops[q, pl.ds((2 * x + i) * ny + j, hy, stride=2), :]
                    total = piece if total is None else total + piece
            sums.append(total)
        restricted = times_exact(jnp.concatenate(sums, axis=0), fold)
        p = [restricted[i * hy : (i + 1) * hy] for i in range(19)]
        rho, m = moments(p)
        inv = 1.0 / rho
        pre = relax(p, rho, [v * inv for v in m], TO_COARSE, 1.0 - TO_COARSE)
        live = cmask[x] == 1
        pre = [jnp.where(live, pre[i], cpops[i, x]) for i in range(19)]
        rho, m = moments(pre)
        inv = 1.0 / rho
        u = [v * inv for v in m]
        down = relax(pre, rho, u, TO_FINE, 1.0 - TO_FINE)
        post = relax(pre, rho, u, 1.0 - 1.0 / TAU_COARSE, 1.0 / TAU_COARSE)
        for i in range(19):
            c = VELOCITIES[i]
            cstream[i, lax.rem(x + (c[0] + hx), hx)] = moved(post[i], c)
        wide = times_exact(jnp.concatenate(down, axis=0), spread)
        for q in range(19):
            value = wide[q * hy : (q + 1) * hy]
            tall[q, pl.ds(0, hy, stride=2), :] = value
            tall[q, pl.ds(1, hy, stride=2), :] = value
        for i in range(2):
            kept = fmask[2 * x + i] == 1
            at = plane_at(2 * x + i)
            for q in range(19):
                pops[q, at] = jnp.where(kept, pops[q, at], tall[q])

    with jax.named_scope("p_ends"):
        pltpu.make_async_copy(*part(0, 4), in_sem.at[2]).wait()
        for load in loads[4:7]:
            load.wait()
        pl.loop(0, 2)(lambda n: prepare(n * (hx - 1)))
        for s in SIGNS:
            x = nx - 1 if s > 0 else 0
            p = [pops[i, plane_at(x)] for i in range(19)]
            rho, m = moments(p)
            for n, value in enumerate([rho, *m, *[p[i] for i in FACE[0, s]]]):
                halo_send[slot_of(s), n] = value
            for t in SIGNS:
                y = ny - 1 if t > 0 else 0
                for n, value in enumerate([rho, *m, p[VELOCITIES.index((s, t, 0))]]):
                    brim_send[slot_of(s), slot_of(t), n : n + 1, :] = value[y : y + 1]

    BRIM, HALO, COARSE_X, COARSE_Y, COARSE_Z, COARSE_EDGE, ROWS, CORNERS, ENDS, COLUMNS = range(10)
    buffers = [
        (brim_send, brim_recv), (halo_send, halo_recv),
        (cxs, cxr), (cys, cyr), (czs, czr), (ces, cer),
        (fys, fyr), (fer, fer), (fxs, fxr), (fzs, fzr),
    ]

    def move(kind, src, dst, where):
        return pltpu.make_async_remote_copy(
            src_ref=src, dst_ref=dst, send_sem=send_sem.at[kind], recv_sem=recv_sem.at[kind],
            device_id=where, device_id_type=MESH,
        )

    def plan(kind, src, dst, offset):
        return move(kind, src, dst, device(offset))

    def send(kind, part, offset):
        src, dst = buffers[kind]
        plan(kind, src.at[part], dst.at[part], offset).start()

    def arrive(*kinds):
        for kind in kinds:
            dst = buffers[kind][1]
            pltpu.make_async_copy(dst, dst, recv_sem.at[kind]).wait()

    def leave(*kinds):
        for kind in kinds:
            src = buffers[kind][0]
            pltpu.make_async_copy(src, src, send_sem.at[kind]).wait()

    def send_ends(kind, later, signs=SIGNS):
        for s in signs:
            other = number(device((s, 0, 0)))
            mine = number((gx, gy, gz))

            @pl.when(other > mine if later else other < mine)
            def _():
                send(kind, slot_of(s), (s, 0, 0))

    @pl.when(jnp.logical_not(first))
    def _():
        send_ends(BRIM, later=False)
        send_ends(HALO, later=False)

    with jax.named_scope("p_middle"):
        for load in loads[7:]:
            load.wait()
        pl.loop(1, hx - 1)(prepare)

    def send_group(g):
        pl.semaphore_wait(ready_sem.at[g], jnp.minimum(per, (g + 1) * per - 1 - me))
        loop(jnp.maximum(me + 1, g * per), (g + 1) * per, send_beads)

    with jax.named_scope("p_barrier2"):
        @pl.when(first)
        def _():
            pl.semaphore_wait(barrier, owners - 1 + lower)
            loop(0, me, send_beads)
            loop(me + 1, owners, send_beads)
            reply_cross()
            send_ends(BRIM, later=False)
            send_ends(HALO, later=False)

        @pl.when(jnp.logical_not(first))
        def _():
            loop(lax.div(me + 1, per), tiles, send_group)

        send_ends(BRIM, later=True)

        @pl.when(lower < len(cross))
        def _():
            pl.semaphore_wait(cross_sem, len(cross) - lower)

    with jax.named_scope("p_csend"):
        pack_x(cstream, cxs, ces)
        for s in SIGNS:
            send(COARSE_X, slot_of(s), (s, 0, 0))
        pack_yz(cstream, cys, czs, ces)
        for s in SIGNS:
            send(COARSE_Y, slot_of(s), (0, s, 0))
            send(COARSE_Z, slot_of(s), (0, 0, s))
        for n, i in enumerate(EDGES):
            send(COARSE_EDGE, n, VELOCITIES[i])
        for n in range(2):
            fzs[n] = jnp.zeros((ny, LANES), f32)
        send_ends(HALO, later=True, signs=(1,))
        force[...] = jnp.zeros_like(force)
        halo_force[...] = jnp.zeros_like(halo_force)

    bins_y, bins_z = ny // 2, nz // BIN_Z
    bins_xy = (nx // 2) * bins_y
    near = jnp.where(sub < per, 0, 1)

    def gathered(t, side_of, mine):
        source = [
            [
                jnp.broadcast_to(bead_recv[t * per + j, side_of, pl.ds(n, 1), :], (FIELDS, LANES))
                for n in range(FIELDS // per)
            ]
            for j in range(per)
        ]
        both = []
        for rows in source:
            value = rows[0]
            for n in range(1, FIELDS // per):
                value = jnp.where(sub >= n * per, rows[n], value)
            both.append(value)
        where = (diagonal + (per - mine)) & (per - 1)
        tile = None
        for m in range(per):
            mixed = both[m % per]
            for f in range(1, per):
                mixed = jnp.where(turn == f, both[(f + m) % per], mixed)
            if m:
                mixed = pltpu.roll(mixed, slots * m, 1)
            tile = mixed if tile is None else jnp.where(where == m, mixed, tile)
        return tile

    row_i = lax.div(sub, 2).astype(f32)
    row_j = (sub & 1).astype(f32)
    depth = lax.broadcasted_iota(jnp.int32, (BIN_Z, LANES), 0).astype(f32)
    own_rows = lax.broadcasted_iota(jnp.int32, (bins_xy, LANES), 0).astype(f32)
    side_rows = lax.broadcasted_iota(jnp.int32, (bins_y, LANES), 0).astype(f32)
    bf16 = jnp.bfloat16

    def operands(t, side_of, first, spots, offset, count):
        mine = lax.rem(lax.rem(gx + (side_of + (ngx - 1)), ngx) * ngy + gy, per)
        tile = gathered(t, side_of, mine)
        number = tile[6:7]
        column = jnp.floor((number + 0.5) * (1.0 / bins_z))
        layer = number - column * bins_z
        dx, dy = first - tile[0:1], row_j - tile[1:2]
        weight = jnp.exp(-0.5 * (dx * dx + dy * dy))
        mask = spots + offset == column
        highs, lows = [], []
        for d in range(3):
            pushed = weight * tile[3 + d : 4 + d]
            high = pushed.astype(bf16).astype(f32)
            low = pushed - high
            for n in range(count):
                highs.append(jnp.where(mask, high[n : n + 1], 0.0))
                lows.append(jnp.where(mask, low[n : n + 1], 0.0))
        lh = jnp.concatenate(highs, axis=0).astype(bf16)
        ll = jnp.concatenate(lows, axis=0).astype(bf16)
        dz = depth - tile[2:3]
        fall = jnp.exp(-0.5 * (dz * dz))
        fh = fall.astype(bf16).astype(f32)
        fl = fall - fh
        rh = jnp.concatenate([jnp.where(layer == n, fh, 0.0) for n in range(bins_z)], axis=0)
        rl = jnp.concatenate([jnp.where(layer == n, fl, 0.0) for n in range(bins_z)], axis=0)
        rh, rl = rh.astype(bf16), rl.astype(bf16)
        return [lh, lh, ll], [rh, rl, rh]

    def product(ts, *rest):
        pairs = [operands(t, *rest) for t in ts]
        return lax.dot_general(
            jnp.concatenate([v for left, _ in pairs for v in left], axis=1),
            jnp.concatenate([v for _, right in pairs for v in right], axis=1),
            (((1,), (1,)), ((), ())),
            preferred_element_type=f32,
        )

    far = lax.div(2 * gx, ngx)

    with jax.named_scope("p_force"):
        span = 2 if tiles % 2 == 0 else 1

        @pl.loop(0, tiles // span)
        def _(step):
            ts = []
            for k in range(span):
                n = step * span + k
                near = (1 - lax.div(n + 2, tiles)) * (n + 1) + lax.div(n + 1, tiles) * (tiles - 1)
                t = near + far * (tiles - 1 - n - near)
                arrived = bead_recv.at[pl.ds(t * per, per)]
                pltpu.make_async_copy(arrived, arrived, tile_sem.at[t]).wait()
                ts.append(t)
            value = product(ts, 1, row_i, own_rows, 0.0, 4)
            for d in range(3):
                for i in range(2):
                    for j in range(2):
                        for b in range(nx // 2):
                            start = ((d * 2 + i) * 2 + j) * bins_xy + b * bins_y
                            at = pl.ds((2 * b + i) * ny + j, bins_y, stride=2)
                            force[d, at, :] += value[start : start + bins_y]

            for h in range(2):
                first = float(1 - h)
                value = product(ts, 2 * h, first, side_rows, first * (bins_xy - bins_y), 2)
                for d in range(3):
                    for j in range(2):
                        start = (d * 2 + j) * bins_y
                        at = pl.ds(j, bins_y, stride=2)
                        halo_force[h, d, at, :] += value[start : start + bins_y]

    send_ends(HALO, later=True, signs=(-1,))

    wide_lane = lax.broadcasted_iota(jnp.int32, (ny, LANES), 1)

    def collided(p, rho, m, f):
        inv = 1.0 / rho
        u = [(v + 0.5 * w) * inv for v, w in zip(m, f)]
        return relax(
            p, rho, u, 1.0 - 1.0 / TAU_FINE, 1.0 / TAU_FINE, f, 1.0 - 0.5 / TAU_FINE
        )

    def made_of(rho, m, f):
        inv = 1.0 / rho
        u = [(v + 0.5 * w) * inv for v, w in zip(m, f)]
        return setup(rho, u, 1.0 / TAU_FINE, f, 1.0 - 0.5 / TAU_FINE)

    keep = 1.0 - 1.0 / TAU_FINE

    def rows(n):
        sign = (1 - 2 * n).astype(f32)
        y = (ny - 1) * (1 - n)
        p = [pops[i, rows_at(y), :] for i in range(19)]
        made = made_of(*moments(p), [force[d, rows_at(y), :] for d in range(3)])
        for j, i in enumerate(FACE[1, 1]):
            c = VELOCITIES[i]
            other = FACE[1, -1][j]
            even, odd = halves(i, made)
            block = keep * jnp.where(n == 0, p[i], p[other]) + (even + sign * odd)
            if c[2]:
                block = pltpu.roll(block, (1 if c[2] > 0 else nz - 1) + n * (c[2] * (nz - 2)), 1)
            if c[0]:
                block = pltpu.roll(block, (1 if c[0] > 0 else nx - 1) + n * (c[0] * (nx - 2)), 0)
            fys[n, j] = block
        where = (gx, lax.rem(gy + (1 - 2 * n) + ngy, ngy), gz)
        move(ROWS, fys.at[n], fyr.at[n], where).start()

    with jax.named_scope("p_rows"):
        pl.loop(0, 2)(rows)
        for n, i in enumerate(EDGES_YZ):
            s = VELOCITIES[i][1]
            block = fys.at[slot_of(s), FACE[1, s].index(i)]
            plan(CORNERS, block, fer.at[n], VELOCITIES[i]).start()

    def end_rows(n):
        sign = (1 - 2 * n).astype(f32)
        y = (ny - 1) * (1 - n)
        for h in range(2):
            made = made_of(
                brim_recv[h, n, 0:1, :],
                [brim_recv[h, n, 1 + d : 2 + d, :] for d in range(3)],
                [halo_force[h, d, pl.ds(y, 1), :] for d in range(3)],
            )
            both = [halves(VELOCITIES.index((s, 1, 0)), made) for s in SIGNS]
            straight = n == h
            even = jnp.where(straight, both[0][0], both[1][0])
            odd = jnp.where(straight, both[0][1], both[1][1])
            fxs[n, h : h + 1, :] = keep * brim_recv[h, n, 4:5, :] + (even + sign * odd)

    with jax.named_scope("p_hwait"):
        arrive(BRIM)

    with jax.named_scope("p_endrows"):
        pl.loop(0, 2)(end_rows)
        for s in SIGNS:
            send(ENDS, slot_of(s), (0, s, 0))

    def collide(p, rho, m, f, x):
        post = collided(p, rho, m, f)
        columns = [fzs[n] for n in range(2)]
        for i in range(19):
            c = VELOCITIES[i]
            if post[i] is None:
                continue
            at = x + c[0] if isinstance(x, int) else lax.rem(x + (c[0] + nx), nx)
            plane = moved(post[i], (0, c[1], 0))
            stream[i, plane_at(at)] = moved(plane, (0, 0, c[2]))
            if c[2]:
                n = slot_of(c[2])
                k = FACE[2, c[2]].index(i) * nx + at
                turned = pltpu.roll(plane, lax.rem(k + (1 - n), LANES), 1)
                columns[n] = jnp.where(wide_lane == k, turned, columns[n])
        for n in range(2):
            fzs[n] = columns[n]

    def collide_own(x):
        p = [pops[i, plane_at(x)] for i in range(19)]
        rho, m = moments(p)
        collide(p, rho, m, [force[d, plane_at(x)] for d in range(3)], x)

    with jax.named_scope("p_collide"):
        pl.loop(0, nx)(collide_own)

    with jax.named_scope("p_hwait2"):
        arrive(HALO)

    with jax.named_scope("p_hcollide"):
        for s in SIGNS:
            n = slot_of(s)
            p = [None] * 19
            for j, i in enumerate(FACE[0, s]):
                p[i] = halo_recv[n, 4 + j]
            collide(
                p, halo_recv[n, 0], [halo_recv[n, 1 + d] for d in range(3)],
                [halo_force[n, d] for d in range(3)], -1 if s > 0 else nx,
            )

    with jax.named_scope("p_sendz"):
        for s in SIGNS:
            send(COLUMNS, slot_of(s), (0, 0, s))

    with jax.named_scope("p_coarse"):
        arrive(COARSE_X, COARSE_Y, COARSE_Z, COARSE_EDGE)
        fill_coarse(cstream, cxr, cyr, czr, cer)

    with jax.named_scope("p_ywait"):
        arrive(ROWS, CORNERS, ENDS)

    with jax.named_scope("p_yfill"):
        corner = lax.broadcasted_iota(jnp.int32, (nx, nz), 1)
        row_x = lax.broadcasted_iota(jnp.int32, (nx, nz), 0)
        for s in SIGNS:
            for j, i in enumerate(FACE[1, s]):
                c = VELOCITIES[i]
                block = fyr[slot_of(s), j]
                if c[2]:
                    block = jnp.where(corner == side(c[2], nz), fer[EDGES_YZ.index(i)], block)
                if c[0]:
                    h = slot_of(c[0])
                    end = fxr[slot_of(s), h : h + 1, :]
                    block = jnp.where(row_x == side(c[0], nx), end, block)
                stream[i, rows_at(side(s, ny)), :] = block

    with jax.named_scope("p_zwait"):
        arrive(COLUMNS)

    with jax.named_scope("p_final"):
        sent = bead_recv.at[pl.ds(0, owners - 1)]
        pltpu.make_async_copy(sent, sent, bead_sem).wait()
        leave(*range(10))


def local(populations, coarse_pops, fine_mask, coarse_mask, bead_data, bead_bins):
    _, nx, ny, nz = populations.shape
    _, hx, hy, hz = coarse_pops.shape
    sizes = tuple(lax.axis_size(axis) for axis in ("gx", "gy", "gz"))
    owners = sizes[0] * sizes[1]
    total = bead_data.shape[4]
    chunks = total // LANES
    slots = total // owners
    per = LANES // slots
    rows = FIELDS // per
    beads = bead_data.reshape(6 * chunks, LANES)
    bins = bead_bins.reshape(chunks, LANES)
    f32, i32 = jnp.float32, jnp.int32
    any_spec = pl.BlockSpec(memory_space=pl.ANY)
    hbm_spec = pl.BlockSpec(memory_space=pltpu.HBM)
    vmem_spec = pl.BlockSpec(memory_space=pltpu.VMEM)
    dma = pltpu.SemaphoreType.DMA

    fine_rim = [(2, 5, nx, nz), (2, ny, LANES), (len(EDGES_YZ), nx, nz)]
    coarse_rim = [(2, 5, hy, hz), (2, 5 * hx, 1, hz), (2, hy, LANES), (12, 1, LANES)]
    shapes = [(19, nx * ny, nz), (2, ny, LANES), coarse_pops.shape]
    vmem = [
        (3, nx * ny, nz), (2, 3, ny, nz),
        (2, 9, ny, nz), (2, 9, ny, nz), (2, 2, 8, nz), (2, 2, 8, nz),
        (FIELDS, LANES), (sizes[1], sizes[0] + 2, rows, LANES), (owners, 3, rows, LANES),
        *fine_rim[:2], (2, 2, nz), (2, 2, nz), *coarse_rim, fine_rim[0], fine_rim[2], *coarse_rim,
    ]
    operands = (
        populations.reshape(19, nx * ny, nz), coarse_pops, fine_mask, coarse_mask, beads, bins
    )
    fine, columns, coarse = pl.pallas_call(
        functools.partial(kernel, sizes, slots),
        out_shape=[jax.ShapeDtypeStruct(shape, f32) for shape in shapes],
        in_specs=[hbm_spec] * 6,
        out_specs=[vmem_spec, any_spec, vmem_spec],
        scratch_shapes=[
            pltpu.VMEM((19, nx * ny, nz), f32),
            pltpu.VMEM((19, hx, hy, hz), f32),
            pltpu.VMEM((nx, ny, nz), i32),
            pltpu.VMEM((hx, hy, hz), i32),
            pltpu.VMEM((6 * chunks, LANES), f32),
            pltpu.VMEM((chunks, LANES), i32),
            pltpu.VMEM((19, ny, nz), f32),
            *[pltpu.VMEM(shape, f32) for shape in vmem],
            dma((7,)),
            dma,
            dma((owners // per,)),
            pltpu.SemaphoreType.REGULAR((owners // per,)),
            pltpu.SemaphoreType.REGULAR,
            dma((10,)),
            dma((10,)),
        ],
        compiler_params=pltpu.CompilerParams(
            collective_id=0, has_side_effects=True, vmem_limit_bytes=LIMIT
        ),
    )(*[pltpu.with_memory_space_constraint(v, pltpu.HBM) for v in operands])
    fine, coarse = pl.pallas_call(
        functools.partial(finish, nx),
        out_shape=[jax.ShapeDtypeStruct(shape, f32) for shape in (shapes[0], shapes[2])],
        in_specs=[vmem_spec] * 3,
        out_specs=[any_spec] * 2,
        scratch_shapes=[pltpu.VMEM((10, nx * ny, nz), f32), dma((8,))],
        compiler_params=pltpu.CompilerParams(vmem_limit_bytes=LIMIT),
    )(fine, columns, coarse)
    return fine.reshape(populations.shape), coarse


def solution(mesh):
    in_specs = (
        P(None, "gx", "gy", "gz"),
        P(None, "gx", "gy", "gz"),
        P("gx", "gy", "gz"),
        P("gx", "gy", "gz"),
        P("gx", "gy", "gz", None, None),
        P("gx", "gy", "gz", None, None),
    )
    out_specs = (P(None, "gx", "gy", "gz"), P(None, "gx", "gy", "gz"))
    return jax.shard_map(local, mesh=mesh, in_specs=in_specs, out_specs=out_specs, check_vma=False)
```

```python
import functools

import jax
import jax.numpy as jnp
from jax import lax
from jax.experimental import pallas as pl
from jax.experimental.pallas import tpu as pltpu
from jax.sharding import PartitionSpec as P

BIN_Z = 32
VELOCITIES = [
    (0, 0, 0), (1, 0, 0), (-1, 0, 0), (0, 1, 0), (0, -1, 0), (0, 0, 1), (0, 0, -1),
    (1, 1, 0), (-1, -1, 0), (1, -1, 0), (-1, 1, 0), (1, 0, 1), (-1, 0, -1), (1, 0, -1),
    (-1, 0, 1), (0, 1, 1), (0, -1, -1), (0, 1, -1), (0, -1, 1),
]
WEIGHTS = [1.0 / 3.0] + [1.0 / 18.0] * 6 + [1.0 / 36.0] * 12
TAU_FINE = 1.2
TAU_COARSE = 0.85
TO_COARSE = 2.0 * TAU_COARSE / TAU_FINE
TO_FINE = TAU_FINE / (2.0 * TAU_COARSE)
LANES = 128
FIELDS = 8
LIMIT = 24 * 2**20
MESH = pl.DeviceIdType.MESH
SIGNS = (1, -1)
FACE = {(a, s): [i for i in range(19) if VELOCITIES[i][a] == s] for a in range(3) for s in SIGNS}
EDGES = [i for i in range(7, 19)]


def corner_messages(ngz):
    return (1,) if ngz == 2 else SIGNS


def along(vector, c):
    total = None
    for part, sign in zip(vector, c):
        if sign:
            total = part if total is None else (total + part if sign > 0 else total - part)
    return total


def moments(p):
    rho = p[0]
    sums = [None] * 19
    m = [None] * 3
    for i in range(1, 19, 2):
        rho = rho + (p[i] + p[i + 1])
        sums[i] = p[i] - p[i + 1]
        for axis, sign in enumerate(VELOCITIES[i]):
            if sign:
                if m[axis] is None:
                    m[axis] = sums[i]
                else:
                    m[axis] = m[axis] + sums[i] if sign > 0 else m[axis] - sums[i]
    return rho, m


def setup(rho, u, b, force=None, k=0.0):
    scaled = b * rho
    base = scaled * (1.0 - 1.5 * (u[0] * u[0] + u[1] * u[1] + u[2] * u[2]))
    lin = [3.0 * scaled * v for v in u]
    quad = [4.5 * scaled * v for v in u]
    if force is not None:
        base = base - (3.0 * k) * (u[0] * force[0] + u[1] * force[1] + u[2] * force[2])
        lin = [v + (3.0 * k) * f for v, f in zip(lin, force)]
        quad = [v + (9.0 * k) * f for v, f in zip(quad, force)]
    return u, base, lin, quad


def halves(i, made):
    u, base, lin, quad = made
    first = i if i % 2 else i - 1
    c, w = VELOCITIES[first], WEIGHTS[first]
    odd = w * along(lin, c)
    return w * (base + along(u, c) * along(quad, c)), odd if i % 2 else -odd


def relax(p, rho, u, a, b, force=None, k=0.0):
    made = setup(rho, u, b, force, k)
    out = [None] * 19
    if p[0] is not None:
        out[0] = a * p[0] + WEIGHTS[0] * made[1]
    for i in range(1, 19, 2):
        if p[i] is None and p[i + 1] is None:
            continue
        even, odd = halves(i, made)
        if p[i] is not None:
            out[i] = a * p[i] + (even + odd)
        if p[i + 1] is not None:
            out[i + 1] = a * p[i + 1] + (even - odd)
    return out


def parts(x):
    high = x.astype(jnp.bfloat16)
    return high, (x - high.astype(jnp.float32)).astype(jnp.bfloat16)


def times_exact(x, table):
    high, low = parts(x)
    dot = functools.partial(jnp.dot, preferred_element_type=jnp.float32)
    return dot(high, table) + dot(low, table)


def moved(plane, c):
    rows, lanes = plane.shape
    if c[1]:
        plane = pltpu.roll(plane, 1 if c[1] > 0 else rows - 1, 0)
    if c[2]:
        plane = pltpu.roll(plane, 1 if c[2] > 0 else lanes - 1, 1)
    return plane


def side(sign, length):
    return 0 if sign > 0 else length - 1


def slot_of(sign):
    return 0 if sign > 0 else 1


def pack_x(target, xs, es):
    _, fx, fy, fz = target.shape
    row = lax.broadcasted_iota(jnp.int32, (fy, LANES), 0)
    diagonal = row == lax.broadcasted_iota(jnp.int32, (fy, LANES), 1)
    for s in SIGNS:
        for j, i in enumerate(FACE[0, s]):
            plane = target[i, side(s, fx)]
            xs[slot_of(s), j] = plane
            c = VELOCITIES[i]
            if c[1]:
                y = side(c[1], fy)
                es[EDGES.index(i), :, 0:fz] = plane[y : y + 1]
            elif c[2]:
                z = side(c[2], fz)
                turned = jnp.where(diagonal, plane[:, z : z + 1], 0.0)
                es[EDGES.index(i)] = jnp.sum(turned, axis=0, keepdims=True)


def pack_yz(target, ys, zs, es):
    _, fx, fy, fz = target.shape
    lane = lax.broadcasted_iota(jnp.int32, (fy, LANES), 1)
    for s in SIGNS:
        y, z = side(s, fy), side(s, fz)
        for j, i in enumerate(FACE[1, s]):
            for x in range(fx):
                ys[slot_of(s), j * fx + x] = target[i, x, y : y + 1, :]
        packed = jnp.zeros((fy, LANES), jnp.float32)
        for j, i in enumerate(FACE[2, s]):
            for x in range(fx):
                packed = jnp.where(lane == j * fx + x, target[i, x, :, z : z + 1], packed)
        zs[slot_of(s)] = packed
        for i in FACE[2, s]:
            c = VELOCITIES[i]
            if c[1]:
                y = side(c[1], fy)
                es[EDGES.index(i)] = packed[y : y + 1]


def fill_coarse(target, xr, yr, zr, er):
    _, fx, fy, fz = target.shape
    lane = lax.broadcasted_iota(jnp.int32, (fy, LANES), 1)
    row = lax.broadcasted_iota(jnp.int32, (fy, LANES), 0)
    last = lax.broadcasted_iota(jnp.int32, (fy, fz), 1)
    columns = []
    for s in SIGNS:
        column = zr[slot_of(s)]
        for j, i in enumerate(FACE[2, s]):
            c = VELOCITIES[i]
            if c[0]:
                value = jnp.sum(
                    jnp.where(row == lane, er[EDGES.index(i)], 0.0), axis=1, keepdims=True
                )
                column = jnp.where(lane == j * fx + side(c[0], fx), value, column)
            elif c[1]:
                spot = (lane >= j * fx) & (lane < (j + 1) * fx) & (row == side(c[1], fy))
                column = jnp.where(spot, er[EDGES.index(i)], column)
        columns.append(column)
    for i in range(1, 19):
        c = VELOCITIES[i]
        if c[0]:
            target[i, side(c[0], fx)] = xr[slot_of(c[0]), FACE[0, c[0]].index(i)]
        if c[1]:
            y, j = side(c[1], fy), FACE[1, c[1]].index(i)
            for x in range(fx):
                if c[0] and x == side(c[0], fx):
                    piece = er[EDGES.index(i), :, 0:fz]
                else:
                    piece = yr[slot_of(c[1]), j * fx + x]
                target[i, x, y : y + 1, :] = piece
        if c[2]:
            j, column = FACE[2, c[2]].index(i), columns[slot_of(c[2])]
            for x in range(fx):
                k = j * fx + x
                target[i, x] = jnp.where(
                    last == side(c[2], fz), column[:, k : k + 1], target[i, x]
                )


def finish(nx, fine, columns, coarse, fine_out, coarse_out, target, store_sem):
    _, height, nz = fine.shape
    ny = height // nx
    turned = [5, 6, *range(11, 19)]
    def store(src, dst, n):
        return pltpu.make_async_copy(src, dst, store_sem.at[n])

    for low, high in ((0, 5), (7, 11)):
        store(fine.at[low:high], fine_out.at[low:high], 0).start()
    store(coarse, coarse_out, 1).start()
    last = lax.broadcasted_iota(jnp.int32, (ny, nz), 1)
    row = lax.broadcasted_iota(jnp.int32, (ny, nz), 0)
    for n, i in enumerate(turned):
        c = VELOCITIES[i]
        column = columns[slot_of(c[2])]
        spot = last == side(c[2], nz)
        if c[1]:
            spot = spot & (row != side(c[1], ny))
        for x in range(nx):
            k = FACE[2, c[2]].index(i) * nx + x
            target[n, x * ny : (x + 1) * ny, :] = jnp.where(
                spot, column[:, k : k + 1], fine[i, x * ny : (x + 1) * ny, :]
            )
        if n % 2:
            store(target.at[n - 1 : n + 1], fine_out.at[i - 1 : i + 1], 2).start()
    store(fine.at[0:9], fine_out.at[0:9], 0).wait()
    store(coarse, coarse_out, 1).wait()
    store(target, fine_out.at[0:10], 2).wait()


def repeat(count, act, most=8):
    if count > most:
        pl.loop(0, count)(act)
    else:
        for n in range(count):
            act(n)


def kernel(
    sizes, slots, pop_in, cpop_in, fmask_in, cmask_in, bead_in, bins_in,
    stream, fzr, cstream,
    pops, cpops, fmask, cmask, bead_ref, bins_ref, tall,
    force, halo_force, halo_send, halo_recv, brim_send, brim_recv,
    bead_rows, bead_send, bead_recv, fys, fzs, cxs, cys, czs, ces,
    fyr, cxr, cyr, czr, cer,
    own_sem, bead_sem, tile_sem, ready_sem, cross_sem, recv_sem,
):
    ngx, ngy, ngz = sizes
    gx, gy, gz = lax.axis_index("gx"), lax.axis_index("gy"), lax.axis_index("gz")
    owners = ngx * ngy
    me = gx * ngy + gy
    nx, ny, nz = fmask.shape
    _, hx, hy, hz = cpops.shape
    chunks = bins_ref.shape[0]
    per = LANES // slots
    tiles = owners // per
    f32 = jnp.float32

    barrier = pltpu.get_barrier_semaphore()
    heads = ngy
    first = me < heads

    def loop(start, stop, act):
        lax.fori_loop(start, stop, lambda n, carry: (act(n), carry)[1], 0)

    def place(o):
        return lax.div(o, ngy), lax.rem(o, ngy), gz

    def greet(o):
        pl.semaphore_signal(barrier, inc=1, device_id=place(o), device_id_type=MESH)

    loop(0, jnp.minimum(me, heads), greet)

    def part(x, w):
        return pop_in.at[:, pl.ds(x * ny, w * ny)], pops.at[:, pl.ds(x * ny, w * ny)]

    loads = [
        pltpu.make_async_copy(src, dst, own_sem.at[n])
        for n, src, dst in (
            (0, bead_in, bead_ref), (1, bins_in, bins_ref), (2, *part(0, 2)), (2, *part(nx - 2, 2)),
            (3, cmask_in, cmask), (4, fmask_in, fmask), (5, cpop_in, cpops),
            (6, *part(2, nx - 4)),
        )
    ]
    for load in loads:
        load.start()

    def plane_at(x):
        return pl.ds(x * ny, ny)

    def rows_at(y):
        return pl.ds(y, nx, stride=ny)

    def device(offset):
        return (
            lax.rem(gx + (offset[0] + ngx), ngx),
            lax.rem(gy + (offset[1] + ngy), ngy),
            lax.rem(gz + (offset[2] + ngz), ngz),
        )

    def number(where):
        return (where[0] * ngy + where[1]) * ngz + where[2]

    def cross_peers(act, later):
        mine = number((gx, gy, gz))
        for offset in cross:
            where = device(offset)
            other = number(where)

            @pl.when(other > mine if later else other < mine)
            def _():
                act(where)

    cross = [(0, 0, 1), (0, 0, -1)] + [VELOCITIES[i] for i in EDGES if VELOCITIES[i][2]]
    lower = jnp.int32(0)
    for offset in cross:
        lower = lower + (number(device(offset)) < number((gx, gy, gz))).astype(jnp.int32)

    with jax.named_scope("p_signals"):
        loop(0, owners - jnp.maximum(heads, me + 1), lambda n: greet(owners - 1 - n))

        @pl.when(first)
        def _():
            loop(me + 1, heads, greet)

        cross_peers(
            lambda where: pl.semaphore_signal(
                barrier, inc=1, device_id=where, device_id_type=MESH
            ),
            later=True,
        )

    lane = lax.broadcasted_iota(jnp.int32, (FIELDS, LANES), 1)
    sub = lax.broadcasted_iota(jnp.int32, (FIELDS, LANES), 0)
    diagonal = (lax.div(lane, slots) + (FIELDS - sub)) & (per - 1)
    turn = sub & (per - 1)

    def put_block(o, block):
        a, b = o // ngy, lax.rem(o, ngy)
        bead_send[b, a + 1] = block

    def pack_chunk(chunk):
        bead_rows[0:6, :] = bead_ref[pl.ds(chunk, 6, stride=chunks), :]
        bead_rows[6:7, :] = bins_ref[pl.ds(chunk, 1), :].astype(f32)
        rows = bead_rows[...]
        turned = rows
        for m in range(1, per):
            turned = jnp.where(turn == m, pltpu.roll(rows, slots * m, 1), turned)
        for k in range(per):
            kept = jnp.where(diagonal == k, turned, 0.0)
            shift = 1
            while shift < per:
                kept = kept + pltpu.roll(kept, FIELDS - shift, 0)
                shift *= 2
            block = [kept[n : n + 1] for n in range(0, FIELDS, per)]
            o = chunk * per + k
            a, b = (o // ngy, o % ngy) if isinstance(o, int) else (lax.div(o, ngy), lax.rem(o, ngy))
            for n, part in enumerate(block):
                bead_send[b, a + 1, pl.ds(n, 1), :] = part

    with jax.named_scope("p_pack"):
        for load in loads[:2]:
            load.wait()
        bead_rows[7:8, :] = jnp.zeros((1, LANES), f32)
        repeat(chunks, pack_chunk)
        for b in range(ngy):
            bead_send[b, 0] = bead_send[b, ngx]
            bead_send[b, ngx + 1] = bead_send[b, 1]
        own_beads = pltpu.make_async_copy(
            bead_send.at[gy, pl.ds(gx, 3)], bead_recv.at[me], tile_sem.at[me // per]
        )
        own_beads.start()

    def send_beads(o):
        where = place(o)
        pltpu.make_async_remote_copy(
            src_ref=bead_send.at[where[1], pl.ds(where[0], 3)],
            dst_ref=bead_recv.at[me],
            send_sem=bead_sem,
            recv_sem=tile_sem.at[me // per],
            device_id=where,
            device_id_type=MESH,
        ).start()

    def reply_cross():
        cross_peers(
            lambda where: pl.semaphore_signal(
                cross_sem, inc=1, device_id=where, device_id_type=MESH
            ),
            later=False,
        )

    with jax.named_scope("p_barrier"):
        @pl.when(jnp.logical_not(first))
        def _():
            pl.semaphore_wait(barrier, me + lower)
            loop(0, heads, send_beads)
            loop(
                heads, me,
                lambda o: pl.semaphore_signal(
                    ready_sem.at[me // per], inc=1, device_id=place(o), device_id_type=MESH
                ),
            )
            loop(heads, me, send_beads)
            reply_cross()

    fold = lax.broadcasted_iota(jnp.int32, (nz, hz), 0) - 2 * lax.broadcasted_iota(
        jnp.int32, (nz, hz), 1
    )
    fold = jnp.where((fold == 0) | (fold == 1), 0.125, 0.0).astype(jnp.bfloat16)
    spread = lax.broadcasted_iota(jnp.int32, (hz, nz), 1) - 2 * lax.broadcasted_iota(
        jnp.int32, (hz, nz), 0
    )
    spread = jnp.where((spread == 0) | (spread == 1), 1.0, 0.0).astype(jnp.bfloat16)

    def prepare(x):
        sums = []
        for q in range(19):
            total = None
            for i in range(2):
                for j in range(2):
                    piece = pops[q, pl.ds((2 * x + i) * ny + j, hy, stride=2), :]
                    total = piece if total is None else total + piece
            sums.append(total)
        restricted = times_exact(jnp.concatenate(sums, axis=0), fold)
        p = [restricted[i * hy : (i + 1) * hy] for i in range(19)]
        rho, m = moments(p)
        inv = 1.0 / rho
        pre = relax(p, rho, [v * inv for v in m], TO_COARSE, 1.0 - TO_COARSE)
        live = cmask[x] == 1
        pre = [jnp.where(live, pre[i], cpops[i, x]) for i in range(19)]
        rho, m = moments(pre)
        inv = 1.0 / rho
        u = [v * inv for v in m]
        down = relax(pre, rho, u, TO_FINE, 1.0 - TO_FINE)
        post = relax(pre, rho, u, 1.0 - 1.0 / TAU_COARSE, 1.0 / TAU_COARSE)
        for i in range(19):
            c = VELOCITIES[i]
            cstream[i, lax.rem(x + (c[0] + hx), hx)] = moved(post[i], c)
        wide = times_exact(jnp.concatenate(down, axis=0), spread)
        for q in range(19):
            value = wide[q * hy : (q + 1) * hy]
            tall[q, pl.ds(0, hy, stride=2), :] = value
            tall[q, pl.ds(1, hy, stride=2), :] = value
        for i in range(2):
            kept = fmask[2 * x + i] == 1
            at = plane_at(2 * x + i)
            for q in range(19):
                pops[q, at] = jnp.where(kept, pops[q, at], tall[q])

    with jax.named_scope("p_ends"):
        pltpu.make_async_copy(*part(0, 4), own_sem.at[2]).wait()
        for load in loads[4:7]:
            load.wait()
        pl.loop(0, 2)(lambda n: prepare(n * (hx - 1)))
        for s in SIGNS:
            x = nx - 1 if s > 0 else 0
            p = [pops[i, plane_at(x)] for i in range(19)]
            rho, m = moments(p)
            for n, value in enumerate([rho, *m, *[p[i] for i in FACE[0, s]]]):
                halo_send[slot_of(s), n] = value
            for t in SIGNS:
                y = ny - 1 if t > 0 else 0
                for n, value in enumerate([rho, *m, p[VELOCITIES.index((s, t, 0))]]):
                    brim_send[slot_of(s), slot_of(t), n : n + 1, :] = value[y : y + 1]

    BRIM, HALO, COARSE_X, COARSE_Y, COARSE_Z, COARSE_EDGE, CROSS_Y, COLUMNS = range(8)
    buffers = [
        (brim_send, brim_recv), (halo_send, halo_recv),
        (cxs, cxr), (cys, cyr), (czs, czr), (ces, cer),
        (fys, fyr), (fzs, fzr),
    ]

    def move(kind, src, dst, where):
        return pltpu.make_async_remote_copy(
            src_ref=src, dst_ref=dst, send_sem=own_sem.at[kind], recv_sem=recv_sem.at[kind],
            device_id=where, device_id_type=MESH,
        )

    def plan(kind, src, dst, offset):
        return move(kind, src, dst, device(offset))

    def send(kind, part, offset):
        src, dst = buffers[kind]
        plan(kind, src.at[part], dst.at[part], offset).start()

    def arrive(*kinds):
        for kind in kinds:
            dst = buffers[kind][1]
            pltpu.make_async_copy(dst, dst, recv_sem.at[kind]).wait()

    def leave(*kinds):
        for kind in kinds:
            src = buffers[kind][0]
            pltpu.make_async_copy(src, src, own_sem.at[kind]).wait()

    def send_ends(kind, later, signs=SIGNS):
        for s in signs:
            other = number(device((s, 0, 0)))
            mine = number((gx, gy, gz))

            @pl.when(other > mine if later else other < mine)
            def _():
                send(kind, slot_of(s), (s, 0, 0))

    @pl.when(jnp.logical_not(first))
    def _():
        send_ends(BRIM, later=False)
        send_ends(HALO, later=False)

    with jax.named_scope("p_middle"):
        for load in loads[7:]:
            load.wait()
        pl.loop(1, hx - 1)(prepare)

    def send_group(g):
        pl.semaphore_wait(ready_sem.at[g], jnp.minimum(per, (g + 1) * per - 1 - me))
        loop(jnp.maximum(me + 1, g * per), (g + 1) * per, send_beads)

    with jax.named_scope("p_barrier2"):
        @pl.when(first)
        def _():
            pl.semaphore_wait(barrier, owners - 1 + lower)
            loop(0, me, send_beads)
            loop(me + 1, owners, send_beads)
            reply_cross()
            send_ends(BRIM, later=False)
            send_ends(HALO, later=False)

        @pl.when(jnp.logical_not(first))
        def _():
            loop(lax.div(me + 1, per), tiles, send_group)

        send_ends(BRIM, later=True)

        @pl.when(lower < len(cross))
        def _():
            pl.semaphore_wait(cross_sem, len(cross) - lower)

    with jax.named_scope("p_csend"):
        pack_x(cstream, cxs, ces)
        for s in SIGNS:
            send(COARSE_X, slot_of(s), (s, 0, 0))
        pack_yz(cstream, cys, czs, ces)
        for s in SIGNS:
            send(COARSE_Y, slot_of(s), (0, s, 0))
            send(COARSE_Z, slot_of(s), (0, 0, s))
        for n, i in enumerate(EDGES):
            send(COARSE_EDGE, n, VELOCITIES[i])
        for n in range(2):
            fzs[n] = jnp.zeros((ny, LANES), f32)
        send_ends(HALO, later=True, signs=(1,))
        force[...] = jnp.zeros_like(force)
        halo_force[...] = jnp.zeros_like(halo_force)

    bins_y, bins_z = ny // 2, nz // BIN_Z
    bins_xy = (nx // 2) * bins_y
    near = jnp.where(sub < per, 0, 1)

    def gathered(t, side_of, mine):
        source = [
            [
                jnp.broadcast_to(bead_recv[t * per + j, side_of, pl.ds(n, 1), :], (FIELDS, LANES))
                for n in range(FIELDS // per)
            ]
            for j in range(per)
        ]
        both = []
        for rows in source:
            value = rows[0]
            for n in range(1, FIELDS // per):
                value = jnp.where(sub >= n * per, rows[n], value)
            both.append(value)
        where = (diagonal + (per - mine)) & (per - 1)
        tile = None
        for m in range(per):
            mixed = both[m % per]
            for f in range(1, per):
                mixed = jnp.where(turn == f, both[(f + m) % per], mixed)
            if m:
                mixed = pltpu.roll(mixed, slots * m, 1)
            tile = mixed if tile is None else jnp.where(where == m, mixed, tile)
        return tile

    row_i = lax.div(sub, 2).astype(f32)
    row_j = (sub & 1).astype(f32)
    depth = lax.broadcasted_iota(jnp.int32, (BIN_Z, LANES), 0).astype(f32)
    own_rows = lax.broadcasted_iota(jnp.int32, (bins_xy, LANES), 0).astype(f32)
    side_rows = lax.broadcasted_iota(jnp.int32, (bins_y, LANES), 0).astype(f32)
    bf16 = jnp.bfloat16

    def operands(t, side_of, first, spots, offset, count):
        mine = lax.rem(lax.rem(gx + (side_of + (ngx - 1)), ngx) * ngy + gy, per)
        tile = gathered(t, side_of, mine)
        number = tile[6:7]
        column = jnp.floor((number + 0.5) * (1.0 / bins_z))
        layer = number - column * bins_z
        dx, dy = first - tile[0:1], row_j - tile[1:2]
        weight = jnp.exp(-0.5 * (dx * dx + dy * dy))
        mask = spots + offset == column
        highs, lows = [], []
        for d in range(3):
            pushed = weight * tile[3 + d : 4 + d]
            high = pushed.astype(bf16).astype(f32)
            low = pushed - high
            for n in range(count):
                highs.append(jnp.where(mask, high[n : n + 1], 0.0))
                lows.append(jnp.where(mask, low[n : n + 1], 0.0))
        lh = jnp.concatenate(highs, axis=0).astype(bf16)
        ll = jnp.concatenate(lows, axis=0).astype(bf16)
        dz = depth - tile[2:3]
        fall = jnp.exp(-0.5 * (dz * dz))
        fh = fall.astype(bf16).astype(f32)
        fl = fall - fh
        rh = jnp.concatenate([jnp.where(layer == n, fh, 0.0) for n in range(bins_z)], axis=0)
        rl = jnp.concatenate([jnp.where(layer == n, fl, 0.0) for n in range(bins_z)], axis=0)
        rh, rl = rh.astype(bf16), rl.astype(bf16)
        return [lh, lh, ll], [rh, rl, rh]

    def product(ts, *rest):
        pairs = [operands(t, *rest) for t in ts]
        return lax.dot_general(
            jnp.concatenate([v for left, _ in pairs for v in left], axis=1),
            jnp.concatenate([v for _, right in pairs for v in right], axis=1),
            (((1,), (1,)), ((), ())),
            preferred_element_type=f32,
        )

    far = lax.div(2 * gx, ngx)

    with jax.named_scope("p_force"):
        span = 2 if tiles % 2 == 0 else 1

        @pl.loop(0, tiles // span)
        def _(step):
            ts = []
            for k in range(span):
                n = step * span + k
                near = (1 - lax.div(n + 2, tiles)) * (n + 1) + lax.div(n + 1, tiles) * (tiles - 1)
                t = near + far * (tiles - 1 - n - near)
                arrived = bead_recv.at[pl.ds(t * per, per)]
                pltpu.make_async_copy(arrived, arrived, tile_sem.at[t]).wait()
                ts.append(t)
            value = product(ts, 1, row_i, own_rows, 0.0, 4)
            for d in range(3):
                for i in range(2):
                    for j in range(2):
                        for b in range(nx // 2):
                            start = ((d * 2 + i) * 2 + j) * bins_xy + b * bins_y
                            at = pl.ds((2 * b + i) * ny + j, bins_y, stride=2)
                            force[d, at, :] += value[start : start + bins_y]

            for h in range(2):
                first = float(1 - h)
                value = product(ts, 2 * h, first, side_rows, first * (bins_xy - bins_y), 2)
                for d in range(3):
                    for j in range(2):
                        start = (d * 2 + j) * bins_y
                        at = pl.ds(j, bins_y, stride=2)
                        halo_force[h, d, at, :] += value[start : start + bins_y]

    send_ends(HALO, later=True, signs=(-1,))

    wide_lane = lax.broadcasted_iota(jnp.int32, (ny, LANES), 1)

    def collided(p, rho, m, f):
        inv = 1.0 / rho
        u = [(v + 0.5 * w) * inv for v, w in zip(m, f)]
        return relax(
            p, rho, u, 1.0 - 1.0 / TAU_FINE, 1.0 / TAU_FINE, f, 1.0 - 0.5 / TAU_FINE
        )

    def made_of(rho, m, f):
        inv = 1.0 / rho
        u = [(v + 0.5 * w) * inv for v, w in zip(m, f)]
        return setup(rho, u, 1.0 / TAU_FINE, f, 1.0 - 0.5 / TAU_FINE)

    keep = 1.0 - 1.0 / TAU_FINE
    lane_x = lax.broadcasted_iota(jnp.int32, (nx, nz), 1)
    corner_signs = corner_messages(ngz)

    def rows(n):
        sign = (1 - 2 * n).astype(f32)
        y = (ny - 1) * (1 - n)
        p = [pops[i, rows_at(y), :] for i in range(19)]
        made = made_of(*moments(p), [force[d, rows_at(y), :] for d in range(3)])
        turned = {}
        for j, i in enumerate(FACE[1, 1]):
            c = VELOCITIES[i]
            other = FACE[1, -1][j]
            even, odd = halves(i, made)
            block = keep * jnp.where(n == 0, p[i], p[other]) + (even + sign * odd)
            if c[2]:
                block = pltpu.roll(block, (1 if c[2] > 0 else nz - 1) + n * (c[2] * (nz - 2)), 1)
            if c[0]:
                block = pltpu.roll(block, (1 if c[0] > 0 else nx - 1) + n * (c[0] * (nx - 2)), 0)
            fys[n, j] = block
            turned[c[2]] = block
        y = lax.rem(gy + (1 - 2 * n) + ngy, ngy)
        move(CROSS_Y, fys.at[n, 0:5], fyr.at[n, 0:5], (gx, y, gz)).start()
        for q, s in enumerate(corner_signs):
            fys[n, 6 + q] = jnp.where((lane_x == 0) == (n == 0), turned[1], turned[-1])
            z = lax.rem(gz + (s + ngz), ngz)
            move(CROSS_Y, fys.at[n, 6 + q], fyr.at[n, 6 + q], (gx, y, z)).start()

    with jax.named_scope("p_rows"):
        pl.loop(0, 2)(rows)

    def end_rows(n):
        sign = (1 - 2 * n).astype(f32)
        y = (ny - 1) * (1 - n)
        for h in range(2):
            made = made_of(
                brim_recv[h, n, 0:1, :],
                [brim_recv[h, n, 1 + d : 2 + d, :] for d in range(3)],
                [halo_force[h, d, pl.ds(y, 1), :] for d in range(3)],
            )
            both = [halves(VELOCITIES.index((s, 1, 0)), made) for s in SIGNS]
            straight = n == h
            even = jnp.where(straight, both[0][0], both[1][0])
            odd = jnp.where(straight, both[0][1], both[1][1])
            fys[n, 5, h : h + 1, :] = keep * brim_recv[h, n, 4:5, :] + (even + sign * odd)

    with jax.named_scope("p_hwait"):
        arrive(BRIM)

    with jax.named_scope("p_endrows"):
        pl.loop(0, 2)(end_rows)
        for s in SIGNS:
            n = slot_of(s)
            plan(CROSS_Y, fys.at[n, 5], fyr.at[n, 5], (0, s, 0)).start()

    def collide(p, rho, m, f, x):
        post = collided(p, rho, m, f)
        columns = [fzs[n] for n in range(2)]
        for i in range(19):
            c = VELOCITIES[i]
            if post[i] is None:
                continue
            at = x + c[0] if isinstance(x, int) else lax.rem(x + (c[0] + nx), nx)
            plane = moved(post[i], (0, c[1], 0))
            stream[i, plane_at(at)] = moved(plane, (0, 0, c[2]))
            if c[2]:
                n = slot_of(c[2])
                k = FACE[2, c[2]].index(i) * nx + at
                turned = pltpu.roll(plane, lax.rem(k + (1 - n), LANES), 1)
                columns[n] = jnp.where(wide_lane == k, turned, columns[n])
        for n in range(2):
            fzs[n] = columns[n]

    def collide_own(x):
        p = [pops[i, plane_at(x)] for i in range(19)]
        rho, m = moments(p)
        collide(p, rho, m, [force[d, plane_at(x)] for d in range(3)], x)

    with jax.named_scope("p_collide"):
        pl.loop(0, nx)(collide_own)

    with jax.named_scope("p_hwait2"):
        arrive(HALO)

    with jax.named_scope("p_hcollide"):
        for s in SIGNS:
            n = slot_of(s)
            p = [None] * 19
            for j, i in enumerate(FACE[0, s]):
                p[i] = halo_recv[n, 4 + j]
            collide(
                p, halo_recv[n, 0], [halo_recv[n, 1 + d] for d in range(3)],
                [halo_force[n, d] for d in range(3)], -1 if s > 0 else nx,
            )

    with jax.named_scope("p_sendz"):
        for s in SIGNS:
            send(COLUMNS, slot_of(s), (0, 0, s))

    with jax.named_scope("p_coarse"):
        arrive(COARSE_X, COARSE_Y, COARSE_Z, COARSE_EDGE)
        fill_coarse(cstream, cxr, cyr, czr, cer)

    with jax.named_scope("p_ywait"):
        arrive(CROSS_Y)

    with jax.named_scope("p_yfill"):
        corner = lax.broadcasted_iota(jnp.int32, (nx, nz), 1)
        row_x = lax.broadcasted_iota(jnp.int32, (nx, nz), 0)
        for s in SIGNS:
            for j, i in enumerate(FACE[1, s]):
                c = VELOCITIES[i]
                block = fyr[slot_of(s), j]
                if c[2]:
                    q = corner_signs.index(c[2]) if c[2] in corner_signs else 0
                    block = jnp.where(corner == side(c[2], nz), fyr[slot_of(s), 6 + q], block)
                if c[0]:
                    h = slot_of(c[0])
                    end = fyr[slot_of(s), 5, h : h + 1, :]
                    block = jnp.where(row_x == side(c[0], nx), end, block)
                stream[i, rows_at(side(s, ny)), :] = block

    with jax.named_scope("p_zwait"):
        arrive(COLUMNS)

    with jax.named_scope("p_final"):
        sent = bead_recv.at[pl.ds(0, owners - 1)]
        pltpu.make_async_copy(sent, sent, bead_sem).wait()
        leave(*range(8))


def local(populations, coarse_pops, fine_mask, coarse_mask, bead_data, bead_bins):
    _, nx, ny, nz = populations.shape
    _, hx, hy, hz = coarse_pops.shape
    sizes = tuple(lax.axis_size(axis) for axis in ("gx", "gy", "gz"))
    owners = sizes[0] * sizes[1]
    total = bead_data.shape[4]
    chunks = total // LANES
    slots = total // owners
    per = LANES // slots
    rows = FIELDS // per
    beads = bead_data.reshape(6 * chunks, LANES)
    bins = bead_bins.reshape(chunks, LANES)
    f32, i32 = jnp.float32, jnp.int32
    any_spec = pl.BlockSpec(memory_space=pl.ANY)
    hbm_spec = pl.BlockSpec(memory_space=pltpu.HBM)
    vmem_spec = pl.BlockSpec(memory_space=pltpu.VMEM)
    dma = pltpu.SemaphoreType.DMA

    cross_y = (2, 6 + len(corner_messages(sizes[2])), nx, nz)
    coarse_rim = [(2, 5, hy, hz), (2, 5 * hx, 1, hz), (2, hy, LANES), (12, 1, LANES)]
    shapes = [(19, nx * ny, nz), (2, ny, LANES), coarse_pops.shape]
    vmem = [
        (3, nx * ny, nz), (2, 3, ny, nz),
        (2, 9, ny, nz), (2, 9, ny, nz), (2, 2, 8, nz), (2, 2, 8, nz),
        (FIELDS, LANES), (sizes[1], sizes[0] + 2, rows, LANES), (owners, 3, rows, LANES),
        cross_y, (2, ny, LANES), *coarse_rim, cross_y, *coarse_rim,
    ]
    operands = (
        populations.reshape(19, nx * ny, nz), coarse_pops, fine_mask, coarse_mask, beads, bins
    )
    fine, columns, coarse = pl.pallas_call(
        functools.partial(kernel, sizes, slots),
        out_shape=[jax.ShapeDtypeStruct(shape, f32) for shape in shapes],
        in_specs=[hbm_spec] * 6,
        out_specs=[vmem_spec, any_spec, vmem_spec],
        scratch_shapes=[
            pltpu.VMEM((19, nx * ny, nz), f32),
            pltpu.VMEM((19, hx, hy, hz), f32),
            pltpu.VMEM((nx, ny, nz), i32),
            pltpu.VMEM((hx, hy, hz), i32),
            pltpu.VMEM((6 * chunks, LANES), f32),
            pltpu.VMEM((chunks, LANES), i32),
            pltpu.VMEM((19, ny, nz), f32),
            *[pltpu.VMEM(shape, f32) for shape in vmem],
            dma((8,)),
            dma,
            dma((owners // per,)),
            pltpu.SemaphoreType.REGULAR((owners // per,)),
            pltpu.SemaphoreType.REGULAR,
            dma((8,)),
        ],
        compiler_params=pltpu.CompilerParams(
            collective_id=0, has_side_effects=True, vmem_limit_bytes=LIMIT
        ),
    )(*[pltpu.with_memory_space_constraint(v, pltpu.HBM) for v in operands])
    fine, coarse = pl.pallas_call(
        functools.partial(finish, nx),
        out_shape=[jax.ShapeDtypeStruct(shape, f32) for shape in (shapes[0], shapes[2])],
        in_specs=[vmem_spec] * 3,
        out_specs=[any_spec] * 2,
        scratch_shapes=[pltpu.VMEM((10, nx * ny, nz), f32), dma((3,))],
        compiler_params=pltpu.CompilerParams(vmem_limit_bytes=LIMIT),
    )(fine, columns, coarse)
    return fine.reshape(populations.shape), coarse


def solution(mesh):
    in_specs = (
        P(None, "gx", "gy", "gz"),
        P(None, "gx", "gy", "gz"),
        P("gx", "gy", "gz"),
        P("gx", "gy", "gz"),
        P("gx", "gy", "gz", None, None),
        P("gx", "gy", "gz", None, None),
    )
    out_specs = (P(None, "gx", "gy", "gz"), P(None, "gx", "gy", "gz"))
    return jax.shard_map(local, mesh=mesh, in_specs=in_specs, out_specs=out_specs, check_vma=False)
```

```python
import functools

import jax
import jax.numpy as jnp
from jax import lax
from jax.experimental import pallas as pl
from jax.experimental.pallas import tpu as pltpu
from jax.sharding import PartitionSpec as P

BIN_Z = 32
VELOCITIES = [
    (0, 0, 0), (1, 0, 0), (-1, 0, 0), (0, 1, 0), (0, -1, 0), (0, 0, 1), (0, 0, -1),
    (1, 1, 0), (-1, -1, 0), (1, -1, 0), (-1, 1, 0), (1, 0, 1), (-1, 0, -1), (1, 0, -1),
    (-1, 0, 1), (0, 1, 1), (0, -1, -1), (0, 1, -1), (0, -1, 1),
]
WEIGHTS = [1.0 / 3.0] + [1.0 / 18.0] * 6 + [1.0 / 36.0] * 12
TAU_FINE = 1.2
TAU_COARSE = 0.85
TO_COARSE = 2.0 * TAU_COARSE / TAU_FINE
TO_FINE = TAU_FINE / (2.0 * TAU_COARSE)
LANES = 128
FIELDS = 8
LIMIT = 24 * 2**20
MESH = pl.DeviceIdType.MESH
SIGNS = (1, -1)
FACE = {(a, s): [i for i in range(19) if VELOCITIES[i][a] == s] for a in range(3) for s in SIGNS}
EDGES = [i for i in range(7, 19)]


def corner_messages(ngz):
    return (1,) if ngz == 2 else SIGNS


def along(vector, c):
    total = None
    for part, sign in zip(vector, c):
        if sign:
            total = part if total is None else (total + part if sign > 0 else total - part)
    return total


def moments(p):
    rho = p[0]
    sums = [None] * 19
    m = [None] * 3
    for i in range(1, 19, 2):
        rho = rho + (p[i] + p[i + 1])
        sums[i] = p[i] - p[i + 1]
        for axis, sign in enumerate(VELOCITIES[i]):
            if sign:
                if m[axis] is None:
                    m[axis] = sums[i]
                else:
                    m[axis] = m[axis] + sums[i] if sign > 0 else m[axis] - sums[i]
    return rho, m


def setup(rho, u, b, force=None, k=0.0):
    scaled = b * rho
    base = scaled * (1.0 - 1.5 * (u[0] * u[0] + u[1] * u[1] + u[2] * u[2]))
    lin = [3.0 * scaled * v for v in u]
    quad = [4.5 * scaled * v for v in u]
    if force is not None:
        base = base - (3.0 * k) * (u[0] * force[0] + u[1] * force[1] + u[2] * force[2])
        lin = [v + (3.0 * k) * f for v, f in zip(lin, force)]
        quad = [v + (9.0 * k) * f for v, f in zip(quad, force)]
    return u, base, lin, quad


def halves(i, made):
    u, base, lin, quad = made
    first = i if i % 2 else i - 1
    c, w = VELOCITIES[first], WEIGHTS[first]
    odd = w * along(lin, c)
    return w * (base + along(u, c) * along(quad, c)), odd if i % 2 else -odd


def relax(p, rho, u, a, b, force=None, k=0.0):
    made = setup(rho, u, b, force, k)
    out = [None] * 19
    if p[0] is not None:
        out[0] = a * p[0] + WEIGHTS[0] * made[1]
    for i in range(1, 19, 2):
        if p[i] is None and p[i + 1] is None:
            continue
        even, odd = halves(i, made)
        if p[i] is not None:
            out[i] = a * p[i] + (even + odd)
        if p[i + 1] is not None:
            out[i + 1] = a * p[i + 1] + (even - odd)
    return out


def parts(x):
    high = x.astype(jnp.bfloat16)
    return high, (x - high.astype(jnp.float32)).astype(jnp.bfloat16)


def times_exact(x, table):
    high, low = parts(x)
    dot = functools.partial(jnp.dot, preferred_element_type=jnp.float32)
    return dot(high, table) + dot(low, table)


def moved(plane, c):
    rows, lanes = plane.shape
    if c[1]:
        plane = pltpu.roll(plane, 1 if c[1] > 0 else rows - 1, 0)
    if c[2]:
        plane = pltpu.roll(plane, 1 if c[2] > 0 else lanes - 1, 1)
    return plane


def side(sign, length):
    return 0 if sign > 0 else length - 1


def slot_of(sign):
    return 0 if sign > 0 else 1


def pack_x(target, xs, es):
    _, fx, fy, fz = target.shape
    row = lax.broadcasted_iota(jnp.int32, (fy, LANES), 0)
    diagonal = row == lax.broadcasted_iota(jnp.int32, (fy, LANES), 1)
    for s in SIGNS:
        for j, i in enumerate(FACE[0, s]):
            plane = target[i, side(s, fx)]
            xs[slot_of(s), j] = plane
            c = VELOCITIES[i]
            if c[1]:
                y = side(c[1], fy)
                es[EDGES.index(i), :, 0:fz] = plane[y : y + 1]
            elif c[2]:
                z = side(c[2], fz)
                turned = jnp.where(diagonal, plane[:, z : z + 1], 0.0)
                es[EDGES.index(i)] = jnp.sum(turned, axis=0, keepdims=True)


def pack_yz(target, ys, zs, es):
    _, fx, fy, fz = target.shape
    lane = lax.broadcasted_iota(jnp.int32, (fy, LANES), 1)
    for s in SIGNS:
        y, z = side(s, fy), side(s, fz)
        for j, i in enumerate(FACE[1, s]):
            for x in range(fx):
                ys[slot_of(s), j * fx + x] = target[i, x, y : y + 1, :]
        packed = jnp.zeros((fy, LANES), jnp.float32)
        for j, i in enumerate(FACE[2, s]):
            for x in range(fx):
                packed = jnp.where(lane == j * fx + x, target[i, x, :, z : z + 1], packed)
        zs[slot_of(s)] = packed
        for i in FACE[2, s]:
            c = VELOCITIES[i]
            if c[1]:
                y = side(c[1], fy)
                es[EDGES.index(i)] = packed[y : y + 1]


def fill_coarse(target, xr, yr, zr, er):
    _, fx, fy, fz = target.shape
    lane = lax.broadcasted_iota(jnp.int32, (fy, LANES), 1)
    row = lax.broadcasted_iota(jnp.int32, (fy, LANES), 0)
    last = lax.broadcasted_iota(jnp.int32, (fy, fz), 1)
    columns = []
    for s in SIGNS:
        column = zr[slot_of(s)]
        for j, i in enumerate(FACE[2, s]):
            c = VELOCITIES[i]
            if c[0]:
                value = jnp.sum(
                    jnp.where(row == lane, er[EDGES.index(i)], 0.0), axis=1, keepdims=True
                )
                column = jnp.where(lane == j * fx + side(c[0], fx), value, column)
            elif c[1]:
                spot = (lane >= j * fx) & (lane < (j + 1) * fx) & (row == side(c[1], fy))
                column = jnp.where(spot, er[EDGES.index(i)], column)
        columns.append(column)
    for i in range(1, 19):
        c = VELOCITIES[i]
        if c[0]:
            target[i, side(c[0], fx)] = xr[slot_of(c[0]), FACE[0, c[0]].index(i)]
        if c[1]:
            y, j = side(c[1], fy), FACE[1, c[1]].index(i)
            for x in range(fx):
                if c[0] and x == side(c[0], fx):
                    piece = er[EDGES.index(i), :, 0:fz]
                else:
                    piece = yr[slot_of(c[1]), j * fx + x]
                target[i, x, y : y + 1, :] = piece
        if c[2]:
            j, column = FACE[2, c[2]].index(i), columns[slot_of(c[2])]
            for x in range(fx):
                k = j * fx + x
                target[i, x] = jnp.where(
                    last == side(c[2], fz), column[:, k : k + 1], target[i, x]
                )


def finish(nx, fine, columns, coarse, fine_out, coarse_out, target, store_sem):
    _, height, nz = fine.shape
    ny = height // nx
    turned = [5, 6, *range(11, 19)]
    def store(src, dst, n):
        return pltpu.make_async_copy(src, dst, store_sem.at[n])

    for low, high in ((0, 5), (7, 11)):
        store(fine.at[low:high], fine_out.at[low:high], 0).start()
    store(coarse, coarse_out, 1).start()
    last = lax.broadcasted_iota(jnp.int32, (ny, nz), 1)
    row = lax.broadcasted_iota(jnp.int32, (ny, nz), 0)
    for n, i in enumerate(turned):
        c = VELOCITIES[i]
        column = columns[slot_of(c[2])]
        spot = last == side(c[2], nz)
        if c[1]:
            spot = spot & (row != side(c[1], ny))
        for x in range(nx):
            k = FACE[2, c[2]].index(i) * nx + x
            target[n, x * ny : (x + 1) * ny, :] = jnp.where(
                spot, column[:, k : k + 1], fine[i, x * ny : (x + 1) * ny, :]
            )
        if n % 2:
            store(target.at[n - 1 : n + 1], fine_out.at[i - 1 : i + 1], 2).start()
    store(fine.at[0:9], fine_out.at[0:9], 0).wait()
    store(coarse, coarse_out, 1).wait()
    store(target, fine_out.at[0:10], 2).wait()


def repeat(count, act, most=8):
    if count > most:
        pl.loop(0, count)(act)
    else:
        for n in range(count):
            act(n)


def kernel(
    sizes, slots, pop_in, cpop_in, fmask_in, cmask_in, bead_in, bins_in,
    stream, fzr, cstream,
    pops, cpops, fmask, cmask, bead_ref, bins_ref, tall,
    force, halo_force, halo_send, halo_recv, brim_send, brim_recv,
    bead_rows, bead_send, bead_recv, fys, fzs, cxs, cys, czs, ces,
    fyr, cxr, cyr, czr, cer,
    own_sem, bead_sem, tile_sem, ready_sem, cross_sem, recv_sem,
):
    ngx, ngy, ngz = sizes
    gx, gy, gz = lax.axis_index("gx"), lax.axis_index("gy"), lax.axis_index("gz")
    owners = ngx * ngy
    me = gx * ngy + gy
    nx, ny, nz = fmask.shape
    _, hx, hy, hz = cpops.shape
    chunks = bins_ref.shape[0]
    per = LANES // slots
    tiles = owners // per
    f32 = jnp.float32

    barrier = pltpu.get_barrier_semaphore()
    heads = ngy
    first = me < heads

    def loop(start, stop, act):
        lax.fori_loop(start, stop, lambda n, carry: (act(n), carry)[1], 0)

    def place(o):
        return lax.div(o, ngy), lax.rem(o, ngy), gz

    def greet(o):
        pl.semaphore_signal(barrier, inc=1, device_id=place(o), device_id_type=MESH)

    loop(0, jnp.minimum(me, heads), greet)

    def part(x, w):
        return pop_in.at[:, pl.ds(x * ny, w * ny)], pops.at[:, pl.ds(x * ny, w * ny)]

    loads = [
        pltpu.make_async_copy(src, dst, own_sem.at[n])
        for n, src, dst in (
            (0, bead_in, bead_ref), (1, bins_in, bins_ref), (2, *part(0, 2)), (2, *part(nx - 2, 2)),
            (3, cmask_in, cmask), (4, fmask_in, fmask), (5, cpop_in, cpops),
            (6, *part(2, nx - 4)),
        )
    ]
    for load in loads:
        load.start()

    def plane_at(x):
        return pl.ds(x * ny, ny)

    def rows_at(y):
        return pl.ds(y, nx, stride=ny)

    def device(offset):
        return (
            lax.rem(gx + (offset[0] + ngx), ngx),
            lax.rem(gy + (offset[1] + ngy), ngy),
            lax.rem(gz + (offset[2] + ngz), ngz),
        )

    def number(where):
        return (where[0] * ngy + where[1]) * ngz + where[2]

    def cross_peers(act, later):
        mine = number((gx, gy, gz))
        for offset in cross:
            where = device(offset)
            other = number(where)

            @pl.when(other > mine if later else other < mine)
            def _():
                act(where)

    cross = [(0, 0, 1), (0, 0, -1)] + [VELOCITIES[i] for i in EDGES if VELOCITIES[i][2]]
    lower = jnp.int32(0)
    for offset in cross:
        lower = lower + (number(device(offset)) < number((gx, gy, gz))).astype(jnp.int32)

    with jax.named_scope("p_signals"):
        loop(0, owners - jnp.maximum(heads, me + 1), lambda n: greet(owners - 1 - n))

        @pl.when(first)
        def _():
            loop(me + 1, heads, greet)

        cross_peers(
            lambda where: pl.semaphore_signal(
                barrier, inc=1, device_id=where, device_id_type=MESH
            ),
            later=True,
        )

    lane = lax.broadcasted_iota(jnp.int32, (FIELDS, LANES), 1)
    sub = lax.broadcasted_iota(jnp.int32, (FIELDS, LANES), 0)
    diagonal = (lax.div(lane, slots) + (FIELDS - sub)) & (per - 1)
    turn = sub & (per - 1)

    def put_block(o, block):
        a, b = o // ngy, lax.rem(o, ngy)
        bead_send[b, a + 1] = block

    def pack_chunk(chunk):
        bead_rows[0:6, :] = bead_ref[pl.ds(chunk, 6, stride=chunks), :]
        bead_rows[6:7, :] = bins_ref[pl.ds(chunk, 1), :].astype(f32)
        rows = bead_rows[...]
        turned = rows
        for m in range(1, per):
            turned = jnp.where(turn == m, pltpu.roll(rows, slots * m, 1), turned)
        for k in range(per):
            kept = jnp.where(diagonal == k, turned, 0.0)
            shift = 1
            while shift < per:
                kept = kept + pltpu.roll(kept, FIELDS - shift, 0)
                shift *= 2
            block = [kept[n : n + 1] for n in range(0, FIELDS, per)]
            o = chunk * per + k
            a, b = (o // ngy, o % ngy) if isinstance(o, int) else (lax.div(o, ngy), lax.rem(o, ngy))
            for n, part in enumerate(block):
                bead_send[b, a + 1, pl.ds(n, 1), :] = part

    with jax.named_scope("p_pack"):
        for load in loads[:2]:
            load.wait()
        bead_rows[7:8, :] = jnp.zeros((1, LANES), f32)
        repeat(chunks, pack_chunk)
        for b in range(ngy):
            bead_send[b, 0] = bead_send[b, ngx]
            bead_send[b, ngx + 1] = bead_send[b, 1]
        own_beads = pltpu.make_async_copy(
            bead_send.at[gy, pl.ds(gx, 3)], bead_recv.at[me], tile_sem.at[me // per]
        )
        own_beads.start()

    def send_beads(o):
        where = place(o)
        pltpu.make_async_remote_copy(
            src_ref=bead_send.at[where[1], pl.ds(where[0], 3)],
            dst_ref=bead_recv.at[me],
            send_sem=bead_sem,
            recv_sem=tile_sem.at[me // per],
            device_id=where,
            device_id_type=MESH,
        ).start()

    def reply_cross():
        cross_peers(
            lambda where: pl.semaphore_signal(
                cross_sem, inc=1, device_id=where, device_id_type=MESH
            ),
            later=False,
        )

    with jax.named_scope("p_barrier"):
        @pl.when(jnp.logical_not(first))
        def _():
            pl.semaphore_wait(barrier, me + lower)
            loop(0, heads, send_beads)
            loop(
                heads, me,
                lambda o: pl.semaphore_signal(
                    ready_sem.at[me // per], inc=1, device_id=place(o), device_id_type=MESH
                ),
            )
            loop(heads, me, send_beads)
            reply_cross()

    fold = lax.broadcasted_iota(jnp.int32, (nz, hz), 0) - 2 * lax.broadcasted_iota(
        jnp.int32, (nz, hz), 1
    )
    fold = jnp.where((fold == 0) | (fold == 1), 0.125, 0.0).astype(jnp.bfloat16)
    spread = lax.broadcasted_iota(jnp.int32, (hz, nz), 1) - 2 * lax.broadcasted_iota(
        jnp.int32, (hz, nz), 0
    )
    spread = jnp.where((spread == 0) | (spread == 1), 1.0, 0.0).astype(jnp.bfloat16)

    def prepare(x):
        sums = []
        for q in range(19):
            total = None
            for i in range(2):
                for j in range(2):
                    piece = pops[q, pl.ds((2 * x + i) * ny + j, hy, stride=2), :]
                    total = piece if total is None else total + piece
            sums.append(total)
        restricted = times_exact(jnp.concatenate(sums, axis=0), fold)
        p = [restricted[i * hy : (i + 1) * hy] for i in range(19)]
        rho, m = moments(p)
        inv = 1.0 / rho
        pre = relax(p, rho, [v * inv for v in m], TO_COARSE, 1.0 - TO_COARSE)
        live = cmask[x] == 1
        pre = [jnp.where(live, pre[i], cpops[i, x]) for i in range(19)]
        rho, m = moments(pre)
        inv = 1.0 / rho
        u = [v * inv for v in m]
        down = relax(pre, rho, u, TO_FINE, 1.0 - TO_FINE)
        post = relax(pre, rho, u, 1.0 - 1.0 / TAU_COARSE, 1.0 / TAU_COARSE)
        for i in range(19):
            c = VELOCITIES[i]
            cstream[i, lax.rem(x + (c[0] + hx), hx)] = moved(post[i], c)
        wide = times_exact(jnp.concatenate(down, axis=0), spread)
        for q in range(19):
            value = wide[q * hy : (q + 1) * hy]
            tall[q, pl.ds(0, hy, stride=2), :] = value
            tall[q, pl.ds(1, hy, stride=2), :] = value
        for i in range(2):
            kept = fmask[2 * x + i] == 1
            at = plane_at(2 * x + i)
            for q in range(19):
                pops[q, at] = jnp.where(kept, pops[q, at], tall[q])

    with jax.named_scope("p_ends"):
        pltpu.make_async_copy(*part(0, 4), own_sem.at[2]).wait()
        for load in loads[4:7]:
            load.wait()
        pl.loop(0, 2)(lambda n: prepare(n * (hx - 1)))
        for s in SIGNS:
            x = nx - 1 if s > 0 else 0
            p = [pops[i, plane_at(x)] for i in range(19)]
            rho, m = moments(p)
            for n, value in enumerate([rho, *m, *[p[i] for i in FACE[0, s]]]):
                halo_send[slot_of(s), n] = value
            for t in SIGNS:
                y = ny - 1 if t > 0 else 0
                for n, value in enumerate([rho, *m, p[VELOCITIES.index((s, t, 0))]]):
                    brim_send[slot_of(s), slot_of(t), n : n + 1, :] = value[y : y + 1]

    BRIM, HALO, COARSE_X, COARSE_Y, COARSE_Z, COARSE_EDGE, CROSS_Y, COLUMNS = range(8)
    buffers = [
        (brim_send, brim_recv), (halo_send, halo_recv),
        (cxs, cxr), (cys, cyr), (czs, czr), (ces, cer),
        (fys, fyr), (fzs, fzr),
    ]

    def move(kind, src, dst, where):
        return pltpu.make_async_remote_copy(
            src_ref=src, dst_ref=dst, send_sem=own_sem.at[kind], recv_sem=recv_sem.at[kind],
            device_id=where, device_id_type=MESH,
        )

    def plan(kind, src, dst, offset):
        return move(kind, src, dst, device(offset))

    def send(kind, part, offset):
        src, dst = buffers[kind]
        plan(kind, src.at[part], dst.at[part], offset).start()

    def arrive(*kinds):
        for kind in kinds:
            dst = buffers[kind][1]
            pltpu.make_async_copy(dst, dst, recv_sem.at[kind]).wait()

    def leave(*kinds):
        for kind in kinds:
            src = buffers[kind][0]
            pltpu.make_async_copy(src, src, own_sem.at[kind]).wait()

    def send_ends(kind, later, signs=SIGNS):
        for s in signs:
            other = number(device((s, 0, 0)))
            mine = number((gx, gy, gz))

            @pl.when(other > mine if later else other < mine)
            def _():
                send(kind, slot_of(s), (s, 0, 0))

    @pl.when(jnp.logical_not(first))
    def _():
        send_ends(BRIM, later=False)
        send_ends(HALO, later=False)

    with jax.named_scope("p_middle"):
        for load in loads[7:]:
            load.wait()
        pl.loop(1, hx - 1)(prepare)

    def send_group(g):
        pl.semaphore_wait(ready_sem.at[g], jnp.minimum(per, (g + 1) * per - 1 - me))
        loop(jnp.maximum(me + 1, g * per), (g + 1) * per, send_beads)

    with jax.named_scope("p_barrier2"):
        @pl.when(first)
        def _():
            pl.semaphore_wait(barrier, owners - 1 + lower)
            loop(0, me, send_beads)
            loop(me + 1, heads, send_beads)
            loop(0, owners - heads, lambda n: send_beads(owners - 1 - n))
            reply_cross()
            send_ends(BRIM, later=False)
            send_ends(HALO, later=False)

        @pl.when(jnp.logical_not(first))
        def _():
            loop(lax.div(me + 1, per), tiles, send_group)

        send_ends(BRIM, later=True)

        @pl.when(lower < len(cross))
        def _():
            pl.semaphore_wait(cross_sem, len(cross) - lower)

    with jax.named_scope("p_csend"):
        pack_x(cstream, cxs, ces)
        for s in SIGNS:
            send(COARSE_X, slot_of(s), (s, 0, 0))
        pack_yz(cstream, cys, czs, ces)
        for s in SIGNS:
            send(COARSE_Y, slot_of(s), (0, s, 0))
            send(COARSE_Z, slot_of(s), (0, 0, s))
        for n, i in enumerate(EDGES):
            send(COARSE_EDGE, n, VELOCITIES[i])
        for n in range(2):
            fzs[n] = jnp.zeros((ny, LANES), f32)
        send_ends(HALO, later=True, signs=(1,))
        force[...] = jnp.zeros_like(force)
        halo_force[...] = jnp.zeros_like(halo_force)

    bins_y, bins_z = ny // 2, nz // BIN_Z
    bins_xy = (nx // 2) * bins_y
    near = jnp.where(sub < per, 0, 1)

    def gathered(t, side_of, mine):
        source = [
            [
                jnp.broadcast_to(bead_recv[t * per + j, side_of, pl.ds(n, 1), :], (FIELDS, LANES))
                for n in range(FIELDS // per)
            ]
            for j in range(per)
        ]
        both = []
        for rows in source:
            value = rows[0]
            for n in range(1, FIELDS // per):
                value = jnp.where(sub >= n * per, rows[n], value)
            both.append(value)
        where = (diagonal + (per - mine)) & (per - 1)
        tile = None
        for m in range(per):
            mixed = both[m % per]
            for f in range(1, per):
                mixed = jnp.where(turn == f, both[(f + m) % per], mixed)
            if m:
                mixed = pltpu.roll(mixed, slots * m, 1)
            tile = mixed if tile is None else jnp.where(where == m, mixed, tile)
        return tile

    row_i = lax.div(sub, 2).astype(f32)
    row_j = (sub & 1).astype(f32)
    depth = lax.broadcasted_iota(jnp.int32, (BIN_Z, LANES), 0).astype(f32)
    own_rows = lax.broadcasted_iota(jnp.int32, (bins_xy, LANES), 0).astype(f32)
    side_rows = lax.broadcasted_iota(jnp.int32, (bins_y, LANES), 0).astype(f32)
    bf16 = jnp.bfloat16

    def operands(t, side_of, first, spots, offset, count):
        mine = lax.rem(lax.rem(gx + (side_of + (ngx - 1)), ngx) * ngy + gy, per)
        tile = gathered(t, side_of, mine)
        number = tile[6:7]
        column = jnp.floor((number + 0.5) * (1.0 / bins_z))
        layer = number - column * bins_z
        dx, dy = first - tile[0:1], row_j - tile[1:2]
        weight = jnp.exp(-0.5 * (dx * dx + dy * dy))
        mask = spots + offset == column
        highs, lows = [], []
        for d in range(3):
            pushed = weight * tile[3 + d : 4 + d]
            high = pushed.astype(bf16).astype(f32)
            low = pushed - high
            for n in range(count):
                highs.append(jnp.where(mask, high[n : n + 1], 0.0))
                lows.append(jnp.where(mask, low[n : n + 1], 0.0))
        lh = jnp.concatenate(highs, axis=0).astype(bf16)
        ll = jnp.concatenate(lows, axis=0).astype(bf16)
        dz = depth - tile[2:3]
        fall = jnp.exp(-0.5 * (dz * dz))
        fh = fall.astype(bf16).astype(f32)
        fl = fall - fh
        rh = jnp.concatenate([jnp.where(layer == n, fh, 0.0) for n in range(bins_z)], axis=0)
        rl = jnp.concatenate([jnp.where(layer == n, fl, 0.0) for n in range(bins_z)], axis=0)
        rh, rl = rh.astype(bf16), rl.astype(bf16)
        return [lh, lh, ll], [rh, rl, rh]

    def product(ts, *rest):
        pairs = [operands(t, *rest) for t in ts]
        return lax.dot_general(
            jnp.concatenate([v for left, _ in pairs for v in left], axis=1),
            jnp.concatenate([v for _, right in pairs for v in right], axis=1),
            (((1,), (1,)), ((), ())),
            preferred_element_type=f32,
        )

    far = lax.div(2 * gx, ngx)

    with jax.named_scope("p_force"):
        span = 2 if tiles % 2 == 0 else 1

        @pl.loop(0, tiles // span)
        def _(step):
            ts = []
            for k in range(span):
                n = step * span + k
                near = (1 - lax.div(n + 2, tiles)) * (n + 1) + lax.div(n + 1, tiles) * (tiles - 1)
                t = near + far * (tiles - 1 - n - near)
                arrived = bead_recv.at[pl.ds(t * per, per)]
                pltpu.make_async_copy(arrived, arrived, tile_sem.at[t]).wait()
                ts.append(t)
            value = product(ts, 1, row_i, own_rows, 0.0, 4)
            for d in range(3):
                for i in range(2):
                    for j in range(2):
                        for b in range(nx // 2):
                            start = ((d * 2 + i) * 2 + j) * bins_xy + b * bins_y
                            at = pl.ds((2 * b + i) * ny + j, bins_y, stride=2)
                            force[d, at, :] += value[start : start + bins_y]

            for h in range(2):
                first = float(1 - h)
                value = product(ts, 2 * h, first, side_rows, first * (bins_xy - bins_y), 2)
                for d in range(3):
                    for j in range(2):
                        start = (d * 2 + j) * bins_y
                        at = pl.ds(j, bins_y, stride=2)
                        halo_force[h, d, at, :] += value[start : start + bins_y]

    send_ends(HALO, later=True, signs=(-1,))

    wide_lane = lax.broadcasted_iota(jnp.int32, (ny, LANES), 1)

    def collided(p, rho, m, f):
        inv = 1.0 / rho
        u = [(v + 0.5 * w) * inv for v, w in zip(m, f)]
        return relax(
            p, rho, u, 1.0 - 1.0 / TAU_FINE, 1.0 / TAU_FINE, f, 1.0 - 0.5 / TAU_FINE
        )

    def made_of(rho, m, f):
        inv = 1.0 / rho
        u = [(v + 0.5 * w) * inv for v, w in zip(m, f)]
        return setup(rho, u, 1.0 / TAU_FINE, f, 1.0 - 0.5 / TAU_FINE)

    keep = 1.0 - 1.0 / TAU_FINE
    lane_x = lax.broadcasted_iota(jnp.int32, (nx, nz), 1)
    corner_signs = corner_messages(ngz)

    def rows(n):
        sign = (1 - 2 * n).astype(f32)
        y = (ny - 1) * (1 - n)
        p = [pops[i, rows_at(y), :] for i in range(19)]
        made = made_of(*moments(p), [force[d, rows_at(y), :] for d in range(3)])
        turned = {}
        for j, i in enumerate(FACE[1, 1]):
            c = VELOCITIES[i]
            other = FACE[1, -1][j]
            even, odd = halves(i, made)
            block = keep * jnp.where(n == 0, p[i], p[other]) + (even + sign * odd)
            if c[2]:
                block = pltpu.roll(block, (1 if c[2] > 0 else nz - 1) + n * (c[2] * (nz - 2)), 1)
            if c[0]:
                block = pltpu.roll(block, (1 if c[0] > 0 else nx - 1) + n * (c[0] * (nx - 2)), 0)
            fys[n, j] = block
            turned[c[2]] = block
        y = lax.rem(gy + (1 - 2 * n) + ngy, ngy)
        move(CROSS_Y, fys.at[n, 0:5], fyr.at[n, 0:5], (gx, y, gz)).start()
        for q, s in enumerate(corner_signs):
            fys[n, 6 + q] = jnp.where((lane_x == 0) == (n == 0), turned[1], turned[-1])
            z = lax.rem(gz + (s + ngz), ngz)
            move(CROSS_Y, fys.at[n, 6 + q], fyr.at[n, 6 + q], (gx, y, z)).start()

    with jax.named_scope("p_rows"):
        pl.loop(0, 2)(rows)

    def end_rows(n):
        sign = (1 - 2 * n).astype(f32)
        y = (ny - 1) * (1 - n)
        for h in range(2):
            made = made_of(
                brim_recv[h, n, 0:1, :],
                [brim_recv[h, n, 1 + d : 2 + d, :] for d in range(3)],
                [halo_force[h, d, pl.ds(y, 1), :] for d in range(3)],
            )
            both = [halves(VELOCITIES.index((s, 1, 0)), made) for s in SIGNS]
            straight = n == h
            even = jnp.where(straight, both[0][0], both[1][0])
            odd = jnp.where(straight, both[0][1], both[1][1])
            fys[n, 5, h : h + 1, :] = keep * brim_recv[h, n, 4:5, :] + (even + sign * odd)

    with jax.named_scope("p_hwait"):
        arrive(BRIM)

    with jax.named_scope("p_endrows"):
        pl.loop(0, 2)(end_rows)
        for s in SIGNS:
            n = slot_of(s)
            plan(CROSS_Y, fys.at[n, 5], fyr.at[n, 5], (0, s, 0)).start()

    def collide(p, rho, m, f, x):
        post = collided(p, rho, m, f)
        columns = [fzs[n] for n in range(2)]
        for i in range(19):
            c = VELOCITIES[i]
            if post[i] is None:
                continue
            at = x + c[0] if isinstance(x, int) else lax.rem(x + (c[0] + nx), nx)
            plane = moved(post[i], (0, c[1], 0))
            stream[i, plane_at(at)] = moved(plane, (0, 0, c[2]))
            if c[2]:
                n = slot_of(c[2])
                k = FACE[2, c[2]].index(i) * nx + at
                turned = pltpu.roll(plane, lax.rem(k + (1 - n), LANES), 1)
                columns[n] = jnp.where(wide_lane == k, turned, columns[n])
        for n in range(2):
            fzs[n] = columns[n]

    def collide_own(x):
        p = [pops[i, plane_at(x)] for i in range(19)]
        rho, m = moments(p)
        collide(p, rho, m, [force[d, plane_at(x)] for d in range(3)], x)

    with jax.named_scope("p_collide"):
        pl.loop(0, nx)(collide_own)

    with jax.named_scope("p_hwait2"):
        arrive(HALO)

    with jax.named_scope("p_hcollide"):
        for s in SIGNS:
            n = slot_of(s)
            p = [None] * 19
            for j, i in enumerate(FACE[0, s]):
                p[i] = halo_recv[n, 4 + j]
            collide(
                p, halo_recv[n, 0], [halo_recv[n, 1 + d] for d in range(3)],
                [halo_force[n, d] for d in range(3)], -1 if s > 0 else nx,
            )

    with jax.named_scope("p_sendz"):
        for s in SIGNS:
            send(COLUMNS, slot_of(s), (0, 0, s))

    with jax.named_scope("p_coarse"):
        arrive(COARSE_X, COARSE_Y, COARSE_Z, COARSE_EDGE)
        fill_coarse(cstream, cxr, cyr, czr, cer)

    with jax.named_scope("p_ywait"):
        arrive(CROSS_Y)

    with jax.named_scope("p_yfill"):
        corner = lax.broadcasted_iota(jnp.int32, (nx, nz), 1)
        row_x = lax.broadcasted_iota(jnp.int32, (nx, nz), 0)
        for s in SIGNS:
            for j, i in enumerate(FACE[1, s]):
                c = VELOCITIES[i]
                block = fyr[slot_of(s), j]
                if c[2]:
                    q = corner_signs.index(c[2]) if c[2] in corner_signs else 0
                    block = jnp.where(corner == side(c[2], nz), fyr[slot_of(s), 6 + q], block)
                if c[0]:
                    h = slot_of(c[0])
                    end = fyr[slot_of(s), 5, h : h + 1, :]
                    block = jnp.where(row_x == side(c[0], nx), end, block)
                stream[i, rows_at(side(s, ny)), :] = block

    with jax.named_scope("p_zwait"):
        arrive(COLUMNS)

    with jax.named_scope("p_final"):
        sent = bead_recv.at[pl.ds(0, owners - 1)]
        pltpu.make_async_copy(sent, sent, bead_sem).wait()
        leave(*range(8))


def local(populations, coarse_pops, fine_mask, coarse_mask, bead_data, bead_bins):
    _, nx, ny, nz = populations.shape
    _, hx, hy, hz = coarse_pops.shape
    sizes = tuple(lax.axis_size(axis) for axis in ("gx", "gy", "gz"))
    owners = sizes[0] * sizes[1]
    total = bead_data.shape[4]
    chunks = total // LANES
    slots = total // owners
    per = LANES // slots
    rows = FIELDS // per
    beads = bead_data.reshape(6 * chunks, LANES)
    bins = bead_bins.reshape(chunks, LANES)
    f32, i32 = jnp.float32, jnp.int32
    any_spec = pl.BlockSpec(memory_space=pl.ANY)
    hbm_spec = pl.BlockSpec(memory_space=pltpu.HBM)
    vmem_spec = pl.BlockSpec(memory_space=pltpu.VMEM)
    dma = pltpu.SemaphoreType.DMA

    cross_y = (2, 6 + len(corner_messages(sizes[2])), nx, nz)
    coarse_rim = [(2, 5, hy, hz), (2, 5 * hx, 1, hz), (2, hy, LANES), (12, 1, LANES)]
    shapes = [(19, nx * ny, nz), (2, ny, LANES), coarse_pops.shape]
    vmem = [
        (3, nx * ny, nz), (2, 3, ny, nz),
        (2, 9, ny, nz), (2, 9, ny, nz), (2, 2, 8, nz), (2, 2, 8, nz),
        (FIELDS, LANES), (sizes[1], sizes[0] + 2, rows, LANES), (owners, 3, rows, LANES),
        cross_y, (2, ny, LANES), *coarse_rim, cross_y, *coarse_rim,
    ]
    operands = (
        populations.reshape(19, nx * ny, nz), coarse_pops, fine_mask, coarse_mask, beads, bins
    )
    fine, columns, coarse = pl.pallas_call(
        functools.partial(kernel, sizes, slots),
        out_shape=[jax.ShapeDtypeStruct(shape, f32) for shape in shapes],
        in_specs=[hbm_spec] * 6,
        out_specs=[vmem_spec, any_spec, vmem_spec],
        scratch_shapes=[
            pltpu.VMEM((19, nx * ny, nz), f32),
            pltpu.VMEM((19, hx, hy, hz), f32),
            pltpu.VMEM((nx, ny, nz), i32),
            pltpu.VMEM((hx, hy, hz), i32),
            pltpu.VMEM((6 * chunks, LANES), f32),
            pltpu.VMEM((chunks, LANES), i32),
            pltpu.VMEM((19, ny, nz), f32),
            *[pltpu.VMEM(shape, f32) for shape in vmem],
            dma((8,)),
            dma,
            dma((owners // per,)),
            pltpu.SemaphoreType.REGULAR((owners // per,)),
            pltpu.SemaphoreType.REGULAR,
            dma((8,)),
        ],
        compiler_params=pltpu.CompilerParams(
            collective_id=0, has_side_effects=True, vmem_limit_bytes=LIMIT
        ),
    )(*[pltpu.with_memory_space_constraint(v, pltpu.HBM) for v in operands])
    fine, coarse = pl.pallas_call(
        functools.partial(finish, nx),
        out_shape=[jax.ShapeDtypeStruct(shape, f32) for shape in (shapes[0], shapes[2])],
        in_specs=[vmem_spec] * 3,
        out_specs=[any_spec] * 2,
        scratch_shapes=[pltpu.VMEM((10, nx * ny, nz), f32), dma((3,))],
        compiler_params=pltpu.CompilerParams(vmem_limit_bytes=LIMIT),
    )(fine, columns, coarse)
    return fine.reshape(populations.shape), coarse


def solution(mesh):
    in_specs = (
        P(None, "gx", "gy", "gz"),
        P(None, "gx", "gy", "gz"),
        P("gx", "gy", "gz"),
        P("gx", "gy", "gz"),
        P("gx", "gy", "gz", None, None),
        P("gx", "gy", "gz", None, None),
    )
    out_specs = (P(None, "gx", "gy", "gz"), P(None, "gx", "gy", "gz"))
    return jax.shard_map(local, mesh=mesh, in_specs=in_specs, out_specs=out_specs, check_vma=False)
```

```python
import functools

import jax
import jax.numpy as jnp
from jax import lax
from jax.experimental import pallas as pl
from jax.experimental.pallas import tpu as pltpu
from jax.sharding import PartitionSpec as P

BIN_Z = 32
VELOCITIES = [
    (0, 0, 0), (1, 0, 0), (-1, 0, 0), (0, 1, 0), (0, -1, 0), (0, 0, 1), (0, 0, -1),
    (1, 1, 0), (-1, -1, 0), (1, -1, 0), (-1, 1, 0), (1, 0, 1), (-1, 0, -1), (1, 0, -1),
    (-1, 0, 1), (0, 1, 1), (0, -1, -1), (0, 1, -1), (0, -1, 1),
]
WEIGHTS = [1.0 / 3.0] + [1.0 / 18.0] * 6 + [1.0 / 36.0] * 12
TAU_FINE = 1.2
TAU_COARSE = 0.85
TO_COARSE = 2.0 * TAU_COARSE / TAU_FINE
TO_FINE = TAU_FINE / (2.0 * TAU_COARSE)
LANES = 128
FIELDS = 8
LIMIT = 24 * 2**20
MESH = pl.DeviceIdType.MESH
SIGNS = (1, -1)
FACE = {(a, s): [i for i in range(19) if VELOCITIES[i][a] == s] for a in range(3) for s in SIGNS}
EDGES = [i for i in range(7, 19)]


def corner_messages(ngz):
    return (1,) if ngz == 2 else SIGNS


def along(vector, c):
    total = None
    for part, sign in zip(vector, c):
        if sign:
            total = part if total is None else (total + part if sign > 0 else total - part)
    return total


def moments(p):
    rho = p[0]
    sums = [None] * 19
    m = [None] * 3
    for i in range(1, 19, 2):
        rho = rho + (p[i] + p[i + 1])
        sums[i] = p[i] - p[i + 1]
        for axis, sign in enumerate(VELOCITIES[i]):
            if sign:
                if m[axis] is None:
                    m[axis] = sums[i]
                else:
                    m[axis] = m[axis] + sums[i] if sign > 0 else m[axis] - sums[i]
    return rho, m


def setup(rho, u, b, force=None, k=0.0):
    scaled = b * rho
    base = scaled * (1.0 - 1.5 * (u[0] * u[0] + u[1] * u[1] + u[2] * u[2]))
    lin = [3.0 * scaled * v for v in u]
    quad = [4.5 * scaled * v for v in u]
    if force is not None:
        base = base - (3.0 * k) * (u[0] * force[0] + u[1] * force[1] + u[2] * force[2])
        lin = [v + (3.0 * k) * f for v, f in zip(lin, force)]
        quad = [v + (9.0 * k) * f for v, f in zip(quad, force)]
    return u, base, lin, quad


def halves(i, made):
    u, base, lin, quad = made
    first = i if i % 2 else i - 1
    c, w = VELOCITIES[first], WEIGHTS[first]
    odd = w * along(lin, c)
    return w * (base + along(u, c) * along(quad, c)), odd if i % 2 else -odd


def relax(p, rho, u, a, b, force=None, k=0.0):
    made = setup(rho, u, b, force, k)
    out = [None] * 19
    if p[0] is not None:
        out[0] = a * p[0] + WEIGHTS[0] * made[1]
    for i in range(1, 19, 2):
        if p[i] is None and p[i + 1] is None:
            continue
        even, odd = halves(i, made)
        if p[i] is not None:
            out[i] = a * p[i] + (even + odd)
        if p[i + 1] is not None:
            out[i + 1] = a * p[i + 1] + (even - odd)
    return out


def parts(x):
    high = x.astype(jnp.bfloat16)
    return high, (x - high.astype(jnp.float32)).astype(jnp.bfloat16)


def times_exact(x, table):
    high, low = parts(x)
    dot = functools.partial(jnp.dot, preferred_element_type=jnp.float32)
    return dot(high, table) + dot(low, table)


def moved(plane, c):
    rows, lanes = plane.shape
    if c[1]:
        plane = pltpu.roll(plane, 1 if c[1] > 0 else rows - 1, 0)
    if c[2]:
        plane = pltpu.roll(plane, 1 if c[2] > 0 else lanes - 1, 1)
    return plane


def side(sign, length):
    return 0 if sign > 0 else length - 1


def slot_of(sign):
    return 0 if sign > 0 else 1


def pack_x(target, xs, es):
    _, fx, fy, fz = target.shape
    row = lax.broadcasted_iota(jnp.int32, (fy, LANES), 0)
    diagonal = row == lax.broadcasted_iota(jnp.int32, (fy, LANES), 1)
    for s in SIGNS:
        for j, i in enumerate(FACE[0, s]):
            plane = target[i, side(s, fx)]
            xs[slot_of(s), j] = plane
            c = VELOCITIES[i]
            if c[1]:
                y = side(c[1], fy)
                es[EDGES.index(i), :, 0:fz] = plane[y : y + 1]
            elif c[2]:
                z = side(c[2], fz)
                turned = jnp.where(diagonal, plane[:, z : z + 1], 0.0)
                es[EDGES.index(i)] = jnp.sum(turned, axis=0, keepdims=True)


def pack_yz(target, ys, zs, es):
    _, fx, fy, fz = target.shape
    lane = lax.broadcasted_iota(jnp.int32, (fy, LANES), 1)
    for s in SIGNS:
        y, z = side(s, fy), side(s, fz)
        for j, i in enumerate(FACE[1, s]):
            for x in range(fx):
                ys[slot_of(s), j * fx + x] = target[i, x, y : y + 1, :]
        packed = jnp.zeros((fy, LANES), jnp.float32)
        for j, i in enumerate(FACE[2, s]):
            for x in range(fx):
                packed = jnp.where(lane == j * fx + x, target[i, x, :, z : z + 1], packed)
        zs[slot_of(s)] = packed
        for i in FACE[2, s]:
            c = VELOCITIES[i]
            if c[1]:
                y = side(c[1], fy)
                es[EDGES.index(i)] = packed[y : y + 1]


def fill_coarse(target, xr, yr, zr, er):
    _, fx, fy, fz = target.shape
    lane = lax.broadcasted_iota(jnp.int32, (fy, LANES), 1)
    row = lax.broadcasted_iota(jnp.int32, (fy, LANES), 0)
    last = lax.broadcasted_iota(jnp.int32, (fy, fz), 1)
    columns = []
    for s in SIGNS:
        column = zr[slot_of(s)]
        for j, i in enumerate(FACE[2, s]):
            c = VELOCITIES[i]
            if c[0]:
                value = jnp.sum(
                    jnp.where(row == lane, er[EDGES.index(i)], 0.0), axis=1, keepdims=True
                )
                column = jnp.where(lane == j * fx + side(c[0], fx), value, column)
            elif c[1]:
                spot = (lane >= j * fx) & (lane < (j + 1) * fx) & (row == side(c[1], fy))
                column = jnp.where(spot, er[EDGES.index(i)], column)
        columns.append(column)
    for i in range(1, 19):
        c = VELOCITIES[i]
        if c[0]:
            target[i, side(c[0], fx)] = xr[slot_of(c[0]), FACE[0, c[0]].index(i)]
        if c[1]:
            y, j = side(c[1], fy), FACE[1, c[1]].index(i)
            for x in range(fx):
                if c[0] and x == side(c[0], fx):
                    piece = er[EDGES.index(i), :, 0:fz]
                else:
                    piece = yr[slot_of(c[1]), j * fx + x]
                target[i, x, y : y + 1, :] = piece
        if c[2]:
            j, column = FACE[2, c[2]].index(i), columns[slot_of(c[2])]
            for x in range(fx):
                k = j * fx + x
                target[i, x] = jnp.where(
                    last == side(c[2], fz), column[:, k : k + 1], target[i, x]
                )


def finish(nx, fine, columns, coarse, fine_out, coarse_out, target, store_sem):
    _, height, nz = fine.shape
    ny = height // nx
    turned = [5, 6, *range(11, 19)]
    def store(src, dst, n):
        return pltpu.make_async_copy(src, dst, store_sem.at[n])

    for low, high in ((0, 5), (7, 11)):
        store(fine.at[low:high], fine_out.at[low:high], 0).start()
    store(coarse, coarse_out, 1).start()
    last = lax.broadcasted_iota(jnp.int32, (ny, nz), 1)
    row = lax.broadcasted_iota(jnp.int32, (ny, nz), 0)
    for n, i in enumerate(turned):
        c = VELOCITIES[i]
        column = columns[slot_of(c[2])]
        spot = last == side(c[2], nz)
        if c[1]:
            spot = spot & (row != side(c[1], ny))
        for x in range(nx):
            k = FACE[2, c[2]].index(i) * nx + x
            target[n, x * ny : (x + 1) * ny, :] = jnp.where(
                spot, column[:, k : k + 1], fine[i, x * ny : (x + 1) * ny, :]
            )
        if n % 2:
            store(target.at[n - 1 : n + 1], fine_out.at[i - 1 : i + 1], 2).start()
    store(fine.at[0:9], fine_out.at[0:9], 0).wait()
    store(coarse, coarse_out, 1).wait()
    store(target, fine_out.at[0:10], 2).wait()


def repeat(count, act, most=8):
    if count > most:
        pl.loop(0, count)(act)
    else:
        for n in range(count):
            act(n)


def kernel(
    sizes, slots, pop_in, cpop_in, fmask_in, cmask_in, bead_in, bins_in,
    stream, fzr, cstream,
    pops, cpops, fmask, cmask, bead_ref, bins_ref, tall,
    force, halo_force, halo_send, halo_recv, brim_send, brim_recv,
    bead_rows, bead_send, bead_recv, fys, fzs, cxs, cys, czs, ces,
    fyr, cxr, cyr, czr, cer,
    own_sem, bead_sem, tile_sem, ready_sem, cross_sem, recv_sem,
):
    ngx, ngy, ngz = sizes
    gx, gy, gz = lax.axis_index("gx"), lax.axis_index("gy"), lax.axis_index("gz")
    owners = ngx * ngy
    me = gx * ngy + gy
    nx, ny, nz = fmask.shape
    _, hx, hy, hz = cpops.shape
    chunks = bins_ref.shape[0]
    per = LANES // slots
    tiles = owners // per
    f32 = jnp.float32

    barrier = pltpu.get_barrier_semaphore()
    heads = ngy
    first = me < heads

    def loop(start, stop, act):
        lax.fori_loop(start, stop, lambda n, carry: (act(n), carry)[1], 0)

    def place(o):
        return lax.div(o, ngy), lax.rem(o, ngy), gz

    def greet(o):
        pl.semaphore_signal(barrier, inc=1, device_id=place(o), device_id_type=MESH)

    loop(0, jnp.minimum(me, heads), greet)

    def part(x, w):
        return pop_in.at[:, pl.ds(x * ny, w * ny)], pops.at[:, pl.ds(x * ny, w * ny)]

    loads = [
        pltpu.make_async_copy(src, dst, own_sem.at[n])
        for n, src, dst in (
            (0, bead_in, bead_ref), (1, bins_in, bins_ref), (2, *part(0, 2)), (2, *part(nx - 2, 2)),
            (3, cmask_in, cmask), (4, fmask_in, fmask), (5, cpop_in, cpops),
            (6, *part(2, nx - 4)),
        )
    ]
    for load in loads:
        load.start()

    def plane_at(x):
        return pl.ds(x * ny, ny)

    def rows_at(y):
        return pl.ds(y, nx, stride=ny)

    def device(offset):
        return (
            lax.rem(gx + (offset[0] + ngx), ngx),
            lax.rem(gy + (offset[1] + ngy), ngy),
            lax.rem(gz + (offset[2] + ngz), ngz),
        )

    def number(where):
        return (where[0] * ngy + where[1]) * ngz + where[2]

    def cross_peers(act, later):
        mine = number((gx, gy, gz))
        for offset in cross:
            where = device(offset)
            other = number(where)

            @pl.when(other > mine if later else other < mine)
            def _():
                act(where)

    cross = [(0, 0, 1), (0, 0, -1)] + [VELOCITIES[i] for i in EDGES if VELOCITIES[i][2]]
    lower = jnp.int32(0)
    for offset in cross:
        lower = lower + (number(device(offset)) < number((gx, gy, gz))).astype(jnp.int32)

    with jax.named_scope("p_signals"):
        loop(0, owners - jnp.maximum(heads, me + 1), lambda n: greet(owners - 1 - n))

        @pl.when(first)
        def _():
            loop(me + 1, heads, greet)

        cross_peers(
            lambda where: pl.semaphore_signal(
                barrier, inc=1, device_id=where, device_id_type=MESH
            ),
            later=True,
        )

    lane = lax.broadcasted_iota(jnp.int32, (FIELDS, LANES), 1)
    sub = lax.broadcasted_iota(jnp.int32, (FIELDS, LANES), 0)
    diagonal = (lax.div(lane, slots) + (FIELDS - sub)) & (per - 1)
    turn = sub & (per - 1)

    def put_block(o, block):
        a, b = o // ngy, lax.rem(o, ngy)
        bead_send[b, a + 1] = block

    def pack_chunk(chunk):
        bead_rows[0:6, :] = bead_ref[pl.ds(chunk, 6, stride=chunks), :]
        bead_rows[6:7, :] = bins_ref[pl.ds(chunk, 1), :].astype(f32)
        rows = bead_rows[...]
        turned = rows
        for m in range(1, per):
            turned = jnp.where(turn == m, pltpu.roll(rows, slots * m, 1), turned)
        for k in range(per):
            kept = jnp.where(diagonal == k, turned, 0.0)
            shift = 1
            while shift < per:
                kept = kept + pltpu.roll(kept, FIELDS - shift, 0)
                shift *= 2
            block = [kept[n : n + 1] for n in range(0, FIELDS, per)]
            o = chunk * per + k
            a, b = (o // ngy, o % ngy) if isinstance(o, int) else (lax.div(o, ngy), lax.rem(o, ngy))
            for n, part in enumerate(block):
                bead_send[b, a + 1, pl.ds(n, 1), :] = part

    with jax.named_scope("p_pack"):
        for load in loads[:2]:
            load.wait()
        bead_rows[7:8, :] = jnp.zeros((1, LANES), f32)
        repeat(chunks, pack_chunk)
        for b in range(ngy):
            bead_send[b, 0] = bead_send[b, ngx]
            bead_send[b, ngx + 1] = bead_send[b, 1]
        own_beads = pltpu.make_async_copy(
            bead_send.at[gy, pl.ds(gx, 3)], bead_recv.at[me], tile_sem.at[me // per]
        )
        own_beads.start()

    def send_beads(o):
        where = place(o)
        pltpu.make_async_remote_copy(
            src_ref=bead_send.at[where[1], pl.ds(where[0], 3)],
            dst_ref=bead_recv.at[me],
            send_sem=bead_sem,
            recv_sem=tile_sem.at[me // per],
            device_id=where,
            device_id_type=MESH,
        ).start()

    def reply_cross():
        cross_peers(
            lambda where: pl.semaphore_signal(
                cross_sem, inc=1, device_id=where, device_id_type=MESH
            ),
            later=False,
        )

    with jax.named_scope("p_barrier"):
        @pl.when(jnp.logical_not(first))
        def _():
            pl.semaphore_wait(barrier, me + lower)
            loop(0, heads, send_beads)
            loop(
                heads, me,
                lambda o: pl.semaphore_signal(
                    ready_sem.at[me // per], inc=1, device_id=place(o), device_id_type=MESH
                ),
            )
            loop(heads, me, send_beads)
            reply_cross()

    fold = lax.broadcasted_iota(jnp.int32, (nz, hz), 0) - 2 * lax.broadcasted_iota(
        jnp.int32, (nz, hz), 1
    )
    fold = jnp.where((fold == 0) | (fold == 1), 0.125, 0.0).astype(jnp.bfloat16)
    spread = lax.broadcasted_iota(jnp.int32, (hz, nz), 1) - 2 * lax.broadcasted_iota(
        jnp.int32, (hz, nz), 0
    )
    spread = jnp.where((spread == 0) | (spread == 1), 1.0, 0.0).astype(jnp.bfloat16)

    def prepare(x):
        sums = []
        for q in range(19):
            total = None
            for i in range(2):
                for j in range(2):
                    piece = pops[q, pl.ds((2 * x + i) * ny + j, hy, stride=2), :]
                    total = piece if total is None else total + piece
            sums.append(total)
        restricted = times_exact(jnp.concatenate(sums, axis=0), fold)
        p = [restricted[i * hy : (i + 1) * hy] for i in range(19)]
        rho, m = moments(p)
        inv = 1.0 / rho
        pre = relax(p, rho, [v * inv for v in m], TO_COARSE, 1.0 - TO_COARSE)
        live = cmask[x] == 1
        pre = [jnp.where(live, pre[i], cpops[i, x]) for i in range(19)]
        rho, m = moments(pre)
        inv = 1.0 / rho
        u = [v * inv for v in m]
        down = relax(pre, rho, u, TO_FINE, 1.0 - TO_FINE)
        post = relax(pre, rho, u, 1.0 - 1.0 / TAU_COARSE, 1.0 / TAU_COARSE)
        for i in range(19):
            c = VELOCITIES[i]
            cstream[i, lax.rem(x + (c[0] + hx), hx)] = moved(post[i], c)
        wide = times_exact(jnp.concatenate(down, axis=0), spread)
        for q in range(19):
            value = wide[q * hy : (q + 1) * hy]
            tall[q, pl.ds(0, hy, stride=2), :] = value
            tall[q, pl.ds(1, hy, stride=2), :] = value
        for i in range(2):
            kept = fmask[2 * x + i] == 1
            at = plane_at(2 * x + i)
            for q in range(19):
                pops[q, at] = jnp.where(kept, pops[q, at], tall[q])

    with jax.named_scope("p_ends"):
        pltpu.make_async_copy(*part(0, 4), own_sem.at[2]).wait()
        for load in loads[4:7]:
            load.wait()
        pl.loop(0, 2)(lambda n: prepare(n * (hx - 1)))
        for s in SIGNS:
            x = nx - 1 if s > 0 else 0
            p = [pops[i, plane_at(x)] for i in range(19)]
            rho, m = moments(p)
            for n, value in enumerate([rho, *m, *[p[i] for i in FACE[0, s]]]):
                halo_send[slot_of(s), n] = value
            for t in SIGNS:
                y = ny - 1 if t > 0 else 0
                for n, value in enumerate([rho, *m, p[VELOCITIES.index((s, t, 0))]]):
                    brim_send[slot_of(s), slot_of(t), n : n + 1, :] = value[y : y + 1]

    BRIM, HALO, COARSE_X, COARSE_Y, COARSE_Z, COARSE_EDGE, CROSS_Y, COLUMNS = range(8)
    buffers = [
        (brim_send, brim_recv), (halo_send, halo_recv),
        (cxs, cxr), (cys, cyr), (czs, czr), (ces, cer),
        (fys, fyr), (fzs, fzr),
    ]

    def move(kind, src, dst, where):
        return pltpu.make_async_remote_copy(
            src_ref=src, dst_ref=dst, send_sem=own_sem.at[kind], recv_sem=recv_sem.at[kind],
            device_id=where, device_id_type=MESH,
        )

    def plan(kind, src, dst, offset):
        return move(kind, src, dst, device(offset))

    def send(kind, part, offset):
        src, dst = buffers[kind]
        plan(kind, src.at[part], dst.at[part], offset).start()

    def arrive(*kinds):
        for kind in kinds:
            dst = buffers[kind][1]
            pltpu.make_async_copy(dst, dst, recv_sem.at[kind]).wait()

    def leave(*kinds):
        for kind in kinds:
            src = buffers[kind][0]
            pltpu.make_async_copy(src, src, own_sem.at[kind]).wait()

    def send_ends(kind, later, signs=SIGNS):
        for s in signs:
            other = number(device((s, 0, 0)))
            mine = number((gx, gy, gz))

            @pl.when(other > mine if later else other < mine)
            def _():
                send(kind, slot_of(s), (s, 0, 0))

    @pl.when(jnp.logical_not(first))
    def _():
        send_ends(BRIM, later=False)
        send_ends(HALO, later=False)

    with jax.named_scope("p_middle"):
        for load in loads[7:]:
            load.wait()
        pl.loop(1, hx - 1)(prepare)

    def send_group(g):
        pl.semaphore_wait(ready_sem.at[g], jnp.minimum(per, (g + 1) * per - 1 - me))
        loop(jnp.maximum(me + 1, g * per), (g + 1) * per, send_beads)

    with jax.named_scope("p_barrier2"):
        @pl.when(first)
        def _():
            pl.semaphore_wait(barrier, owners - 1 + lower)
            loop(0, me, send_beads)
            loop(me + 1, heads, send_beads)
            loop(0, owners - heads, lambda n: send_beads(owners - 1 - n))
            reply_cross()
            send_ends(BRIM, later=False)
            send_ends(HALO, later=False)

        @pl.when(jnp.logical_not(first))
        def _():
            loop(lax.div(me + 1, per), tiles, send_group)

        send_ends(BRIM, later=True)

        @pl.when(lower < len(cross))
        def _():
            pl.semaphore_wait(cross_sem, len(cross) - lower)

    with jax.named_scope("p_csend"):
        send_ends(HALO, later=True, signs=(1,))
        pack_x(cstream, cxs, ces)
        for s in SIGNS:
            send(COARSE_X, slot_of(s), (s, 0, 0))
        pack_yz(cstream, cys, czs, ces)
        for s in SIGNS:
            send(COARSE_Y, slot_of(s), (0, s, 0))
            send(COARSE_Z, slot_of(s), (0, 0, s))
        for n, i in enumerate(EDGES):
            send(COARSE_EDGE, n, VELOCITIES[i])
        for n in range(2):
            fzs[n] = jnp.zeros((ny, LANES), f32)
        force[...] = jnp.zeros_like(force)
        halo_force[...] = jnp.zeros_like(halo_force)

    bins_y, bins_z = ny // 2, nz // BIN_Z
    bins_xy = (nx // 2) * bins_y
    near = jnp.where(sub < per, 0, 1)

    def gathered(t, side_of, mine):
        source = [
            [
                jnp.broadcast_to(bead_recv[t * per + j, side_of, pl.ds(n, 1), :], (FIELDS, LANES))
                for n in range(FIELDS // per)
            ]
            for j in range(per)
        ]
        both = []
        for rows in source:
            value = rows[0]
            for n in range(1, FIELDS // per):
                value = jnp.where(sub >= n * per, rows[n], value)
            both.append(value)
        where = (diagonal + (per - mine)) & (per - 1)
        tile = None
        for m in range(per):
            mixed = both[m % per]
            for f in range(1, per):
                mixed = jnp.where(turn == f, both[(f + m) % per], mixed)
            if m:
                mixed = pltpu.roll(mixed, slots * m, 1)
            tile = mixed if tile is None else jnp.where(where == m, mixed, tile)
        return tile

    row_i = lax.div(sub, 2).astype(f32)
    row_j = (sub & 1).astype(f32)
    depth = lax.broadcasted_iota(jnp.int32, (BIN_Z, LANES), 0).astype(f32)
    own_rows = lax.broadcasted_iota(jnp.int32, (bins_xy, LANES), 0).astype(f32)
    side_rows = lax.broadcasted_iota(jnp.int32, (bins_y, LANES), 0).astype(f32)
    bf16 = jnp.bfloat16

    def operands(t, side_of, first, spots, offset, count):
        mine = lax.rem(lax.rem(gx + (side_of + (ngx - 1)), ngx) * ngy + gy, per)
        tile = gathered(t, side_of, mine)
        number = tile[6:7]
        column = jnp.floor((number + 0.5) * (1.0 / bins_z))
        layer = number - column * bins_z
        dx, dy = first - tile[0:1], row_j - tile[1:2]
        weight = jnp.exp(-0.5 * (dx * dx + dy * dy))
        mask = spots + offset == column
        highs, lows = [], []
        for d in range(3):
            pushed = weight * tile[3 + d : 4 + d]
            high = pushed.astype(bf16).astype(f32)
            low = pushed - high
            for n in range(count):
                highs.append(jnp.where(mask, high[n : n + 1], 0.0))
                lows.append(jnp.where(mask, low[n : n + 1], 0.0))
        lh = jnp.concatenate(highs, axis=0).astype(bf16)
        ll = jnp.concatenate(lows, axis=0).astype(bf16)
        dz = depth - tile[2:3]
        fall = jnp.exp(-0.5 * (dz * dz))
        fh = fall.astype(bf16).astype(f32)
        fl = fall - fh
        rh = jnp.concatenate([jnp.where(layer == n, fh, 0.0) for n in range(bins_z)], axis=0)
        rl = jnp.concatenate([jnp.where(layer == n, fl, 0.0) for n in range(bins_z)], axis=0)
        rh, rl = rh.astype(bf16), rl.astype(bf16)
        return [lh, lh, ll], [rh, rl, rh]

    def product(ts, *rest):
        pairs = [operands(t, *rest) for t in ts]
        return lax.dot_general(
            jnp.concatenate([v for left, _ in pairs for v in left], axis=1),
            jnp.concatenate([v for _, right in pairs for v in right], axis=1),
            (((1,), (1,)), ((), ())),
            preferred_element_type=f32,
        )

    far = lax.div(2 * gx, ngx)

    with jax.named_scope("p_force"):
        span = 2 if tiles % 2 == 0 else 1

        @pl.loop(0, tiles // span)
        def _(step):
            ts = []
            for k in range(span):
                n = step * span + k
                near = (1 - lax.div(n + 2, tiles)) * (n + 1) + lax.div(n + 1, tiles) * (tiles - 1)
                t = near + far * (tiles - 1 - n - near)
                arrived = bead_recv.at[pl.ds(t * per, per)]
                pltpu.make_async_copy(arrived, arrived, tile_sem.at[t]).wait()
                ts.append(t)
            value = product(ts, 1, row_i, own_rows, 0.0, 4)
            for d in range(3):
                for i in range(2):
                    for j in range(2):
                        for b in range(nx // 2):
                            start = ((d * 2 + i) * 2 + j) * bins_xy + b * bins_y
                            at = pl.ds((2 * b + i) * ny + j, bins_y, stride=2)
                            force[d, at, :] += value[start : start + bins_y]

            for h in range(2):
                first = float(1 - h)
                value = product(ts, 2 * h, first, side_rows, first * (bins_xy - bins_y), 2)
                for d in range(3):
                    for j in range(2):
                        start = (d * 2 + j) * bins_y
                        at = pl.ds(j, bins_y, stride=2)
                        halo_force[h, d, at, :] += value[start : start + bins_y]

    send_ends(HALO, later=True, signs=(-1,))

    wide_lane = lax.broadcasted_iota(jnp.int32, (ny, LANES), 1)

    def collided(p, rho, m, f):
        inv = 1.0 / rho
        u = [(v + 0.5 * w) * inv for v, w in zip(m, f)]
        return relax(
            p, rho, u, 1.0 - 1.0 / TAU_FINE, 1.0 / TAU_FINE, f, 1.0 - 0.5 / TAU_FINE
        )

    def made_of(rho, m, f):
        inv = 1.0 / rho
        u = [(v + 0.5 * w) * inv for v, w in zip(m, f)]
        return setup(rho, u, 1.0 / TAU_FINE, f, 1.0 - 0.5 / TAU_FINE)

    keep = 1.0 - 1.0 / TAU_FINE
    lane_x = lax.broadcasted_iota(jnp.int32, (nx, nz), 1)
    corner_signs = corner_messages(ngz)

    def rows(n):
        sign = (1 - 2 * n).astype(f32)
        y = (ny - 1) * (1 - n)
        p = [pops[i, rows_at(y), :] for i in range(19)]
        made = made_of(*moments(p), [force[d, rows_at(y), :] for d in range(3)])
        turned = {}
        for j, i in enumerate(FACE[1, 1]):
            c = VELOCITIES[i]
            other = FACE[1, -1][j]
            even, odd = halves(i, made)
            block = keep * jnp.where(n == 0, p[i], p[other]) + (even + sign * odd)
            if c[2]:
                block = pltpu.roll(block, (1 if c[2] > 0 else nz - 1) + n * (c[2] * (nz - 2)), 1)
            if c[0]:
                block = pltpu.roll(block, (1 if c[0] > 0 else nx - 1) + n * (c[0] * (nx - 2)), 0)
            fys[n, j] = block
            turned[c[2]] = block
        y = lax.rem(gy + (1 - 2 * n) + ngy, ngy)
        move(CROSS_Y, fys.at[n, 0:5], fyr.at[n, 0:5], (gx, y, gz)).start()
        for q, s in enumerate(corner_signs):
            fys[n, 6 + q] = jnp.where((lane_x == 0) == (n == 0), turned[1], turned[-1])
            z = lax.rem(gz + (s + ngz), ngz)
            move(CROSS_Y, fys.at[n, 6 + q], fyr.at[n, 6 + q], (gx, y, z)).start()

    with jax.named_scope("p_rows"):
        pl.loop(0, 2)(rows)

    def end_rows(n):
        sign = (1 - 2 * n).astype(f32)
        y = (ny - 1) * (1 - n)
        for h in range(2):
            made = made_of(
                brim_recv[h, n, 0:1, :],
                [brim_recv[h, n, 1 + d : 2 + d, :] for d in range(3)],
                [halo_force[h, d, pl.ds(y, 1), :] for d in range(3)],
            )
            both = [halves(VELOCITIES.index((s, 1, 0)), made) for s in SIGNS]
            straight = n == h
            even = jnp.where(straight, both[0][0], both[1][0])
            odd = jnp.where(straight, both[0][1], both[1][1])
            fys[n, 5, h : h + 1, :] = keep * brim_recv[h, n, 4:5, :] + (even + sign * odd)

    with jax.named_scope("p_hwait"):
        arrive(BRIM)

    with jax.named_scope("p_endrows"):
        pl.loop(0, 2)(end_rows)
        for s in SIGNS:
            n = slot_of(s)
            plan(CROSS_Y, fys.at[n, 5], fyr.at[n, 5], (0, s, 0)).start()

    def collide(p, rho, m, f, x):
        post = collided(p, rho, m, f)
        columns = [fzs[n] for n in range(2)]
        for i in range(19):
            c = VELOCITIES[i]
            if post[i] is None:
                continue
            at = x + c[0] if isinstance(x, int) else lax.rem(x + (c[0] + nx), nx)
            plane = moved(post[i], (0, c[1], 0))
            stream[i, plane_at(at)] = moved(plane, (0, 0, c[2]))
            if c[2]:
                n = slot_of(c[2])
                k = FACE[2, c[2]].index(i) * nx + at
                turned = pltpu.roll(plane, lax.rem(k + (1 - n), LANES), 1)
                columns[n] = jnp.where(wide_lane == k, turned, columns[n])
        for n in range(2):
            fzs[n] = columns[n]

    def collide_own(x):
        p = [pops[i, plane_at(x)] for i in range(19)]
        rho, m = moments(p)
        collide(p, rho, m, [force[d, plane_at(x)] for d in range(3)], x)

    with jax.named_scope("p_collide"):
        pl.loop(0, nx)(collide_own)

    with jax.named_scope("p_hwait2"):
        arrive(HALO)

    with jax.named_scope("p_hcollide"):
        for s in SIGNS:
            n = slot_of(s)
            p = [None] * 19
            for j, i in enumerate(FACE[0, s]):
                p[i] = halo_recv[n, 4 + j]
            collide(
                p, halo_recv[n, 0], [halo_recv[n, 1 + d] for d in range(3)],
                [halo_force[n, d] for d in range(3)], -1 if s > 0 else nx,
            )

    with jax.named_scope("p_sendz"):
        for s in SIGNS:
            send(COLUMNS, slot_of(s), (0, 0, s))

    with jax.named_scope("p_coarse"):
        arrive(COARSE_X, COARSE_Y, COARSE_Z, COARSE_EDGE)
        fill_coarse(cstream, cxr, cyr, czr, cer)

    with jax.named_scope("p_ywait"):
        arrive(CROSS_Y)

    with jax.named_scope("p_yfill"):
        corner = lax.broadcasted_iota(jnp.int32, (nx, nz), 1)
        row_x = lax.broadcasted_iota(jnp.int32, (nx, nz), 0)
        for s in SIGNS:
            for j, i in enumerate(FACE[1, s]):
                c = VELOCITIES[i]
                block = fyr[slot_of(s), j]
                if c[2]:
                    q = corner_signs.index(c[2]) if c[2] in corner_signs else 0
                    block = jnp.where(corner == side(c[2], nz), fyr[slot_of(s), 6 + q], block)
                if c[0]:
                    h = slot_of(c[0])
                    end = fyr[slot_of(s), 5, h : h + 1, :]
                    block = jnp.where(row_x == side(c[0], nx), end, block)
                stream[i, rows_at(side(s, ny)), :] = block

    with jax.named_scope("p_zwait"):
        arrive(COLUMNS)

    with jax.named_scope("p_final"):
        sent = bead_recv.at[pl.ds(0, owners - 1)]
        pltpu.make_async_copy(sent, sent, bead_sem).wait()
        leave(*range(8))


def local(populations, coarse_pops, fine_mask, coarse_mask, bead_data, bead_bins):
    _, nx, ny, nz = populations.shape
    _, hx, hy, hz = coarse_pops.shape
    sizes = tuple(lax.axis_size(axis) for axis in ("gx", "gy", "gz"))
    owners = sizes[0] * sizes[1]
    total = bead_data.shape[4]
    chunks = total // LANES
    slots = total // owners
    per = LANES // slots
    rows = FIELDS // per
    beads = bead_data.reshape(6 * chunks, LANES)
    bins = bead_bins.reshape(chunks, LANES)
    f32, i32 = jnp.float32, jnp.int32
    any_spec = pl.BlockSpec(memory_space=pl.ANY)
    hbm_spec = pl.BlockSpec(memory_space=pltpu.HBM)
    vmem_spec = pl.BlockSpec(memory_space=pltpu.VMEM)
    dma = pltpu.SemaphoreType.DMA

    cross_y = (2, 6 + len(corner_messages(sizes[2])), nx, nz)
    coarse_rim = [(2, 5, hy, hz), (2, 5 * hx, 1, hz), (2, hy, LANES), (12, 1, LANES)]
    shapes = [(19, nx * ny, nz), (2, ny, LANES), coarse_pops.shape]
    vmem = [
        (3, nx * ny, nz), (2, 3, ny, nz),
        (2, 9, ny, nz), (2, 9, ny, nz), (2, 2, 8, nz), (2, 2, 8, nz),
        (FIELDS, LANES), (sizes[1], sizes[0] + 2, rows, LANES), (owners, 3, rows, LANES),
        cross_y, (2, ny, LANES), *coarse_rim, cross_y, *coarse_rim,
    ]
    operands = (
        populations.reshape(19, nx * ny, nz), coarse_pops, fine_mask, coarse_mask, beads, bins
    )
    fine, columns, coarse = pl.pallas_call(
        functools.partial(kernel, sizes, slots),
        out_shape=[jax.ShapeDtypeStruct(shape, f32) for shape in shapes],
        in_specs=[hbm_spec] * 6,
        out_specs=[vmem_spec, any_spec, vmem_spec],
        scratch_shapes=[
            pltpu.VMEM((19, nx * ny, nz), f32),
            pltpu.VMEM((19, hx, hy, hz), f32),
            pltpu.VMEM((nx, ny, nz), i32),
            pltpu.VMEM((hx, hy, hz), i32),
            pltpu.VMEM((6 * chunks, LANES), f32),
            pltpu.VMEM((chunks, LANES), i32),
            pltpu.VMEM((19, ny, nz), f32),
            *[pltpu.VMEM(shape, f32) for shape in vmem],
            dma((8,)),
            dma,
            dma((owners // per,)),
            pltpu.SemaphoreType.REGULAR((owners // per,)),
            pltpu.SemaphoreType.REGULAR,
            dma((8,)),
        ],
        compiler_params=pltpu.CompilerParams(
            collective_id=0, has_side_effects=True, vmem_limit_bytes=LIMIT
        ),
    )(*[pltpu.with_memory_space_constraint(v, pltpu.HBM) for v in operands])
    fine, coarse = pl.pallas_call(
        functools.partial(finish, nx),
        out_shape=[jax.ShapeDtypeStruct(shape, f32) for shape in (shapes[0], shapes[2])],
        in_specs=[vmem_spec] * 3,
        out_specs=[any_spec] * 2,
        scratch_shapes=[pltpu.VMEM((10, nx * ny, nz), f32), dma((3,))],
        compiler_params=pltpu.CompilerParams(vmem_limit_bytes=LIMIT),
    )(fine, columns, coarse)
    return fine.reshape(populations.shape), coarse


def solution(mesh):
    in_specs = (
        P(None, "gx", "gy", "gz"),
        P(None, "gx", "gy", "gz"),
        P("gx", "gy", "gz"),
        P("gx", "gy", "gz"),
        P("gx", "gy", "gz", None, None),
        P("gx", "gy", "gz", None, None),
    )
    out_specs = (P(None, "gx", "gy", "gz"), P(None, "gx", "gy", "gz"))
    return jax.shard_map(local, mesh=mesh, in_specs=in_specs, out_specs=out_specs, check_vma=False)
```
